32 devices in a mesh: dp: 16 (over z, y, x), mp: 2 (over core).
Axes of the slice: x: 2, y: 2, z: 4, core: 2. Of those that a mesh axis runs over, the one named last changes fastest.
Arguments:
- x_rows: bfloat16 [24576, 384], P(('dp', 'mp')), may hold values from -6 to 6
- cotangent: float32 [24576, 384], P(('dp', 'mp')), may hold values from -12 to 12
- task_ids: int32 [16], P('dp'), may hold values from 0 to 4
- routes: int32 [24576, 4], P('dp'), may hold values from 0 to 7, all different within a row; in each aligned block of 1536 rows (0 to 1535, 1536 to 3071, ...) at most 1536 rows name the same one
- norm_params: float32 [4, 384], replicated, may hold values from -0.4 to 3
- norm_first: float32 [4, 384], replicated, may hold values from -0.00390625 to 0.00390625
- norm_second: float32 [4, 384], replicated, may hold values from 6.3861902e-09 to 2.5544761e-08
- norm_ema: float32 [4, 384], replicated, may hold values from -0.4 to 2
- qkv_weight: float32 [3, 384, 384], P(None, 'dp', 'mp'), may hold values from -0.3125 to 0.3125
- qkv_first: float32 [3, 384, 384], P(None, 'dp', 'mp'), may hold values from -0.001953125 to 0.001953125
- qkv_second: float32 [3, 384, 384], P(None, 'dp', 'mp'), may hold values from 1.5965476e-09 to 6.3861902e-09
- qkv_ema: float32 [3, 384, 384], P(None, 'dp', 'mp'), may hold values from -0.3125 to 0.3125
- out_weight: float32 [384, 384], P('dp', 'mp'), may hold values from -1.5 to 1.5
- out_first: float32 [384, 384], P('dp', 'mp'), may hold values from -0.0009765625 to 0.0009765625
- out_second: float32 [384, 384], P('dp', 'mp'), may hold values from 3.991369e-10 to 1.5965476e-09
- out_ema: float32 [384, 384], P('dp', 'mp'), may hold values from -1.5 to 1.5
- router: float32 [389, 8], replicated, may hold values from -2 to 2
- router_first: float32 [389, 8], replicated, may hold values from -0.00048828125 to 0.00048828125
- router_second: float32 [389, 8], replicated, may hold values from 9.978422e-11 to 3.991369e-10
- router_ema: float32 [389, 8], replicated, may hold values from -2 to 2
- expert_in: float32 [8, 384, 1536], P(None, 'dp', 'mp'), may hold values from -0.3125 to 0.3125
- expert_in_first: float32 [8, 384, 1536], P(None, 'dp', 'mp'), may hold values from -0.00024414062 to 0.00024414062
- expert_in_second: float32 [8, 384, 1536], P(None, 'dp', 'mp'), may hold values from 2.4946056e-11 to 9.978422e-11
- expert_in_ema: float32 [8, 384, 1536], P(None, 'dp', 'mp'), may hold values from -0.3125 to 0.3125
- expert_out: float32 [8, 384, 1536], P(None, 'dp', 'mp'), may hold values from -0.3125 to 0.3125
- expert_out_first: float32 [8, 384, 1536], P(None, 'dp', 'mp'), may hold values from -0.00061035156 to 0.00061035156
- expert_out_second: float32 [8, 384, 1536], P(None, 'dp', 'mp'), may hold values from 1.6863534e-10 to 6.7454137e-10
- expert_out_ema: float32 [8, 384, 1536], P(None, 'dp', 'mp'), may hold values from -0.3125 to 0.3125
Outputs:
- output: float32 [24576, 384], P(('dp', 'mp'))
- input_grad: float32 [24576, 384], P(('dp', 'mp'))
- grad_norm: float32 [1], replicated
- norm_params_new: float32 [4, 384], replicated
- norm_first_new: float32 [4, 384], replicated
- norm_second_new: float32 [4, 384], replicated
- norm_ema_new: float32 [4, 384], replicated
- qkv_weight_new: float32 [3, 384, 384], P(None, 'dp', 'mp')
- qkv_first_new: float32 [3, 384, 384], P(None, 'dp', 'mp')
- qkv_second_new: float32 [3, 384, 384], P(None, 'dp', 'mp')
- qkv_ema_new: float32 [3, 384, 384], P(None, 'dp', 'mp')
- out_weight_new: float32 [384, 384], P('dp', 'mp')
- out_first_new: float32 [384, 384], P('dp', 'mp')
- out_second_new: float32 [384, 384], P('dp', 'mp')
- out_ema_new: float32 [384, 384], P('dp', 'mp')
- router_new: float32 [389, 8], replicated
- router_first_new: float32 [389, 8], replicated
- router_second_new: float32 [389, 8], replicated
- router_ema_new: float32 [389, 8], replicated
- expert_in_new: float32 [8, 384, 1536], P(None, 'dp', 'mp')
- expert_in_first_new: float32 [8, 384, 1536], P(None, 'dp', 'mp')
- expert_in_second_new: float32 [8, 384, 1536], P(None, 'dp', 'mp')
- expert_in_ema_new: float32 [8, 384, 1536], P(None, 'dp', 'mp')
- expert_out_new: float32 [8, 384, 1536], P(None, 'dp', 'mp')
- expert_out_first_new: float32 [8, 384, 1536], P(None, 'dp', 'mp')
- expert_out_second_new: float32 [8, 384, 1536], P(None, 'dp', 'mp')
- expert_out_ema_new: float32 [8, 384, 1536], P(None, 'dp', 'mp')
The draws below stay inside these ranges and needn't reach their ends.
Inputs may be any that keep to these rules, and one draw needn't show every extreme that they name: `routes`: each row names 4 different experts; within each aligned block of 1536 rows (the patches of one index of dp) no expert is named by more than 1536 rows.
All inputs are finite; a program needn't handle non-finite values.
Results may differ from the reference program's by a relative error of at most 0.02.
Values may be sent and summed in bfloat16 or wider, within the bound.
A program may use at most 192 MiB of HBM per device.

```python
import math
import jax
import jax.numpy as jnp
import numpy as np
from jax import lax

D = 384
H = 6
HD = 64
HALL = 384
FF = 1536
E = 8
TOP = 4
TASKS = 5
L = 1536
STEP = 10
R = 1536
CAP = 1536
IMAGES = 16
TOKENS = 24576
PARAMS = 10031656
N_DP = 16


def feature_ramp(low_end, factor):
    position = jnp.arange(D, dtype=jnp.float32) / (D - 1)
    return low_end * jnp.exp(position * math.log(factor))


def norm_table(key):
    gaussian = jax.random.truncated_normal(key, -4.0, 4.0, (4, D), jnp.float32)
    ramp = feature_ramp(0.6, 3.0)
    gain_row = ramp * (1.0 + 0.1 * gaussian[0])
    gain_row_two = ramp * (1.0 + 0.1 * gaussian[2])
    bias_row = 0.1 * gaussian[1]
    bias_row_two = 0.1 * gaussian[3]
    return jnp.stack([gain_row, bias_row, gain_row_two, bias_row_two], axis=0)


def average_table(key):
    gaussian = jax.random.truncated_normal(jax.random.fold_in(key, 3), -4.0, 4.0, (4, D), jnp.float32)
    level = jax.random.uniform(jax.random.fold_in(key, 5), (4, D), jnp.float32, math.log(0.5), math.log(2.0))
    gain_like = jnp.exp(level)
    bias_like = 0.1 * gaussian
    return jnp.stack([gain_like[0], bias_like[1], gain_like[2], bias_like[3]], axis=0)


def draw_norm_params(key, part):
    return norm_table(jax.random.fold_in(key, 11))


def draw_norm_ema(key, part):
    return average_table(jax.random.fold_in(key, 13))


def router_table(key):
    gaussian = jax.random.truncated_normal(key, -4.0, 4.0, (D + TASKS, E), jnp.float32)
    row_scale = jnp.where(jnp.arange(D + TASKS) < D, 0.5 / math.sqrt(D), 0.5).astype(jnp.float32)
    return gaussian * row_scale[:, None]


def draw_router(key, part):
    return router_table(jax.random.fold_in(key, 17))


def draw_router_ema(key, part):
    return router_table(jax.random.fold_in(key, 19))


def draw_cotangent(key, part):
    gaussian = jax.random.truncated_normal(jax.random.fold_in(key, 23), -4.0, 4.0, (TOKENS, D), jnp.float32)
    ramp = feature_ramp(0.5, 3.0)
    return gaussian * ramp[None, :]


def plant(array, own_key, least, top_value):
    longest = array.shape.index(max(array.shape))
    spots = []
    for shift in (0, 1):
        where = [jax.random.randint(jax.random.fold_in(own_key, axis), (), 0, length) for axis, length in enumerate(array.shape)]
        where[longest] = (where[longest] + shift) % array.shape[longest]
        spots.append(tuple(where))
    return array.at[spots[0]].set(least).at[spots[1]].set(top_value)


def block_scale(own_key, extent, cuts, least, high):
    def one(axis_at, blocks):
        heights = jax.random.uniform(jax.random.fold_in(jax.random.fold_in(own_key, 6), axis_at), (blocks,), jnp.float32, least / len(cuts), high / len(cuts))
        return jnp.repeat(jnp.exp(heights), extent[axis_at] // blocks).reshape((-1,) + (1,) * (len(extent) - axis_at - 1))

    factor_of = one(*cuts[0])
    for cut in cuts[1:]:
        factor_of = factor_of * one(*cut)
    return factor_of


def deal_out(stream_key, own, number, rows, count, top, reach, slope):
    order = jax.random.permutation(stream_key, count)
    heavy_load, ordinary = shares(count, rows * top, reach, slope, True), shares(count, rows * top, reach, slope, False)
    places = jnp.arange(count)

    def named(sizes, offset_by):
        used = int((sizes > 0).sum())
        fixed = max(1, used // 4)
        shifted = fixed + (places - fixed + offset_by * (used - fixed)) % max(1, count - fixed)
        return jnp.zeros((count,), jnp.int32).at[order[jnp.where(places < fixed, places, shifted)]].set(jnp.asarray(sizes, jnp.int32))

    sizes = jnp.where(number % 4 == 0, named(heavy_load, number // 4), named(ordinary, number - number // 4 - 1))
    mixed = jax.random.permutation(jax.random.fold_in(own, 3), count)
    donor, taker = mixed[0:count // 2 * 2:2], mixed[1:count // 2 * 2:2]
    slack = jnp.minimum(sizes[donor] - 1, reach - sizes[taker]) // 2
    slack = jnp.where((donor == order[0]) | (taker == order[0]) | (sizes[taker] == 0), 0, jnp.maximum(slack, 0))
    shifted = jax.random.randint(jax.random.fold_in(own, 4), (count // 2,), 0, 1 << 20) % (slack + 1)
    sizes = sizes.at[donor].add(-shifted).at[taker].add(shifted)
    items = jnp.searchsorted(jnp.cumsum(sizes), jnp.arange(rows * top), side="right").astype(jnp.int32)
    listing = items.reshape(top, rows).T
    listing = listing[jax.random.permutation(jax.random.fold_in(own, 1), rows)]
    offset_by = jax.random.randint(jax.random.fold_in(own, 2), (rows, 1), 0, top)
    return jnp.take_along_axis(listing, (jnp.arange(top)[None, :] + offset_by) % top, axis=1)


def shares(amount, total, most, skew, full):
    loads = [(1 << 20) // math.isqrt(standing ** skew) + 1 for standing in range(1, amount + 1)]
    largest = most if full else min(most, max(-(-total // amount), total * loads[0] // sum(loads)))
    least = 1 if total - largest >= amount - 1 else 0
    counts, spare = [largest] + [least] * (amount - 1), total - largest - least * (amount - 1)
    while spare > 0:
        candidates = [i for i in range(1, amount) if counts[i] < largest] or [i for i in range(1, amount) if counts[i] < most]
        mass, left = sum([loads[i] for i in candidates]), spare
        for i in candidates:
            addition = min(most - counts[i], max(1, left * loads[i] // mass), spare)
            counts[i] = counts[i] + addition
            spare = spare - addition
    return np.array(counts)


def scatter_about(rng, dims, scale, limit, pieces=(), kind=jnp.bfloat16):
    result = scale * jax.random.normal(rng, dims, jnp.float32)
    if pieces:
        result = result * block_scale(rng, dims, pieces, -0.22, 0.18)
    return jnp.clip(result, -limit, limit).astype(kind)


def setup_inputs(seed: int = 0) -> dict:
    key_of = jax.random.split(jax.random.key(seed), 29)
    x_rows = scatter_about(key_of[0], (TOKENS, D), 1.0, 6.0, ((0, 32),))
    cotangent = draw_cotangent(jax.random.fold_in(key_of[28], 71), 0)
    task_ids = plant(jax.random.randint(key_of[2], (IMAGES,), 0, TASKS), jax.random.fold_in(key_of[2], 1), 0, TASKS - 1).astype(jnp.int32)
    routes_keys = jax.random.split(jax.random.fold_in(key_of[3], 1), TOKENS // R)
    routes_turns = jax.random.permutation(jax.random.fold_in(key_of[3], 3), TOKENS // R)
    routes = jax.vmap(lambda own, number: deal_out(jax.random.fold_in(key_of[3], 2), own, number, R, E, TOP, CAP, 2))(routes_keys, routes_turns).reshape((TOKENS, TOP))
    norm_params = draw_norm_params(jax.random.fold_in(key_of[28], 71), 0)
    norm_first = scatter_about(key_of[5], (4, D), (0.888 / PARAMS ** 0.5), 0.00390625, (), jnp.float32)
    norm_second = jnp.clip(jnp.exp(jax.random.uniform(key_of[6], (4, D), jnp.float32, math.log(6.386190243290457e-09), math.log(2.554476097316183e-08))), 6.386190243290457e-09, 2.554476097316183e-08)
    norm_ema = draw_norm_ema(jax.random.fold_in(key_of[28], 71), 0)
    qkv_weight = scatter_about(key_of[8], (3, D, HALL), D ** -0.5, 0.3125, ((1, 16), (2, 2)), jnp.float32)
    qkv_first = scatter_about(key_of[9], (3, D, HALL), (0.444 / PARAMS ** 0.5), 0.001953125, ((1, 16), (2, 2)), jnp.float32)
    qkv_second = jnp.clip(jnp.exp(math.log(6.386190243290457e-09) - 1.3862944 * jax.random.uniform(key_of[10], (3, D, HALL), jnp.float32) ** block_scale(key_of[10], (3, D, HALL), ((1, 16), (2, 2)), -0.2, 0.2)), 1.5965475608226143e-09, 6.386190243290457e-09)
    qkv_ema = scatter_about(key_of[11], (3, D, HALL), D ** -0.5, 0.3125, ((1, 16), (2, 2)), jnp.float32)
    out_weight = scatter_about(key_of[12], (D, HALL), (HALL * 64 // L) ** -0.5, 1.5, ((0, 16), (1, 2)), jnp.float32)
    out_first = scatter_about(key_of[13], (D, HALL), (0.222 / PARAMS ** 0.5), 0.0009765625, ((0, 16), (1, 2)), jnp.float32)
    out_second = jnp.clip(jnp.exp(math.log(1.5965475608226143e-09) - 1.3862944 * jax.random.uniform(key_of[14], (D, HALL), jnp.float32) ** block_scale(key_of[14], (D, HALL), ((0, 16), (1, 2)), -0.2, 0.2)), 3.9913689020565357e-10, 1.5965475608226143e-09)
    out_ema = scatter_about(key_of[15], (D, HALL), (HALL * 64 // L) ** -0.5, 1.5, ((0, 16), (1, 2)), jnp.float32)
    router = draw_router(jax.random.fold_in(key_of[28], 71), 0)
    router_first = scatter_about(key_of[17], (D + TASKS, E), (0.111 / PARAMS ** 0.5), 0.00048828125, (), jnp.float32)
    router_second = jnp.clip(jnp.exp(jax.random.uniform(key_of[18], (D + TASKS, E), jnp.float32, math.log(9.978422255141339e-11), math.log(3.9913689020565357e-10))), 9.978422255141339e-11, 3.9913689020565357e-10)
    router_ema = draw_router_ema(jax.random.fold_in(key_of[28], 71), 0)
    expert_in = scatter_about(key_of[20], (E, D, FF), D ** -0.5, 0.3125, ((1, 16), (2, 2)), jnp.float32)
    expert_in_first = scatter_about(key_of[21], (E, D, FF), (0.0555 / PARAMS ** 0.5), 0.00024414062, ((1, 16), (2, 2)), jnp.float32)
    expert_in_second = jnp.clip(jnp.exp(math.log(9.978422255141339e-11) - 1.3862944 * jax.random.uniform(key_of[22], (E, D, FF), jnp.float32) ** block_scale(key_of[22], (E, D, FF), ((1, 16), (2, 2)), -0.2, 0.2)), 2.4946055637853348e-11, 9.978422255141339e-11)
    expert_in_ema = scatter_about(key_of[23], (E, D, FF), D ** -0.5, 0.3125, ((1, 16), (2, 2)), jnp.float32)
    expert_out = scatter_about(key_of[24], (E, D, FF), (FF // 4) ** -0.5, 0.3125, ((1, 16), (2, 2)), jnp.float32)
    expert_out_first = scatter_about(key_of[25], (E, D, FF), (0.144 / PARAMS ** 0.5), 0.00061035156, ((1, 16), (2, 2)), jnp.float32)
    expert_out_second = jnp.clip(jnp.exp(math.log(6.745413672071265e-10) - 1.3862944 * jax.random.uniform(key_of[26], (E, D, FF), jnp.float32) ** block_scale(key_of[26], (E, D, FF), ((1, 16), (2, 2)), -0.2, 0.2)), 1.6863534180178164e-10, 6.745413672071265e-10)
    expert_out_ema = scatter_about(key_of[27], (E, D, FF), (FF // 4) ** -0.5, 0.3125, ((1, 16), (2, 2)), jnp.float32)
    return dict(x_rows=x_rows, cotangent=cotangent, task_ids=task_ids, routes=routes, norm_params=norm_params, norm_first=norm_first, norm_second=norm_second, norm_ema=norm_ema, qkv_weight=qkv_weight, qkv_first=qkv_first, qkv_second=qkv_second, qkv_ema=qkv_ema, out_weight=out_weight, out_first=out_first, out_second=out_second, out_ema=out_ema, router=router, router_first=router_first, router_second=router_second, router_ema=router_ema, expert_in=expert_in, expert_in_first=expert_in_first, expert_in_second=expert_in_second, expert_in_ema=expert_in_ema, expert_out=expert_out, expert_out_first=expert_out_first, expert_out_second=expert_out_second, expert_out_ema=expert_out_ema)


@jax.custom_vjp
def low(v):
    return lax.optimization_barrier(v.astype(jnp.bfloat16)).astype(jnp.float32)

@jax.custom_vjp
def low_back(v):
    return v

def low_keep(v):
    return (low(v), None)

def low_pass(kept, grad):
    return (grad,)

def back_keep(v):
    return (v, None)

def back_low(kept, grad):
    return (low(grad),)
low.defvjp(low_keep, low_pass)
low_back.defvjp(back_keep, back_low)
NORM_EPS = 1e-06
SCORE_SCALE = 0.125
CLIP_LIMIT = 1.0
BETA_FIRST = 0.9
BETA_SECOND = 0.999
LEARN_RATE = 0.1
NORM_RATE = 0.5
WEIGHT_DECAY = 0.05
ADAM_EPS = 1e-08
EMA_KEEP = 0.6
SQRT_HALF = 0.7071067811865476

def dense(left, right):
    return jnp.dot(left, right, precision=lax.Precision.HIGHEST, preferred_element_type=jnp.float32)

def norm_forward(rows, gain, shift):
    row_mean = lax.optimization_barrier(jnp.mean(rows, axis=-1, keepdims=True))
    centered = rows - row_mean
    inv_std = lax.rsqrt(lax.optimization_barrier(jnp.mean(centered * centered, axis=-1, keepdims=True)) + NORM_EPS)
    return centered * inv_std * gain + shift

def gelu_exact(values):
    return 0.5 * values * (1.0 + lax.erf(values * SQRT_HALF))

def slot_table(route_rows, experts, capacity):
    flat_routes = route_rows.reshape(-1).astype(jnp.int32)
    one_hot = (flat_routes[:, None] == jnp.arange(experts, dtype=jnp.int32)[None, :]).astype(jnp.int32)
    earlier = jnp.cumsum(one_hot, axis=0) - one_hot
    position = lax.optimization_barrier(jnp.sum(earlier * one_hot, axis=1))
    return (flat_routes * capacity + position).astype(jnp.int32)

def attend_image(triple):
    queries, keys_img, values_img = triple
    scores = jnp.einsum('qhd,khd->hqk', queries, keys_img, precision=lax.Precision.HIGHEST) * SCORE_SCALE
    scores = low_back(scores)
    probability = low(jax.nn.softmax(scores, axis=-1))
    blended = jnp.einsum('hqk,khd->qhd', probability, values_img, precision=lax.Precision.HIGHEST)
    return blended.reshape(L, H * HD)

def expert_block(member, in_low, out_low):
    rows_block, routes_block, gates_block = member
    slots = slot_table(routes_block, E, CAP)
    token_index = (jnp.arange(R * TOP, dtype=jnp.int32) // TOP).astype(jnp.int32)
    dispatched = jnp.zeros((E * CAP, D), jnp.float32).at[slots].set(rows_block[token_index])
    dispatched = dispatched.reshape(E, CAP, D)
    pre = low_back(jnp.einsum('ecd,edf->ecf', dispatched, in_low, precision=lax.Precision.HIGHEST))
    hidden = low(gelu_exact(pre))
    produced = low_back(jnp.einsum('ecf,edf->ecd', hidden, out_low, precision=lax.Precision.HIGHEST))
    pairs = produced.reshape(E * CAP, D)[slots].reshape(R, TOP, D)
    return lax.optimization_barrier(jnp.sum(gates_block[:, :, None] * pairs, axis=1))

def forward(x_float, norm_params, qkv_weight, out_weight, router, expert_in, expert_out, task_ids, routes):
    qkv_low = low(qkv_weight)
    out_low = low(out_weight)
    in_low = low(expert_in)
    eout_low = low(expert_out)
    first_normed = low(norm_forward(x_float, norm_params[0], norm_params[1]))
    triple = jnp.einsum('td,cdh->cth', first_normed, qkv_low, precision=lax.Precision.HIGHEST)
    triple = low_back(low(triple))
    heads = triple.reshape(3, IMAGES, L, H, HD)
    context = lax.map(jax.checkpoint(attend_image), (heads[0], heads[1], heads[2]))
    context = low_back(low(context.reshape(TOKENS, H * HD)))
    attended = low_back(dense(context, out_low.T))
    mid = x_float + attended
    second_normed = low(norm_forward(mid, norm_params[2], norm_params[3]))
    task_onehot = (task_ids[:, None] == jnp.arange(TASKS, dtype=jnp.int32)[None, :]).astype(jnp.float32)
    task_bias = dense(task_onehot, router[D:])
    logits = dense(second_normed, router[:D]) + jnp.repeat(task_bias, L, axis=0)
    chosen = jnp.take_along_axis(logits, routes, axis=1)
    gates = jax.nn.softmax(chosen, axis=-1)
    blocks = (second_normed.reshape(N_DP, R, D), routes.reshape(N_DP, R, TOP), gates.reshape(N_DP, R, TOP))
    mixture = lax.map(jax.checkpoint(lambda member: expert_block(member, in_low, eout_low)), blocks)
    mixture = low_back(mixture.reshape(TOKENS, D))
    return mid + mixture

def adam_update(weight, first, second, average, gradient, clip_scale, rate):
    clipped = clip_scale * gradient
    first_new = BETA_FIRST * first + (1.0 - BETA_FIRST) * clipped
    second_new = BETA_SECOND * second + (1.0 - BETA_SECOND) * clipped * clipped
    first_hat = first_new / (1.0 - BETA_FIRST ** STEP)
    second_hat = second_new / (1.0 - BETA_SECOND ** STEP)
    weight_new = weight - rate * (first_hat / (jnp.sqrt(second_hat) + ADAM_EPS) + WEIGHT_DECAY * weight)
    average_new = EMA_KEEP * average + (1.0 - EMA_KEEP) * weight_new
    return (weight_new, first_new, second_new, average_new)

def reference(x_rows, cotangent, task_ids, routes, norm_params, norm_first, norm_second, norm_ema, qkv_weight, qkv_first, qkv_second, qkv_ema, out_weight, out_first, out_second, out_ema, router, router_first, router_second, router_ema, expert_in, expert_in_first, expert_in_second, expert_in_ema, expert_out, expert_out_first, expert_out_second, expert_out_ema):
    x_float = x_rows.astype(jnp.float32)

    def wrapped(x_in, norms_in, qkv_in, out_in, router_in, exp_in, exp_out):
        return forward(x_in, norms_in, qkv_in, out_in, router_in, exp_in, exp_out, task_ids, routes)
    output, pullback = jax.vjp(wrapped, x_float, norm_params, qkv_weight, out_weight, router, expert_in, expert_out)
    grads = pullback(cotangent.astype(jnp.float32))
    input_grad = grads[0]
    total_squares = jnp.sum(grads[1] * grads[1])
    for gradient in grads[2:]:
        total_squares = total_squares + jnp.sum(gradient * gradient)
    grad_norm = jnp.sqrt(total_squares)
    clip_scale = jnp.minimum(1.0, CLIP_LIMIT / (grad_norm + 1e-06))
    norm_new, norm_first_new, norm_second_new, norm_ema_new = adam_update(norm_params, norm_first, norm_second, norm_ema, grads[1], clip_scale, NORM_RATE)
    qkv_new, qkv_first_new, qkv_second_new, qkv_ema_new = adam_update(qkv_weight, qkv_first, qkv_second, qkv_ema, grads[2], clip_scale, LEARN_RATE)
    out_new, out_first_new, out_second_new, out_ema_new = adam_update(out_weight, out_first, out_second, out_ema, grads[3], clip_scale, LEARN_RATE)
    router_new, router_first_new, router_second_new, router_ema_new = adam_update(router, router_first, router_second, router_ema, grads[4], clip_scale, LEARN_RATE)
    in_new, in_first_new, in_second_new, in_ema_new = adam_update(expert_in, expert_in_first, expert_in_second, expert_in_ema, grads[5], clip_scale, LEARN_RATE)
    eout_new, eout_first_new, eout_second_new, eout_ema_new = adam_update(expert_out, expert_out_first, expert_out_second, expert_out_ema, grads[6], clip_scale, LEARN_RATE)
    return (output, input_grad, grad_norm.reshape(1), norm_new, norm_first_new, norm_second_new, norm_ema_new, qkv_new, qkv_first_new, qkv_second_new, qkv_ema_new, out_new, out_first_new, out_second_new, out_ema_new, router_new, router_first_new, router_second_new, router_ema_new, in_new, in_first_new, in_second_new, in_ema_new, eout_new, eout_first_new, eout_second_new, eout_ema_new)
```

```python
import jax
import jax.numpy as jnp
from jax import lax
from jax.experimental import pallas as pl
from jax.experimental.pallas import tpu as pltpu
from jax.sharding import PartitionSpec as P

D = 384
HD = 64
E = 8
TOP = 4
TASKS = 5
L = 1536
STEP = 10
IMGS = 1
R = 1536
QB = 512
CAP = 1536


NORM_EPS = 1e-06
SCORE_SCALE = 0.125
CLIP_LIMIT = 1.0
BETA_FIRST = 0.9
BETA_SECOND = 0.999
LEARN_RATE = 0.1
NORM_RATE = 0.5
WEIGHT_DECAY = 0.05
ADAM_EPS = 1e-08
EMA_KEEP = 0.6
SQRT_HALF = 0.7071067811865476
INV_SQRT_TWO_PI = 0.3989422804014327


def norm_forward(rows, gain, shift):
    row_mean = jnp.mean(rows, axis=-1, keepdims=True)
    centered = rows - row_mean
    inv_std = lax.rsqrt(jnp.mean(centered * centered, axis=-1, keepdims=True) + NORM_EPS)
    unit = centered * inv_std
    return (unit * gain + shift, unit, inv_std)


def norm_backward(upstream, unit, inv_std, gain):
    scaled = upstream * gain
    inner = jnp.mean(scaled * unit, axis=-1, keepdims=True)
    grad_rows = inv_std * (scaled - jnp.mean(scaled, axis=-1, keepdims=True) - unit * inner)
    return (grad_rows, jnp.sum(upstream * unit, axis=0), jnp.sum(upstream, axis=0))


def gelu_exact(values):
    return 0.5 * values * (1.0 + lax.erf(values * SQRT_HALF))


def gelu_slope(values):
    return 0.5 * (1.0 + lax.erf(values * SQRT_HALF)) + values * INV_SQRT_TWO_PI * jnp.exp(
        -0.5 * values * values
    )


def dense_exact(left, right):
    return jnp.dot(left, right, precision=lax.Precision.HIGHEST, preferred_element_type=jnp.float32)


def slot_table(route_rows, experts, capacity):
    flat_routes = route_rows.reshape(-1)
    one_hot = (flat_routes[:, None] == jnp.arange(experts, dtype=jnp.int32)[None, :]).astype(
        jnp.int32
    )
    earlier = jnp.cumsum(one_hot, axis=0) - one_hot
    position = jnp.sum(earlier * one_hot, axis=1)
    return flat_routes * capacity + position


def attend_image(queries, keys_img, values_img, block_rows):
    blended_parts = []
    total_parts = []
    for offset in range(0, queries.shape[0], block_rows):
        query_block = queries[offset : offset + block_rows]
        scores = (
            jnp.einsum("qhd,khd->hqk", query_block, keys_img, preferred_element_type=jnp.float32)
            * SCORE_SCALE
        )
        row_peak = jnp.max(scores, axis=-1, keepdims=True)
        powers = jnp.exp(scores - row_peak)
        row_total = jnp.sum(powers, axis=-1, keepdims=True)
        probability = (powers / row_total).astype(jnp.bfloat16)
        blended = jnp.einsum(
            "hqk,khd->qhd", probability, values_img, preferred_element_type=jnp.float32
        )
        blended_parts.append(blended.astype(jnp.bfloat16))
        total_parts.append((row_peak + jnp.log(row_total))[:, :, 0])
    return (jnp.concatenate(blended_parts, axis=0), jnp.concatenate(total_parts, axis=1))


def attend_image_back(queries, keys_img, values_img, log_total, grad_context, block_rows):
    query_parts = []
    grad_keys = jnp.zeros(keys_img.shape, jnp.float32)
    grad_values = jnp.zeros(values_img.shape, jnp.float32)
    for offset in range(0, queries.shape[0], block_rows):
        query_block = queries[offset : offset + block_rows]
        grad_block = grad_context[offset : offset + block_rows]
        scores = (
            jnp.einsum("qhd,khd->hqk", query_block, keys_img, preferred_element_type=jnp.float32)
            * SCORE_SCALE
        )
        probability = jnp.exp(scores - log_total[:, offset : offset + block_rows, None])
        prob_low = probability.astype(jnp.bfloat16)
        grad_prob = jnp.einsum(
            "qhd,khd->hqk", grad_block, values_img, preferred_element_type=jnp.float32
        )
        inner = jnp.sum(probability * grad_prob, axis=-1, keepdims=True)
        grad_scores = (probability * (grad_prob - inner)).astype(jnp.bfloat16)
        query_parts.append(
            jnp.einsum("hqk,khd->qhd", grad_scores, keys_img, preferred_element_type=jnp.float32)
            * SCORE_SCALE
        )
        grad_keys = (
            grad_keys
            + jnp.einsum(
                "hqk,qhd->khd", grad_scores, query_block, preferred_element_type=jnp.float32
            )
            * SCORE_SCALE
        )
        grad_values = grad_values + jnp.einsum(
            "hqk,qhd->khd", prob_low, grad_block, preferred_element_type=jnp.float32
        )
    grad_queries = jnp.concatenate(query_parts, axis=0)
    return (
        grad_queries.astype(jnp.bfloat16),
        grad_keys.astype(jnp.bfloat16),
        grad_values.astype(jnp.bfloat16),
    )


def adam_update(weight, first, second, average, gradient, clip_scale, rate):
    clipped = clip_scale * gradient
    first_new = BETA_FIRST * first + (1.0 - BETA_FIRST) * clipped
    second_new = BETA_SECOND * second + (1.0 - BETA_SECOND) * clipped * clipped
    first_hat = first_new / (1.0 - BETA_FIRST**STEP)
    second_hat = second_new / (1.0 - BETA_SECOND**STEP)
    weight_new = weight - rate * (
        first_hat / (jnp.sqrt(second_hat) + ADAM_EPS) + WEIGHT_DECAY * weight
    )
    average_new = EMA_KEEP * average + (1.0 - EMA_KEEP) * weight_new
    return (weight_new, first_new, second_new, average_new)


F32 = jnp.float32
BF16 = jnp.bfloat16
MESH = pl.DeviceIdType.MESH
LOG2E = 1.4426950408889634
NN = ((1,), (0,))
NT = ((1,), (1,))
TN = ((0,), (0,))
GRID_Z, GRID_Y, GRID_X = 4, 2, 2
ROW_BLOCK = 256


def mm(left, right, dims=NN):
    return lax.dot_general(left, right, (dims, ((), ())), preferred_element_type=F32)


def row_stats(rows):
    centered = rows - jnp.mean(rows, axis=-1, keepdims=True)
    inv_std = lax.rsqrt(jnp.mean(centered * centered, axis=-1, keepdims=True) + NORM_EPS)
    return centered * inv_std, inv_std


def row_back(upstream, unit, inv_std, gain):
    scaled = upstream * gain
    inner = jnp.mean(scaled * unit, axis=-1, keepdims=True)
    return inv_std * (scaled - jnp.mean(scaled, axis=-1, keepdims=True) - unit * inner)


def step_kernel(
    x_ref,
    cot_ref,
    task_ref,
    routes_ref,
    norm_ref,
    qkv_ref,
    wo_ref,
    router_ref,
    win_ref,
    wout_ref,
    out_ref,
    igrad_ref,
    red_ref,
    redq_ref,
    small_ref,
    sumsq_ref,
    p_hbm,
    x_sib,
    g_all,
    x1,
    qs,
    ks,
    vs,
    ctx,
    att_s,
    att_r,
    mid,
    x2,
    gates,
    wgt,
    mix,
    gsec,
    gs_r,
    mix_s,
    mix_r,
    gm_own,
    gml,
    gctx,
    gfirst_s,
    gfirst_r,
    gw,
    r1,
    r2,
    r3,
    gq,
    gg,
    q1,
    q2,
    q3,
    ar_s,
    ar_r,
    sc_s,
    sc_r,
    ag_ss,
    ag_rs,
    rs_ss,
    rs_rs,
    gq_ss,
    gq_rs,
    gr_ss,
    gr_rs,
    sib_ss,
    sib_rs,
    att_ss,
    att_rs,
    gs_ss,
    gs_rs,
    ar_ss,
    ar_rs,
    sc_ss,
    sc_rs,
    p_sem,
):
    experts = win_ref.shape[0]
    half = x_ref.shape[0]
    rows_all = 2 * half
    width = qs.shape[1]
    heads = width // HD
    tb = ROW_BLOCK
    blocks = rows_all // tb
    own_blocks = half // tb

    d = lax.axis_index("dp")
    m = lax.axis_index("mp")
    z = d // 4
    y = (d // 2) % 2
    x = d % 2
    sib = (d, 1 - m)
    xn = (d + 1 - 2 * x, m)
    yn = (d + 2 - 4 * y, m)
    zs = [((z + k) % 4) for k in (1, 2, 3)]
    zn = [(zs[k] * 4 + y * 2 + x, m) for k in range(3)]

    barrier = pltpu.get_barrier_semaphore()
    for peer in [sib, xn, yn] + zn:
        pl.semaphore_signal(barrier, inc=1, device_id=peer, device_id_type=MESH)
    pl.semaphore_wait(barrier, 6)

    def rcopy(src, dst, ss, rs, dev):
        return pltpu.make_async_remote_copy(
            src_ref=src, dst_ref=dst, send_sem=ss, recv_sem=rs, device_id=dev, device_id_type=MESH
        )

    def own_rows(b):
        return pl.ds(pl.multiple_of(m * half + b * tb, tb), tb)

    def sib_rows(b):
        return pl.ds(pl.multiple_of((1 - m) * half + b * tb, tb), tb)

    def blk_rows(b):
        return pl.ds(pl.multiple_of(b * tb, tb), tb)

    own_half = pl.ds(pl.multiple_of(m * half, half), half)

    def ag1(e):
        return [
            rcopy(gw.at[:, e, z, y, x], gw.at[:, e, z, y, x], ag_ss.at[e, k], ag_rs.at[e, k], zn[k])
            for k in range(3)
        ]

    def ag2(e):
        return [
            rcopy(gw.at[0, e, :, y, x], gw.at[0, e, :, y, x], ag_ss.at[e, 3], ag_rs.at[e, 3], xn),
            rcopy(gw.at[1, e, :, y, x], gw.at[1, e, :, y, x], ag_ss.at[e, 4], ag_rs.at[e, 4], yn),
        ]

    def ag3(e):
        return [
            rcopy(gw.at[0, e, :, y], gw.at[0, e, :, y], ag_ss.at[e, 5], ag_rs.at[e, 5], yn),
            rcopy(gw.at[1, e, :, :, x], gw.at[1, e, :, :, x], ag_ss.at[e, 6], ag_rs.at[e, 6], xn),
        ]

    def start(copies):
        for c in copies:
            c.start()

    def arrive(copies):
        for c in copies:
            c.wait_recv()

    def sent(copies):
        for c in copies:
            c.wait_send()

    def ag_tick(t):
        @pl.when(jnp.logical_and(t >= 0, t < experts))
        def _():
            arrive(ag1(t))
            start(ag2(t))

        @pl.when(t + 2 < experts)
        def _():
            start(ag1(t + 2))

        @pl.when(jnp.logical_and(t >= 1, t < experts + 1))
        def _():
            arrive(ag2(t - 1))
            start(ag3(t - 1))

        @pl.when(jnp.logical_and(t >= 2, t < experts + 2))
        def _():
            arrive(ag3(t - 2))

    def rs1(e):
        return [
            rcopy(gw.at[0, e, :, 1 - y], r1.at[e, 0], rs_ss.at[e, 0], rs_rs.at[e, 0], yn),
            rcopy(gw.at[1, e, :, :, 1 - x], r1.at[e, 1], rs_ss.at[e, 1], rs_rs.at[e, 1], xn),
        ]

    def rs2(e):
        return [
            rcopy(gw.at[0, e, :, y, 1 - x], r2.at[e, 0], rs_ss.at[e, 2], rs_rs.at[e, 2], xn),
            rcopy(gw.at[1, e, :, 1 - y, x], r2.at[e, 1], rs_ss.at[e, 3], rs_rs.at[e, 3], yn),
        ]

    def rs3(e):
        return [
            rcopy(
                gw.at[:, e, zs[k], y, x], r3.at[e, k], rs_ss.at[e, 4 + k], rs_rs.at[e, 4 + k], zn[k]
            )
            for k in range(3)
        ]

    def rs_tick(t):
        @pl.when(jnp.logical_and(t >= 0, t < experts))
        def _():
            start(rs1(t))

        @pl.when(jnp.logical_and(t >= 1, t < experts + 1))
        def _():
            e = t - 1
            arrive(rs1(e))
            gw[0, e, :, y] = (gw[0, e, :, y].astype(F32) + r1[e, 0].astype(F32)).astype(BF16)
            gw[1, e, :, :, x] = (gw[1, e, :, :, x].astype(F32) + r1[e, 1].astype(F32)).astype(BF16)
            start(rs2(e))

        @pl.when(jnp.logical_and(t >= 2, t < experts + 2))
        def _():
            e = t - 2
            arrive(rs2(e))
            for a in range(2):
                gw[a, e, :, y, x] = (
                    gw[a, e, :, y, x].astype(F32) + r2[e, a].astype(F32)
                ).astype(BF16)
            start(rs3(e))

        @pl.when(jnp.logical_and(t >= 3, t < experts + 3))
        def _():
            e = t - 3
            arrive(rs3(e))
            total = gw[:, e, z, y, x].astype(F32)
            for k in range(3):
                total = total + r3[e, k].astype(F32)
            red_ref[:, e] = total

    gq1 = [
        rcopy(gq.at[:, z, y, x], gq.at[:, z, y, x], gq_ss.at[k], gq_rs.at[k], zn[k])
        for k in range(3)
    ]
    gq2 = [
        rcopy(gq.at[0:2, :, y, x], gq.at[0:2, :, y, x], gq_ss.at[3], gq_rs.at[3], xn),
        rcopy(gq.at[2:4, :, y, x], gq.at[2:4, :, y, x], gq_ss.at[4], gq_rs.at[4], yn),
    ]
    gq3 = [
        rcopy(gq.at[0:2, :, y], gq.at[0:2, :, y], gq_ss.at[5], gq_rs.at[5], yn),
        rcopy(gq.at[2:4, :, :, x], gq.at[2:4, :, :, x], gq_ss.at[6], gq_rs.at[6], xn),
    ]
    gr1 = [
        rcopy(gg.at[0:2, :, 1 - y], q1.at[0], gr_ss.at[0], gr_rs.at[0], yn),
        rcopy(gg.at[2:4, :, :, 1 - x], q1.at[1], gr_ss.at[1], gr_rs.at[1], xn),
    ]
    gr2 = [
        rcopy(gg.at[0:2, :, y, 1 - x], q2.at[0], gr_ss.at[2], gr_rs.at[2], xn),
        rcopy(gg.at[2:4, :, 1 - y, x], q2.at[1], gr_ss.at[3], gr_rs.at[3], yn),
    ]
    gr3 = [
        rcopy(gg.at[:, zs[k], y, x], q3.at[k], gr_ss.at[4 + k], gr_rs.at[4 + k], zn[k])
        for k in range(3)
    ]

    send_x = rcopy(x_ref, x_sib, sib_ss.at[0], sib_rs.at[0], sib)
    send_x.start()
    for c in range(3):
        gq[c, z, y, x] = qkv_ref[c].astype(BF16)
    gq[3, z, y, x] = wo_ref[...].astype(BF16)
    start(gq1)

    def cast_weights(e, carry):
        gw[0, e, z, y, x] = win_ref[e].astype(BF16)
        gw[1, e, z, y, x] = wout_ref[e].astype(BF16)
        return carry

    lax.fori_loop(0, 2, cast_weights, 0)
    start(ag1(0))
    start(ag1(1))
    lax.fori_loop(2, experts, cast_weights, 0)

    def cast_cot(b, carry):
        g_all[own_rows(b), :] = cot_ref[blk_rows(b), :].astype(BF16)
        return carry

    lax.fori_loop(0, own_blocks, cast_cot, 0)
    send_g = rcopy(g_all.at[own_half], g_all.at[own_half], sib_ss.at[1], sib_rs.at[1], sib)
    send_g.start()

    gain1 = norm_ref[0:1, :]
    bias1 = norm_ref[1:2, :]
    gain2 = norm_ref[2:3, :]
    bias2 = norm_ref[3:4, :]

    def first_norm(rows, source, b):
        unit, _ = row_stats(source[blk_rows(b), :].astype(F32))
        x1[rows, :] = (unit * gain1 + bias1).astype(BF16)

    def first_own(b, carry):
        first_norm(own_rows(b), x_ref, b)
        return carry

    def first_sib(b, carry):
        first_norm(sib_rows(b), x_sib, b)
        return carry

    lax.fori_loop(0, own_blocks, first_own, 0)
    arrive(gq1)
    start(gq2)
    send_x.wait_recv()
    lax.fori_loop(0, own_blocks, first_sib, 0)
    arrive(gq2)
    start(gq3)
    ag_tick(jnp.int32(0))
    arrive(gq3)

    def flat(c):
        return gq[c].reshape(D, width)

    def project(b, carry):
        r = blk_rows(b)
        normed = x1[r, :]
        qs[r, :] = (mm(normed, flat(0)).astype(BF16).astype(F32) * SCORE_SCALE).astype(BF16)
        ks[r, :] = mm(normed, flat(1)).astype(BF16)
        vs[r, :] = mm(normed, flat(2)).astype(BF16)
        return carry

    lax.fori_loop(0, blocks, project, 0)

    def att_copy(b):
        r = blk_rows(b)
        return rcopy(att_s.at[r], att_r.at[r], att_ss.at[b], att_rs.at[b], sib)

    def attention(pbuf):
        def p_out(b):
            return pltpu.make_async_copy(pbuf.at[b % 2], p_hbm.at[b], p_sem.at[b % 2])

        def attend(b, carry):
            r = blk_rows(b)

            @pl.when(b >= 2)
            def _():
                p_out(b - 2).wait()

            outs = []
            for h in range(heads):
                cs = slice(h * HD, (h + 1) * HD)
                s = mm(qs[r, cs], ks[:, cs], NT)
                powers = jnp.exp2((s - jnp.max(s, axis=1, keepdims=True)) * LOG2E)
                inv = 1.0 / jnp.sum(powers, axis=1, keepdims=True)
                prob = (powers * inv).astype(BF16)
                pbuf[b % 2, h] = prob
                outs.append(mm(prob, vs[:, cs]))
            p_out(b).start()
            context = jnp.concatenate(outs, axis=1).astype(BF16)
            ctx[r, :] = context
            att_s[r, :] = mm(context, flat(3), NT).astype(BF16)
            att_copy(b).start()

            @pl.when(b == 1)
            def _():
                ag_tick(jnp.int32(1))

            @pl.when(b == 4)
            def _():
                ag_tick(jnp.int32(2))

            return carry

        lax.fori_loop(0, blocks, attend, 0)
        p_out(blocks - 2).wait()
        p_out(blocks - 1).wait()


    pshape = (2, heads, tb, rows_all)
    pl.run_scoped(attention, pltpu.VMEM(pshape, BF16))

    router_main = router_ref[0:D, :]
    router_hi = router_main.astype(BF16)
    router_lo = (router_main - router_hi.astype(F32)).astype(BF16)
    task = task_ref[0]
    n_tasks = router_ref.shape[0] - D
    task_pick = lax.broadcasted_iota(jnp.int32, (n_tasks, experts), 0) == task
    task_bias = jnp.sum(jnp.where(task_pick, router_ref[D:, :], 0.0), axis=0, keepdims=True)
    lane = lax.broadcasted_iota(jnp.int32, (tb, experts), 1)

    def second_norm(rows, source, b, gb):
        att_copy(gb).wait_recv()
        rows_mid = (
            source[blk_rows(b), :].astype(F32)
            + att_s[rows, :].astype(F32)
            + att_r[rows, :].astype(F32)
        )
        mid[rows, :] = rows_mid
        unit, _ = row_stats(rows_mid)
        normed = (unit * gain2 + bias2).astype(BF16)
        x2[rows, :] = normed
        logits = mm(normed, router_hi) + mm(normed, router_lo) + task_bias
        picks = routes_ref[rows, :]
        chosen = lane == picks[:, 0:1]
        for k in range(1, TOP):
            chosen = jnp.logical_or(chosen, lane == picks[:, k : k + 1])
        peak = jnp.max(jnp.where(chosen, logits, -jnp.inf), axis=1, keepdims=True)
        powers = jnp.where(chosen, jnp.exp(logits - peak), 0.0)
        gates[rows, :] = powers / jnp.sum(powers, axis=1, keepdims=True)

    def second_own(b, carry):
        second_norm(own_rows(b), x_ref, b, m * own_blocks + b)
        return carry

    def second_sib(b, carry):
        second_norm(sib_rows(b), x_sib, b, (1 - m) * own_blocks + b)
        return carry

    lax.fori_loop(0, own_blocks, second_own, 0)
    lax.fori_loop(0, own_blocks, second_sib, 0)
    send_g.wait_recv()
    ag_tick(jnp.int32(3))

    def clear(b, carry):
        r = blk_rows(b)
        mix[r, :] = jnp.zeros((tb, D), F32)
        gsec[r, :] = jnp.zeros((tb, D), F32)
        wgt[r, :] = jnp.zeros((tb, experts), F32)
        return carry

    lax.fori_loop(0, blocks, clear, 0)

    def all_experts(g_gate, hid, gpre):
        def expert(e, carry):
            ag_tick(e + 4)
            rs_tick(e - 1)

            def block(b, carry2):
                r = blk_rows(b)
                w_in = gw[0, e].reshape(D, gw.shape[-1])
                w_out = gw[1, e].reshape(D, gw.shape[-1])
                gate = jnp.sum(jnp.where(lane == e, gates[r, :], 0.0), axis=1, keepdims=True)
                pre = mm(x2[r, :], w_in)
                incoming = (gate * g_all[r, :].astype(F32)).astype(BF16)
                g_gate[r, :] = incoming
                grad_hidden = mm(incoming, w_out)
                phi = 0.5 + 0.5 * lax.erf(pre * SQRT_HALF)
                density = jnp.exp2(pre * pre * (-0.5 * LOG2E)) * INV_SQRT_TWO_PI
                hidden = (pre * phi).astype(BF16)
                hid[r, :] = hidden
                grad_pre = (grad_hidden * (phi + pre * density)).astype(BF16)
                gpre[r, :] = grad_pre
                produced = mm(hidden, w_out, NT)
                mix[r, :] += gate * produced
                weight = jnp.sum(incoming.astype(F32) * produced, axis=1, keepdims=True)
                wgt[r, :] = jnp.where(lane == e, weight, wgt[r, :])
                gsec[r, :] += mm(grad_pre, w_in, NT)
                return carry2

            lax.fori_loop(0, blocks, block, 0)
            sent(ag1(e) + ag2(e) + ag3(e))
            shape = gw.shape[2:]
            gw[0, e] = mm(x2[...], gpre[...], TN).reshape(shape).astype(BF16)
            gw[1, e] = mm(g_gate[...], hid[...], TN).reshape(shape).astype(BF16)
            return carry

        lax.fori_loop(0, experts, expert, 0)

    pl.run_scoped(
        all_experts,
        pltpu.VMEM((rows_all, D), BF16),
        pltpu.VMEM((rows_all, gw.shape[-1]), BF16),
        pltpu.VMEM((rows_all, gw.shape[-1]), BF16),
    )
    rs_tick(jnp.int32(experts - 1))

    def gs_copy(b):
        r = blk_rows(b)
        return rcopy(att_s.at[r], gs_r.at[r], gs_ss.at[b], gs_rs.at[b], sib)

    for b in range(blocks):
        att_copy(b).wait_send()

    ones = jnp.ones((tb, 128), BF16)

    def gate_grad(b, carry):
        rg, tg = carry
        r = blk_rows(b)
        share = wgt[r, :]
        grad_logits = share - gates[r, :] * jnp.sum(share, axis=1, keepdims=True)
        high = grad_logits.astype(BF16)
        low = (grad_logits - high.astype(F32)).astype(BF16)
        att_s[r, :] = (gsec[r, :] + mm(high, router_hi, NT)).astype(BF16)
        gs_copy(b).start()
        normed = x2[r, :]
        rg = rg + mm(high, normed, TN) + mm(low, normed, TN)
        tg = tg + mm(high, ones, TN) + mm(low, ones, TN)
        return rg, tg

    rg, tg = lax.fori_loop(
        0,
        blocks,
        gate_grad,
        (jnp.zeros((experts, D), F32), jnp.zeros((experts, 128), F32)),
    )
    task_lane = lax.broadcasted_iota(jnp.int32, (experts, 128), 1) == task
    ar_s[0] = jnp.zeros(ar_s.shape[1:], F32)
    ar_s[0, 8:16, :] = rg
    ar_s[0, 16:24, 0:128] = jnp.where(task_lane, tg, 0.0)

    def mix_out(b, carry):
        mix_s[blk_rows(b), :] = mix[sib_rows(b), :].astype(BF16)
        return carry

    lax.fori_loop(0, own_blocks, mix_out, 0)
    send_mix = rcopy(mix_s, mix_r, sib_ss.at[2], sib_rs.at[2], sib)
    send_mix.start()

    def back_second(rows, gb):
        gs_copy(gb).wait_recv()
        grad_second = att_s[rows, :].astype(F32) + gs_r[rows, :].astype(F32)
        unit, inv_std = row_stats(mid[rows, :])
        back = row_back(grad_second, unit, inv_std, gain2)
        return grad_second, unit, back

    w_o = flat(3)

    def back_own(b, carry):
        gain_sum, bias_sum = carry
        rows = own_rows(b)
        grad_second, unit, back = back_second(rows, m * own_blocks + b)
        grad_mid = cot_ref[blk_rows(b), :] + back
        gm_own[blk_rows(b), :] = grad_mid
        grad_low = grad_mid.astype(BF16)
        gml[rows, :] = grad_low
        gctx[rows, :] = mm(grad_low, w_o).astype(BF16)
        gain_sum = gain_sum + jnp.sum(grad_second * unit, axis=0, keepdims=True)
        bias_sum = bias_sum + jnp.sum(grad_second, axis=0, keepdims=True)
        return gain_sum, bias_sum

    def back_sib(b, carry):
        rows = sib_rows(b)
        grad_second, unit, back = back_second(rows, (1 - m) * own_blocks + b)
        grad_low = (g_all[rows, :].astype(F32) + back).astype(BF16)
        gml[rows, :] = grad_low
        gctx[rows, :] = mm(grad_low, w_o).astype(BF16)
        return carry

    zero_row = jnp.zeros((1, D), F32)
    gain2_grad, bias2_grad = lax.fori_loop(0, own_blocks, back_own, (zero_row, zero_row))
    ar_s[0, 2:3, :] = gain2_grad
    ar_s[0, 3:4, :] = bias2_grad
    lax.fori_loop(0, own_blocks, back_sib, 0)
    qshape = gg.shape[1:]
    gg[3] = mm(gml[...], ctx[...], TN).reshape(qshape).astype(BF16)

    def last_part(pbuf, keys_acc, values_acc, dq):
        def p_in(b):
            return pltpu.make_async_copy(p_hbm.at[b], pbuf.at[b % 2], p_sem.at[b % 2])

        p_in(0).start()
        keys_acc[...] = jnp.zeros(keys_acc.shape, F32)
        values_acc[...] = jnp.zeros(values_acc.shape, F32)

        def attend_back(b, carry):
            r = blk_rows(b)

            @pl.when(b + 1 < blocks)
            def _():
                p_in(b + 1).start()

            p_in(b).wait()
            outs = []
            for h in range(heads):
                cs = slice(h * HD, (h + 1) * HD)
                grad_block = gctx[r, cs]
                inner = jnp.sum(
                    grad_block.astype(F32) * ctx[r, cs].astype(F32), axis=1, keepdims=True
                )
                grad_prob = mm(grad_block, vs[:, cs], NT)
                prob = pbuf[b % 2, h]
                grad_scores = (prob.astype(F32) * (grad_prob - inner)).astype(BF16)
                outs.append(mm(grad_scores, ks[:, cs]) * SCORE_SCALE)
                keys_acc[cs, :] += mm(qs[r, cs], grad_scores, TN)
                values_acc[cs, :] += mm(grad_block, prob, TN)
            dq[r, :] = jnp.concatenate(outs, axis=1).astype(BF16)
            rs_tick(b + experts)
            return carry

        lax.fori_loop(0, blocks, attend_back, 0)

        send_mix.wait_recv()

        def write_out(b, carry):
            r = blk_rows(b)
            rows = own_rows(b)
            out_ref[r, :] = mid[rows, :] + mix[rows, :] + mix_r[r, :].astype(F32)
            return carry

        lax.fori_loop(0, own_blocks, write_out, 0)

        normed = x1[...]
        gg[0] = mm(normed, dq[...], TN).reshape(qshape).astype(BF16)
        gg[1] = mm(normed, keys_acc[...].astype(BF16), ((0,), (1,))).reshape(qshape).astype(BF16)
        gg[2] = mm(normed, values_acc[...].astype(BF16), ((0,), (1,))).reshape(qshape).astype(BF16)
        start(gr1)

        def grad_first(rows):
            return (
                mm(dq[rows, :], flat(0), NT)
                + mm(keys_acc[:, rows].astype(BF16), flat(1), ((0,), (1,)))
                + mm(values_acc[:, rows].astype(BF16), flat(2), ((0,), (1,)))
            )

        def first_back_sib(b, carry):
            gfirst_s[blk_rows(b), :] = grad_first(sib_rows(b)).astype(BF16)
            return carry

        def first_back_own(b, carry):
            mix[blk_rows(b), :] = grad_first(own_rows(b))
            return carry

        lax.fori_loop(0, own_blocks, first_back_sib, 0)
        send_first.start()
        lax.fori_loop(0, own_blocks, first_back_own, 0)

    send_first = rcopy(gfirst_s, gfirst_r, sib_ss.at[3], sib_rs.at[3], sib)
    pl.run_scoped(
        last_part,
        pltpu.VMEM(pshape, BF16),
        pltpu.VMEM((width, rows_all), F32),
        pltpu.VMEM((width, rows_all), F32),
        pltpu.VMEM((rows_all, width), BF16),
    )

    arrive(gr1)
    gg[0:2, :, y] = (gg[0:2, :, y].astype(F32) + q1[0].astype(F32)).astype(BF16)
    gg[2:4, :, :, x] = (gg[2:4, :, :, x].astype(F32) + q1[1].astype(F32)).astype(BF16)
    start(gr2)

    send_first.wait_recv()

    def back_first(b, carry):
        gain_sum, bias_sum = carry
        r = blk_rows(b)
        upstream = mix[r, :] + gfirst_r[r, :].astype(F32)
        unit, inv_std = row_stats(x_ref[r, :].astype(F32))
        igrad_ref[r, :] = gm_own[r, :] + row_back(upstream, unit, inv_std, gain1)
        gain_sum = gain_sum + jnp.sum(upstream * unit, axis=0, keepdims=True)
        bias_sum = bias_sum + jnp.sum(upstream, axis=0, keepdims=True)
        return gain_sum, bias_sum

    gain1_grad, bias1_grad = lax.fori_loop(0, own_blocks, back_first, (zero_row, zero_row))
    ar_s[0, 0:1, :] = gain1_grad
    ar_s[0, 1:2, :] = bias1_grad

    arrive(gr2)
    gg[0:2, :, y, x] = (gg[0:2, :, y, x].astype(F32) + q2[0].astype(F32)).astype(BF16)
    gg[2:4, :, y, x] = (gg[2:4, :, y, x].astype(F32) + q2[1].astype(F32)).astype(BF16)
    start(gr3)

    def sum_all(src, dst, ss, rs):
        for i, peer in enumerate([sib, xn, yn]):
            c = rcopy(src.at[i], dst.at[i], ss.at[i], rs.at[i], peer)
            c.start()
            c.wait()
            src[i + 1] = src[i] + dst[i]
        dst[3 + z] = src[3]
        copies = [
            rcopy(src.at[3], dst.at[3 + z], ss.at[3 + k], rs.at[3 + k], zn[k]) for k in range(3)
        ]
        start(copies)
        for c in copies:
            c.wait()
        return dst[3] + dst[4] + dst[5] + dst[6]

    small = sum_all(ar_s, ar_r, ar_ss, ar_rs)
    small_ref[...] = small

    arrive(gr3)
    total = gg[:, z, y, x].astype(F32)
    for k in range(3):
        total = total + q3[k].astype(F32)
    redq_ref[...] = total

    def squares(e, acc):
        for a in range(2):
            acc = acc + jnp.sum(red_ref[a, e] * red_ref[a, e])
        return acc

    share = 1.0 / (2 * GRID_Z * GRID_Y * GRID_X)
    local_sum = lax.fori_loop(0, experts, squares, jnp.sum(total * total))
    local_sum = local_sum + share * jnp.sum(small * small)
    sc_s[0] = jnp.full(sc_s.shape[1:], local_sum, F32)
    sumsq_ref[...] = sum_all(sc_s, sc_r, sc_ss, sc_rs)

    sent(gq1 + gq2 + gq3 + gr1 + gr2 + gr3)

    def drain(e, carry):
        sent(rs1(e) + rs2(e) + rs3(e))
        return carry

    lax.fori_loop(0, experts, drain, 0)
    for c in [send_x, send_g, send_mix, send_first]:
        c.wait_send()

    def drain_rows(b, carry):
        gs_copy(b).wait_send()
        return carry

    lax.fori_loop(0, blocks, drain_rows, 0)


def step_call(x_rows, cotangent, task_ids, routes, norms, qkv, wo, router, win, wout):
    half = x_rows.shape[0]
    rows_all = 2 * half
    experts, shard, hidden = win.shape
    width = wo.shape[1]
    blocks = rows_all // ROW_BLOCK
    heads = width // HD
    vmem = pl.BlockSpec(memory_space=pltpu.VMEM)
    grid = (GRID_Z, GRID_Y, GRID_X)
    struct = jax.ShapeDtypeStruct
    dma = pltpu.SemaphoreType.DMA
    outs = (
        struct((half, D), F32),
        struct((half, D), F32),
        struct((2, experts, shard, hidden), F32),
        struct((4, shard, width), F32),
        struct((24, D), F32),
        struct((8, 128), F32),
        struct((blocks, heads, ROW_BLOCK, rows_all), BF16),
    )
    scratch = [
        pltpu.VMEM((half, D), BF16),
        pltpu.VMEM((rows_all, D), BF16),
        pltpu.VMEM((rows_all, D), BF16),
        pltpu.VMEM((rows_all, width), BF16),
        pltpu.VMEM((rows_all, width), BF16),
        pltpu.VMEM((rows_all, width), BF16),
        pltpu.VMEM((rows_all, width), BF16),
        pltpu.VMEM((rows_all, D), BF16),
        pltpu.VMEM((rows_all, D), BF16),
        pltpu.VMEM((rows_all, D), F32),
        pltpu.VMEM((rows_all, D), BF16),
        pltpu.VMEM((rows_all, experts), F32),
        pltpu.VMEM((rows_all, experts), F32),
        pltpu.VMEM((rows_all, D), F32),
        pltpu.VMEM((rows_all, D), F32),
        pltpu.VMEM((rows_all, D), BF16),
        pltpu.VMEM((half, D), BF16),
        pltpu.VMEM((half, D), BF16),
        pltpu.VMEM((half, D), F32),
        pltpu.VMEM((rows_all, D), BF16),
        pltpu.VMEM((rows_all, width), BF16),
        pltpu.VMEM((half, D), BF16),
        pltpu.VMEM((half, D), BF16),
        pltpu.VMEM((2, experts) + grid + (shard, hidden), BF16),
        pltpu.VMEM((experts, 2, 4, 2, shard, hidden), BF16),
        pltpu.VMEM((experts, 2, 4, shard, hidden), BF16),
        pltpu.VMEM((experts, 3, 2, shard, hidden), BF16),
        pltpu.VMEM((4,) + grid + (shard, width), BF16),
        pltpu.VMEM((4,) + grid + (shard, width), BF16),
        pltpu.VMEM((2, 2, 4, 2, shard, width), BF16),
        pltpu.VMEM((2, 2, 4, shard, width), BF16),
        pltpu.VMEM((3, 4, shard, width), BF16),
        pltpu.VMEM((4, 24, D), F32),
        pltpu.VMEM((7, 24, D), F32),
        pltpu.VMEM((4, 8, 128), F32),
        pltpu.VMEM((7, 8, 128), F32),
        dma((experts, 7)),
        dma((experts, 7)),
        dma((experts, 7)),
        dma((experts, 7)),
        dma((7,)),
        dma((7,)),
        dma((7,)),
        dma((7,)),
        dma((4,)),
        dma((4,)),
        dma((blocks,)),
        dma((blocks,)),
        dma((blocks,)),
        dma((blocks,)),
        dma((6,)),
        dma((6,)),
        dma((6,)),
        dma((6,)),
        dma((2,)),
    ]
    return pl.pallas_call(
        step_kernel,
        out_shape=outs,
        in_specs=[vmem, vmem, pl.BlockSpec(memory_space=pltpu.SMEM)] + [vmem] * 7,
        out_specs=[vmem] * 6 + [pl.BlockSpec(memory_space=pl.ANY)],
        scratch_shapes=scratch,
        compiler_params=pltpu.CompilerParams(
            collective_id=0, has_side_effects=True, vmem_limit_bytes=64 << 20
        ),
        name="step",
    )(x_rows, cotangent, task_ids, routes, norms, qkv, wo, router, win, wout)


def shards(
    x_rows,
    cotangent,
    task_ids,
    routes,
    norm_params,
    norm_first,
    norm_second,
    norm_ema,
    qkv_weight,
    qkv_first,
    qkv_second,
    qkv_ema,
    out_weight,
    out_first,
    out_second,
    out_ema,
    router,
    router_first,
    router_second,
    router_ema,
    expert_in,
    expert_in_first,
    expert_in_second,
    expert_in_ema,
    expert_out,
    expert_out_first,
    expert_out_second,
    expert_out_ema,
):
    qkv_full, out_full, in_full, eout_full = (
        lax.all_gather(qkv_weight.astype(jnp.bfloat16), "dp", axis=1, tiled=True),
        lax.all_gather(out_weight.astype(jnp.bfloat16), "dp", axis=0, tiled=True),
        lax.all_gather(expert_in.astype(jnp.bfloat16), "dp", axis=1, tiled=True),
        lax.all_gather(expert_out.astype(jnp.bfloat16), "dp", axis=1, tiled=True),
    )
    local_width = qkv_full.shape[2]
    local_heads = local_width // HD
    x_float = x_rows.astype(jnp.float32)
    first_normed, first_unit, first_inv = norm_forward(x_float, norm_params[0], norm_params[1])
    first_all = lax.all_gather(first_normed.astype(jnp.bfloat16), "mp", axis=0, tiled=True)
    triple = jnp.einsum(
        "rd,cdh->crh", first_all, qkv_full, preferred_element_type=jnp.float32
    ).astype(jnp.bfloat16)
    heads = triple.reshape(3, IMGS, L, local_heads, HD)
    context_heads, log_total = lax.map(
        lambda member: attend_image(member[0], member[1], member[2], QB),
        (heads[0], heads[1], heads[2]),
    )
    context = context_heads.reshape(R, local_width)
    attended_part = jnp.einsum("rh,dh->rd", context, out_full, preferred_element_type=jnp.float32)
    attended = lax.psum_scatter(
        attended_part.astype(jnp.bfloat16), "mp", scatter_dimension=0, tiled=True
    ).astype(jnp.float32)
    mid = x_float + attended
    second_normed, second_unit, second_inv = norm_forward(mid, norm_params[2], norm_params[3])
    second_all = lax.all_gather(second_normed.astype(jnp.bfloat16), "mp", axis=0, tiled=True)
    second_float = second_all.astype(jnp.float32)
    task_onehot = (task_ids[:, None] == jnp.arange(TASKS, dtype=jnp.int32)[None, :]).astype(
        jnp.float32
    )
    task_bias = dense_exact(task_onehot, router[D:])
    logits = dense_exact(second_float, router[:D])
    logits = (logits.reshape(IMGS, L, E) + task_bias[:, None, :]).reshape(R, E)
    route_hot = (routes[:, :, None] == jnp.arange(E, dtype=jnp.int32)[None, None, :]).astype(
        jnp.float32
    )
    chosen = jnp.sum(route_hot * logits[:, None, :], axis=-1)
    gates = jax.nn.softmax(chosen, axis=-1)
    slots = slot_table(routes, E, CAP)
    pair_ids = jnp.arange(R * TOP, dtype=jnp.int32)
    slot_pair = jnp.full((E * CAP,), R * TOP, jnp.int32).at[slots].set(pair_ids)
    slot_token = (slot_pair // TOP).reshape(E, CAP)
    gate_padded = jnp.concatenate([gates.reshape(-1), jnp.zeros((1,), jnp.float32)])
    slot_gate = gate_padded[slot_pair].reshape(E, CAP)
    padded_rows = jnp.concatenate([second_all, jnp.zeros((1, D), jnp.bfloat16)], axis=0)

    def expert_forward(carry, member):
        weight_in, weight_out, owners, owner_gate = member
        dispatched = padded_rows[owners]
        pre = jnp.dot(dispatched, weight_in, preferred_element_type=jnp.float32)
        hidden = gelu_exact(pre).astype(jnp.bfloat16)
        produced = jnp.einsum("cf,df->cd", hidden, weight_out, preferred_element_type=jnp.float32)
        return (carry.at[owners].add(owner_gate[:, None] * produced), None)

    mixture_acc, unused = lax.scan(
        expert_forward,
        jnp.zeros((R + 1, D), jnp.float32),
        (in_full, eout_full, slot_token, slot_gate),
    )
    mixture = lax.psum_scatter(
        mixture_acc[:R].astype(jnp.bfloat16), "mp", scatter_dimension=0, tiled=True
    ).astype(jnp.float32)
    output = mid + mixture
    grad_low_all = lax.all_gather(cotangent.astype(jnp.bfloat16), "mp", axis=0, tiled=True)
    grad_padded = jnp.concatenate([grad_low_all, jnp.zeros((1, D), jnp.bfloat16)], axis=0)

    def expert_backward(carry, member):
        weight_in, weight_out, owners, owner_gate = member
        dispatched = padded_rows[owners]
        pre = jnp.dot(dispatched, weight_in, preferred_element_type=jnp.float32)
        hidden = gelu_exact(pre).astype(jnp.bfloat16)
        produced = jnp.einsum("cf,df->cd", hidden, weight_out, preferred_element_type=jnp.float32)
        incoming = grad_padded[owners].astype(jnp.float32)
        slot_grad_gate = jnp.sum(incoming * produced, axis=-1)
        grad_produced = (owner_gate[:, None] * incoming).astype(jnp.bfloat16)
        grad_hidden = jnp.dot(grad_produced, weight_out, preferred_element_type=jnp.float32)
        grad_pre = (grad_hidden * gelu_slope(pre)).astype(jnp.bfloat16)
        grad_weight_out = jnp.einsum(
            "cd,cf->df", grad_produced, hidden, preferred_element_type=jnp.float32
        )
        grad_weight_in = jnp.einsum(
            "cd,cf->df", dispatched, grad_pre, preferred_element_type=jnp.float32
        )
        grad_dispatched = jnp.einsum(
            "cf,df->cd", grad_pre, weight_in, preferred_element_type=jnp.float32
        )
        return (
            carry.at[owners].add(grad_dispatched),
            (grad_weight_in, grad_weight_out, slot_grad_gate),
        )

    expert_carry, expert_outs = lax.scan(
        expert_backward,
        jnp.zeros((R + 1, D), jnp.float32),
        (in_full, eout_full, slot_token, slot_gate),
    )
    grad_in_stack, grad_eout_stack, slot_grad_gate = expert_outs
    in_reduced, eout_reduced = (
        lax.psum_scatter(grad_in_stack, "dp", scatter_dimension=1, tiled=True),
        lax.psum_scatter(grad_eout_stack, "dp", scatter_dimension=1, tiled=True),
    )
    grad_gates = slot_grad_gate.reshape(-1)[slots].reshape(R, TOP)
    grad_chosen = gates * (grad_gates - jnp.sum(gates * grad_gates, axis=-1, keepdims=True))
    grad_logits = jnp.sum(route_hot * grad_chosen[:, :, None], axis=1)
    router_rows_grad = dense_exact(second_float.T, grad_logits)
    task_rows_grad = dense_exact(task_onehot.T, jnp.sum(grad_logits.reshape(IMGS, L, E), axis=1))
    router_grad_part = jnp.concatenate([router_rows_grad, task_rows_grad], axis=0)
    grad_second_part = expert_carry[:R] + dense_exact(grad_logits, router[:D].T)
    grad_second = lax.psum_scatter(
        grad_second_part.astype(jnp.bfloat16), "mp", scatter_dimension=0, tiled=True
    ).astype(jnp.float32)
    grad_mid_norm, gain_two_grad, shift_two_grad = norm_backward(
        grad_second, second_unit, second_inv, norm_params[2]
    )
    grad_mid = cotangent + grad_mid_norm
    grad_mid_all = lax.all_gather(grad_mid.astype(jnp.bfloat16), "mp", axis=0, tiled=True)
    grad_out_weight = jnp.einsum(
        "rd,rh->dh", grad_mid_all, context, preferred_element_type=jnp.float32
    )
    grad_context = jnp.dot(grad_mid_all, out_full, preferred_element_type=jnp.float32).astype(
        jnp.bfloat16
    )
    grad_context_heads = grad_context.reshape(IMGS, L, local_heads, HD)
    grad_queries, grad_keys, grad_values = lax.map(
        lambda member: attend_image_back(member[0], member[1], member[2], member[3], member[4], QB),
        (heads[0], heads[1], heads[2], log_total, grad_context_heads),
    )
    grad_triple = jnp.stack(
        [
            grad_queries.reshape(R, local_width),
            grad_keys.reshape(R, local_width),
            grad_values.reshape(R, local_width),
        ],
        axis=0,
    )
    grad_qkv_weight = jnp.einsum(
        "rd,crh->cdh", first_all, grad_triple, preferred_element_type=jnp.float32
    )
    grad_first_part = jnp.einsum(
        "crh,cdh->rd", grad_triple, qkv_full, preferred_element_type=jnp.float32
    )
    grad_first = lax.psum_scatter(
        grad_first_part.astype(jnp.bfloat16), "mp", scatter_dimension=0, tiled=True
    ).astype(jnp.float32)
    grad_x_norm, gain_one_grad, shift_one_grad = norm_backward(
        grad_first, first_unit, first_inv, norm_params[0]
    )
    input_grad = grad_mid + grad_x_norm
    norm_grad_part = jnp.stack(
        [gain_one_grad, shift_one_grad, gain_two_grad, shift_two_grad], axis=0
    )
    norm_grad, router_grad = lax.psum((norm_grad_part, router_grad_part), ("dp", "mp"))
    qkv_reduced, out_reduced = (
        lax.psum_scatter(grad_qkv_weight, "dp", scatter_dimension=1, tiled=True),
        lax.psum_scatter(grad_out_weight, "dp", scatter_dimension=0, tiled=True),
    )
    local_squares = (
        jnp.sum(qkv_reduced * qkv_reduced)
        + jnp.sum(out_reduced * out_reduced)
        + jnp.sum(in_reduced * in_reduced)
        + jnp.sum(eout_reduced * eout_reduced)
    )
    share = 1.0 / (lax.axis_size("dp") * lax.axis_size("mp"))
    small_squares = jnp.sum(norm_grad * norm_grad) + jnp.sum(router_grad * router_grad)
    total_squares = lax.psum(local_squares + share * small_squares, ("dp", "mp"))
    grad_norm = jnp.sqrt(total_squares)
    clip_scale = jnp.minimum(1.0, CLIP_LIMIT / (grad_norm + 1e-06))
    norm_new, norm_first_new, norm_second_new, norm_ema_new = adam_update(
        norm_params, norm_first, norm_second, norm_ema, norm_grad, clip_scale, NORM_RATE
    )
    qkv_new, qkv_first_new, qkv_second_new, qkv_ema_new = adam_update(
        qkv_weight, qkv_first, qkv_second, qkv_ema, qkv_reduced, clip_scale, LEARN_RATE
    )
    out_new, out_first_new, out_second_new, out_ema_new = adam_update(
        out_weight, out_first, out_second, out_ema, out_reduced, clip_scale, LEARN_RATE
    )
    router_new, router_first_new, router_second_new, router_ema_new = adam_update(
        router, router_first, router_second, router_ema, router_grad, clip_scale, LEARN_RATE
    )
    in_new, in_first_new, in_second_new, in_ema_new = adam_update(
        expert_in,
        expert_in_first,
        expert_in_second,
        expert_in_ema,
        in_reduced,
        clip_scale,
        LEARN_RATE,
    )
    eout_new, eout_first_new, eout_second_new, eout_ema_new = adam_update(
        expert_out,
        expert_out_first,
        expert_out_second,
        expert_out_ema,
        eout_reduced,
        clip_scale,
        LEARN_RATE,
    )
    return (
        output,
        input_grad,
        grad_norm.reshape(1),
        norm_new,
        norm_first_new,
        norm_second_new,
        norm_ema_new,
        qkv_new,
        qkv_first_new,
        qkv_second_new,
        qkv_ema_new,
        out_new,
        out_first_new,
        out_second_new,
        out_ema_new,
        router_new,
        router_first_new,
        router_second_new,
        router_ema_new,
        in_new,
        in_first_new,
        in_second_new,
        in_ema_new,
        eout_new,
        eout_first_new,
        eout_second_new,
        eout_ema_new,
    )


def shards_fused(
    x_rows,
    cotangent,
    task_ids,
    routes,
    norm_params,
    norm_first,
    norm_second,
    norm_ema,
    qkv_weight,
    qkv_first,
    qkv_second,
    qkv_ema,
    out_weight,
    out_first,
    out_second,
    out_ema,
    router,
    router_first,
    router_second,
    router_ema,
    expert_in,
    expert_in_first,
    expert_in_second,
    expert_in_ema,
    expert_out,
    expert_out_first,
    expert_out_second,
    expert_out_ema,
):
    output, input_grad, expert_red, qkvo_red, small, squares, unused = step_call(
        x_rows,
        cotangent,
        task_ids,
        routes,
        norm_params,
        qkv_weight,
        out_weight,
        router,
        expert_in,
        expert_out,
    )
    in_reduced, eout_reduced = expert_red[0], expert_red[1]
    qkv_reduced, out_reduced = qkvo_red[0:3], qkvo_red[3]
    norm_grad = small[0:4]
    router_grad = jnp.concatenate([small[8:16].T, small[16:24, 0:TASKS].T], axis=0)
    total_squares = squares[0, 0]
    grad_norm = jnp.sqrt(total_squares)
    clip_scale = jnp.minimum(1.0, CLIP_LIMIT / (grad_norm + 1e-06))
    norm_new, norm_first_new, norm_second_new, norm_ema_new = adam_update(
        norm_params, norm_first, norm_second, norm_ema, norm_grad, clip_scale, NORM_RATE
    )
    qkv_new, qkv_first_new, qkv_second_new, qkv_ema_new = adam_update(
        qkv_weight, qkv_first, qkv_second, qkv_ema, qkv_reduced, clip_scale, LEARN_RATE
    )
    out_new, out_first_new, out_second_new, out_ema_new = adam_update(
        out_weight, out_first, out_second, out_ema, out_reduced, clip_scale, LEARN_RATE
    )
    router_new, router_first_new, router_second_new, router_ema_new = adam_update(
        router, router_first, router_second, router_ema, router_grad, clip_scale, LEARN_RATE
    )
    in_new, in_first_new, in_second_new, in_ema_new = adam_update(
        expert_in,
        expert_in_first,
        expert_in_second,
        expert_in_ema,
        in_reduced,
        clip_scale,
        LEARN_RATE,
    )
    eout_new, eout_first_new, eout_second_new, eout_ema_new = adam_update(
        expert_out,
        expert_out_first,
        expert_out_second,
        expert_out_ema,
        eout_reduced,
        clip_scale,
        LEARN_RATE,
    )
    return (
        output,
        input_grad,
        grad_norm.reshape(1),
        norm_new,
        norm_first_new,
        norm_second_new,
        norm_ema_new,
        qkv_new,
        qkv_first_new,
        qkv_second_new,
        qkv_ema_new,
        out_new,
        out_first_new,
        out_second_new,
        out_ema_new,
        router_new,
        router_first_new,
        router_second_new,
        router_ema_new,
        in_new,
        in_first_new,
        in_second_new,
        in_ema_new,
        eout_new,
        eout_first_new,
        eout_second_new,
        eout_ema_new,
    )


def solution(mesh):
    fused = mesh.shape["dp"] == GRID_Z * GRID_Y * GRID_X and mesh.shape["mp"] == 2
    return jax.shard_map(
        shards_fused if fused else shards,
        mesh=mesh,
        in_specs=(
            P(("dp", "mp"), None),
            P(("dp", "mp"), None),
            P("dp"),
            P("dp", None),
            P(),
            P(),
            P(),
            P(),
            P(None, "dp", "mp"),
            P(None, "dp", "mp"),
            P(None, "dp", "mp"),
            P(None, "dp", "mp"),
            P("dp", "mp"),
            P("dp", "mp"),
            P("dp", "mp"),
            P("dp", "mp"),
            P(),
            P(),
            P(),
            P(),
            P(None, "dp", "mp"),
            P(None, "dp", "mp"),
            P(None, "dp", "mp"),
            P(None, "dp", "mp"),
            P(None, "dp", "mp"),
            P(None, "dp", "mp"),
            P(None, "dp", "mp"),
            P(None, "dp", "mp"),
        ),
        out_specs=(
            P(("dp", "mp"), None),
            P(("dp", "mp"), None),
            P(),
            P(),
            P(),
            P(),
            P(),
            P(None, "dp", "mp"),
            P(None, "dp", "mp"),
            P(None, "dp", "mp"),
            P(None, "dp", "mp"),
            P("dp", "mp"),
            P("dp", "mp"),
            P("dp", "mp"),
            P("dp", "mp"),
            P(),
            P(),
            P(),
            P(),
            P(None, "dp", "mp"),
            P(None, "dp", "mp"),
            P(None, "dp", "mp"),
            P(None, "dp", "mp"),
            P(None, "dp", "mp"),
            P(None, "dp", "mp"),
            P(None, "dp", "mp"),
            P(None, "dp", "mp"),
        ),
        check_vma=False,
    )
```

```python
import jax
import jax.numpy as jnp
from jax import lax
from jax.experimental import pallas as pl
from jax.experimental.pallas import tpu as pltpu
from jax.sharding import PartitionSpec as P

D = 384
HD = 64
E = 8
TOP = 4
TASKS = 5
L = 1536
STEP = 10
IMGS = 1
R = 1536
QB = 512
CAP = 1536


NORM_EPS = 1e-06
SCORE_SCALE = 0.125
CLIP_LIMIT = 1.0
BETA_FIRST = 0.9
BETA_SECOND = 0.999
LEARN_RATE = 0.1
NORM_RATE = 0.5
WEIGHT_DECAY = 0.05
ADAM_EPS = 1e-08
EMA_KEEP = 0.6
SQRT_HALF = 0.7071067811865476
INV_SQRT_TWO_PI = 0.3989422804014327


def norm_forward(rows, gain, shift):
    row_mean = jnp.mean(rows, axis=-1, keepdims=True)
    centered = rows - row_mean
    inv_std = lax.rsqrt(jnp.mean(centered * centered, axis=-1, keepdims=True) + NORM_EPS)
    unit = centered * inv_std
    return (unit * gain + shift, unit, inv_std)


def norm_backward(upstream, unit, inv_std, gain):
    scaled = upstream * gain
    inner = jnp.mean(scaled * unit, axis=-1, keepdims=True)
    grad_rows = inv_std * (scaled - jnp.mean(scaled, axis=-1, keepdims=True) - unit * inner)
    return (grad_rows, jnp.sum(upstream * unit, axis=0), jnp.sum(upstream, axis=0))


def gelu_exact(values):
    return 0.5 * values * (1.0 + lax.erf(values * SQRT_HALF))


def gelu_slope(values):
    return 0.5 * (1.0 + lax.erf(values * SQRT_HALF)) + values * INV_SQRT_TWO_PI * jnp.exp(
        -0.5 * values * values
    )


def dense_exact(left, right):
    return jnp.dot(left, right, precision=lax.Precision.HIGHEST, preferred_element_type=jnp.float32)


def slot_table(route_rows, experts, capacity):
    flat_routes = route_rows.reshape(-1)
    one_hot = (flat_routes[:, None] == jnp.arange(experts, dtype=jnp.int32)[None, :]).astype(
        jnp.int32
    )
    earlier = jnp.cumsum(one_hot, axis=0) - one_hot
    position = jnp.sum(earlier * one_hot, axis=1)
    return flat_routes * capacity + position


def attend_image(queries, keys_img, values_img, block_rows):
    blended_parts = []
    total_parts = []
    for offset in range(0, queries.shape[0], block_rows):
        query_block = queries[offset : offset + block_rows]
        scores = (
            jnp.einsum("qhd,khd->hqk", query_block, keys_img, preferred_element_type=jnp.float32)
            * SCORE_SCALE
        )
        row_peak = jnp.max(scores, axis=-1, keepdims=True)
        powers = jnp.exp(scores - row_peak)
        row_total = jnp.sum(powers, axis=-1, keepdims=True)
        probability = (powers / row_total).astype(jnp.bfloat16)
        blended = jnp.einsum(
            "hqk,khd->qhd", probability, values_img, preferred_element_type=jnp.float32
        )
        blended_parts.append(blended.astype(jnp.bfloat16))
        total_parts.append((row_peak + jnp.log(row_total))[:, :, 0])
    return (jnp.concatenate(blended_parts, axis=0), jnp.concatenate(total_parts, axis=1))


def attend_image_back(queries, keys_img, values_img, log_total, grad_context, block_rows):
    query_parts = []
    grad_keys = jnp.zeros(keys_img.shape, jnp.float32)
    grad_values = jnp.zeros(values_img.shape, jnp.float32)
    for offset in range(0, queries.shape[0], block_rows):
        query_block = queries[offset : offset + block_rows]
        grad_block = grad_context[offset : offset + block_rows]
        scores = (
            jnp.einsum("qhd,khd->hqk", query_block, keys_img, preferred_element_type=jnp.float32)
            * SCORE_SCALE
        )
        probability = jnp.exp(scores - log_total[:, offset : offset + block_rows, None])
        prob_low = probability.astype(jnp.bfloat16)
        grad_prob = jnp.einsum(
            "qhd,khd->hqk", grad_block, values_img, preferred_element_type=jnp.float32
        )
        inner = jnp.sum(probability * grad_prob, axis=-1, keepdims=True)
        grad_scores = (probability * (grad_prob - inner)).astype(jnp.bfloat16)
        query_parts.append(
            jnp.einsum("hqk,khd->qhd", grad_scores, keys_img, preferred_element_type=jnp.float32)
            * SCORE_SCALE
        )
        grad_keys = (
            grad_keys
            + jnp.einsum(
                "hqk,qhd->khd", grad_scores, query_block, preferred_element_type=jnp.float32
            )
            * SCORE_SCALE
        )
        grad_values = grad_values + jnp.einsum(
            "hqk,qhd->khd", prob_low, grad_block, preferred_element_type=jnp.float32
        )
    grad_queries = jnp.concatenate(query_parts, axis=0)
    return (
        grad_queries.astype(jnp.bfloat16),
        grad_keys.astype(jnp.bfloat16),
        grad_values.astype(jnp.bfloat16),
    )


def adam_update(weight, first, second, average, gradient, clip_scale, rate):
    clipped = clip_scale * gradient
    first_new = BETA_FIRST * first + (1.0 - BETA_FIRST) * clipped
    second_new = BETA_SECOND * second + (1.0 - BETA_SECOND) * clipped * clipped
    first_hat = first_new / (1.0 - BETA_FIRST**STEP)
    second_hat = second_new / (1.0 - BETA_SECOND**STEP)
    weight_new = weight - rate * (
        first_hat / (jnp.sqrt(second_hat) + ADAM_EPS) + WEIGHT_DECAY * weight
    )
    average_new = EMA_KEEP * average + (1.0 - EMA_KEEP) * weight_new
    return (weight_new, first_new, second_new, average_new)


F32 = jnp.float32
BF16 = jnp.bfloat16
MESH = pl.DeviceIdType.MESH
LOG2E = 1.4426950408889634
NN = ((1,), (0,))
NT = ((1,), (1,))
TN = ((0,), (0,))
TT = ((0,), (1,))
GRID_Z, GRID_Y, GRID_X = 4, 2, 2
ROW_BLOCK = 256


def mm(left, right, dims=NN):
    return lax.dot_general(left, right, (dims, ((), ())), preferred_element_type=F32)


def row_stats(rows):
    centered = rows - jnp.mean(rows, axis=-1, keepdims=True)
    inv_std = lax.rsqrt(jnp.mean(centered * centered, axis=-1, keepdims=True) + NORM_EPS)
    return centered * inv_std, inv_std


def row_back(upstream, unit, inv_std, gain):
    scaled = upstream * gain
    inner = jnp.mean(scaled * unit, axis=-1, keepdims=True)
    return inv_std * (scaled - jnp.mean(scaled, axis=-1, keepdims=True) - unit * inner)


def step_kernel(
    x_ref,
    cot_ref,
    task_ref,
    routes_ref,
    norm_ref,
    qkv_ref,
    wo_ref,
    router_ref,
    win_ref,
    wout_ref,
    out_ref,
    igrad_ref,
    red_ref,
    redq_ref,
    small_ref,
    late_ref,
    p_hbm,
    x_sib,
    g_all,
    x1,
    qs,
    ks,
    vs,
    ctx,
    att_s,
    att_r,
    mid,
    x2,
    gates,
    wgt_t,
    mix,
    gsec,
    gs_r,
    mix_s,
    mix_r,
    gctx,
    gfirst_r,
    pair_s,
    pair_r,
    back_r,
    gw,
    gd,
    wsend,
    r1,
    r2,
    r3,
    r4,
    gq,
    gg,
    q1,
    q2,
    q3,
    ar_s,
    ar_g,
    ar_z,
    la_s,
    la_g,
    la_z,
    ag_ss,
    ag_rs,
    rs_ss,
    rs_rs,
    gq_ss,
    gq_rs,
    gr_ss,
    gr_rs,
    sib_ss,
    sib_rs,
    near_ss,
    near_rs,
    x2_ss,
    x2_rs,
    x2f_ss,
    x2f_rs,
    att_ss,
    att_rs,
    gs_ss,
    gs_rs,
    ar_ss,
    ar_rs,
    la_ss,
    la_rs,
    p_sem,
    in_sem,
):
    experts = win_ref.shape[0]
    local = experts // 2
    half = x_ref.shape[0]
    rows_all = 2 * half
    width = qs.shape[1]
    hidden_width = gw.shape[-1]
    heads = width // HD
    tb = ROW_BLOCK
    blocks = rows_all // tb
    own_blocks = half // tb
    pshape = (2, heads, tb, rows_all)
    wshape = gw.shape[2:]
    qshape = gg.shape[1:]

    d = lax.axis_index("dp")
    m = lax.axis_index("mp")
    z = d // 4
    y = (d // 2) % 2
    x = d % 2
    zg = z // 2
    zl = z % 2
    zp = z + 1 - 2 * zl
    sib = (d, 1 - m)
    xn = (d + 1 - 2 * x, m)
    yn = (d + 2 - 4 * y, m)
    near = (zp * 4 + y * 2 + x, m)
    far = ((z + 2 - 4 * zg) * 4 + y * 2 + x, m)
    zs = [((z + k) % 4) for k in (1, 2, 3)]
    zn = [(zs[k] * 4 + y * 2 + x, m) for k in range(3)]
    base = zl * local
    other = (1 - zl) * local

    load_in = pltpu.make_async_copy(win_ref, red_ref.at[0], in_sem.at[0])
    load_out = pltpu.make_async_copy(wout_ref, red_ref.at[1], in_sem.at[1])
    load_cot = pltpu.make_async_copy(cot_ref, igrad_ref, in_sem.at[2])
    for c in [load_in, load_out, load_cot]:
        c.start()

    barrier = pltpu.get_barrier_semaphore()
    plane = [
        (
            z * 4 + (y + a * (1 - 2 * y)) * 2 + (x + b * (1 - 2 * x)),
            m + c * (1 - 2 * m),
        )
        for a in (0, 1)
        for b in (0, 1)
        for c in (0, 1)
        if a + b + c > 0
    ]
    for peer in plane + zn:
        pl.semaphore_signal(barrier, inc=1, device_id=peer, device_id_type=MESH)
    pl.semaphore_wait(barrier, 10)

    def rcopy(src, dst, ss, rs, dev):
        return pltpu.make_async_remote_copy(
            src_ref=src, dst_ref=dst, send_sem=ss, recv_sem=rs, device_id=dev, device_id_type=MESH
        )

    def start(copies):
        for c in copies:
            c.start()

    def arrive(copies):
        for c in copies:
            c.wait_recv()

    def sent(copies):
        for c in copies:
            c.wait_send()

    def blk_rows(b):
        return pl.ds(pl.multiple_of(b * tb, tb), tb)

    def own_rows(b):
        return pl.ds(pl.multiple_of(m * half + b * tb, tb), tb)

    def sib_rows(b):
        return pl.ds(pl.multiple_of((1 - m) * half + b * tb, tb), tb)

    own_half = pl.ds(pl.multiple_of(m * half, half), half)

    zpair = pl.ds(zg * 2, 2)
    zaway = pl.ds((1 - zg) * 2, 2)

    def ag0(i):
        return [
            rcopy(wsend.at[:, i], gw.at[:, i, z, y, x], ag_ss.at[i, 0], ag_rs.at[i, 0], near)
        ]

    def ag1(i):
        part = gw.at[:, i, zpair, y, x]
        return [rcopy(part, part, ag_ss.at[i, 1], ag_rs.at[i, 1], far)]

    def ag2(i):
        return [
            rcopy(gw.at[0, i, :, y, x], gw.at[0, i, :, y, x], ag_ss.at[i, 2], ag_rs.at[i, 2], xn),
            rcopy(gw.at[1, i, :, y, x], gw.at[1, i, :, y, x], ag_ss.at[i, 3], ag_rs.at[i, 3], yn),
        ]

    def ag3(i):
        return [
            rcopy(gw.at[0, i, :, y], gw.at[0, i, :, y], ag_ss.at[i, 4], ag_rs.at[i, 4], yn),
            rcopy(gw.at[1, i, :, :, x], gw.at[1, i, :, :, x], ag_ss.at[i, 5], ag_rs.at[i, 5], xn),
        ]

    def ag_tick(t):
        if 0 <= t < local:
            arrive(ag0(t))
            start(ag1(t))
        if 0 <= t - 1 < local:
            arrive(ag1(t - 1))
            start(ag2(t - 1))
        if 0 <= t - 2 < local:
            arrive(ag2(t - 2))
            start(ag3(t - 2))

    def rs1(i):
        return [
            rcopy(gd.at[0, i, :, 1 - y], r1.at[i, 0], rs_ss.at[i, 0], rs_rs.at[i, 0], yn),
            rcopy(gd.at[1, i, :, :, 1 - x], r1.at[i, 1], rs_ss.at[i, 1], rs_rs.at[i, 1], xn),
        ]

    def rs2(i):
        return [
            rcopy(gd.at[0, i, :, y, 1 - x], r2.at[i, 0], rs_ss.at[i, 2], rs_rs.at[i, 2], xn),
            rcopy(gd.at[1, i, :, 1 - y, x], r2.at[i, 1], rs_ss.at[i, 3], rs_rs.at[i, 3], yn),
        ]

    def rs3(i):
        return [
            rcopy(gd.at[:, i, zaway, y, x], r3.at[i], rs_ss.at[i, 4], rs_rs.at[i, 4], far)
        ]

    def rs4(i):
        return [rcopy(gd.at[:, i, zp, y, x], r4.at[i], rs_ss.at[i, 5], rs_rs.at[i, 5], near)]

    def add_low(one, two):
        return (one.astype(F32) + two.astype(F32)).astype(BF16)

    def rs_b(i):
        arrive(rs1(i))
        gd[0, i, :, y] = add_low(gd[0, i, :, y], r1[i, 0])
        gd[1, i, :, :, x] = add_low(gd[1, i, :, :, x], r1[i, 1])
        start(rs2(i))

    def rs_c(i):
        arrive(rs2(i))
        for a in range(2):
            gd[a, i, :, y, x] = add_low(gd[a, i, :, y, x], r2[i, a])
        start(rs3(i))

    def rs_d(i):
        arrive(rs3(i))
        red_ref[:, base + i] = gd[:, i, z, y, x].astype(F32) + r3[i, :, zl].astype(F32)
        gd[:, i, zp, y, x] = add_low(gd[:, i, zp, y, x], r3[i, :, 1 - zl])
        start(rs4(i))

    def rs_e(i):
        arrive(rs4(i))
        red_ref[:, other + i] = r4[i].astype(F32)

    gq1 = [
        rcopy(gq.at[:, z, y, x], gq.at[:, z, y, x], gq_ss.at[k], gq_rs.at[k], zn[k])
        for k in range(3)
    ]
    gq2 = [
        rcopy(gq.at[0:2, :, y, x], gq.at[0:2, :, y, x], gq_ss.at[3], gq_rs.at[3], xn),
        rcopy(gq.at[2:4, :, y, x], gq.at[2:4, :, y, x], gq_ss.at[4], gq_rs.at[4], yn),
    ]
    gq3 = [
        rcopy(gq.at[0:2, :, y], gq.at[0:2, :, y], gq_ss.at[5], gq_rs.at[5], yn),
        rcopy(gq.at[2:4, :, :, x], gq.at[2:4, :, :, x], gq_ss.at[6], gq_rs.at[6], xn),
    ]
    gr1 = [
        rcopy(gg.at[0:2, :, 1 - y], q1.at[0], gr_ss.at[0], gr_rs.at[0], yn),
        rcopy(gg.at[2:4, :, :, 1 - x], q1.at[1], gr_ss.at[1], gr_rs.at[1], xn),
    ]
    gr2 = [
        rcopy(gg.at[0:2, :, y, 1 - x], q2.at[0], gr_ss.at[2], gr_rs.at[2], xn),
        rcopy(gg.at[2:4, :, 1 - y, x], q2.at[1], gr_ss.at[3], gr_rs.at[3], yn),
    ]
    gr3 = [
        rcopy(gg.at[:, zs[k], y, x], q3.at[k], gr_ss.at[4 + k], gr_rs.at[4 + k], zn[k])
        for k in range(3)
    ]

    send_x = rcopy(x_ref, x_sib, sib_ss.at[0], sib_rs.at[0], sib)
    own_g = g_all.at[0, own_half]
    pair_g = g_all.at[1, own_half]
    send_g = rcopy(own_g, own_g, sib_ss.at[1], sib_rs.at[1], sib)
    near_g = rcopy(own_g, pair_g, near_ss.at[0], near_rs.at[0], near)
    pass_g = rcopy(pair_g, pair_g, sib_ss.at[2], sib_rs.at[2], sib)
    near_gates = rcopy(gates.at[0], gates.at[1], near_ss.at[1], near_rs.at[1], near)

    def near_x2(b):
        r = own_rows(b)
        return rcopy(x2.at[0, r], x2.at[1, r], x2_ss.at[b], x2_rs.at[b], near)

    def pass_x2(b):
        r = own_rows(b)
        return rcopy(x2.at[1, r], x2.at[1, r], x2f_ss.at[b], x2f_rs.at[b], sib)

    pair_copies = [
        rcopy(pair_s.at[k], pair_r.at[k], sib_ss.at[3 + k], sib_rs.at[3 + k], sib)
        for k in range(2)
    ]
    back_copies = [
        rcopy(x_sib, back_r.at[0], near_ss.at[2], near_rs.at[2], near),
        rcopy(mix_s, back_r.at[1], near_ss.at[3], near_rs.at[3], near),
    ]
    send_mix = rcopy(pair_s.at[1], mix_r, sib_ss.at[5], sib_rs.at[5], sib)
    send_first = rcopy(pair_s.at[0], gfirst_r, sib_ss.at[6], sib_rs.at[6], sib)

    place = (y * 2 + x) * 2 + m

    class SumAll:
        def __init__(self, src, group, line, ss, rs):
            self.src, self.group, self.line = src, group, line
            self.near = [
                rcopy(src.at[0], group.at[place], ss.at[k], rs.at[k], plane[k]) for k in range(7)
            ]
            self.along = [
                rcopy(src.at[1], line.at[z], ss.at[7 + k], rs.at[7 + k], zn[k]) for k in range(3)
            ]

        def one(self):
            start(self.near)
            self.group[place] = self.src[0]

        def two(self):
            arrive(self.near)
            total = self.group[0]
            for k in range(1, 8):
                total = total + self.group[k]
            self.src[1] = total
            start(self.along)
            self.line[z] = total

        def three(self):
            arrive(self.along)
            return (self.line[0] + self.line[1]) + (self.line[2] + self.line[3])

        def done(self):
            sent(self.near + self.along)

    early = SumAll(ar_s, ar_g, ar_z, ar_ss, ar_rs)
    late = SumAll(la_s, la_g, la_z, la_ss, la_rs)

    send_x.start()
    for c in range(3):
        gq[c, z, y, x] = qkv_ref[c].astype(BF16)
    gq[3, z, y, x] = wo_ref[...].astype(BF16)
    start(gq1)

    load_in.wait()
    load_out.wait()

    def cast_weights(i, carry):
        for a in range(2):
            wsend[a, i] = red_ref[a, other + i].astype(BF16)
        start(ag0(i))
        for a in range(2):
            gw[a, i, z, y, x] = red_ref[a, base + i].astype(BF16)
        return carry

    lax.fori_loop(0, local, cast_weights, 0)

    gain1 = norm_ref[0:1, :]
    bias1 = norm_ref[1:2, :]
    gain2 = norm_ref[2:3, :]
    bias2 = norm_ref[3:4, :]

    def first_norm(rows, source, b):
        unit, _ = row_stats(source[blk_rows(b), :].astype(F32))
        x1[rows, :] = (unit * gain1 + bias1).astype(BF16)

    def first_own(b, carry):
        first_norm(own_rows(b), x_ref, b)
        return carry

    def first_sib(b, carry):
        first_norm(sib_rows(b), x_sib, b)
        return carry

    lax.fori_loop(0, own_blocks, first_own, 0)
    arrive(gq1)
    start(gq2)
    ag_tick(0)
    send_x.wait_recv()
    lax.fori_loop(0, own_blocks, first_sib, 0)
    arrive(gq2)
    start(gq3)

    def cast_cot(b, carry):
        g_all[0, own_rows(b), :] = igrad_ref[blk_rows(b), :].astype(BF16)
        return carry

    load_cot.wait()
    lax.fori_loop(0, own_blocks, cast_cot, 0)
    send_g.start()
    ag_tick(1)
    arrive(gq3)

    def flat(c):
        return gq[c].reshape(D, width)

    def project(b, carry):
        r = blk_rows(b)
        normed = x1[r, :]
        qs[r, :] = (mm(normed, flat(0)).astype(BF16).astype(F32) * SCORE_SCALE).astype(BF16)
        ks[r, :] = mm(normed, flat(1)).astype(BF16)
        vs[r, :] = mm(normed, flat(2)).astype(BF16)
        return carry

    lax.fori_loop(0, blocks, project, 0)

    def att_copy(b):
        r = blk_rows(b)
        return rcopy(att_s.at[r], att_r.at[r], att_ss.at[b], att_rs.at[b], sib)

    def attention(pbuf):
        def p_out(b):
            return pltpu.make_async_copy(pbuf.at[b % 2], p_hbm.at[b], p_sem.at[b % 2])

        def attend(b, carry):
            r = blk_rows(b)

            @pl.when(b >= 2)
            def _():
                p_out(b - 2).wait()

            outs = []
            for h in range(heads):
                cs = slice(h * HD, (h + 1) * HD)
                s = mm(qs[r, cs], ks[:, cs], NT)
                powers = jnp.exp2((s - jnp.max(s, axis=1, keepdims=True)) * LOG2E)
                inv = 1.0 / jnp.sum(powers, axis=1, keepdims=True)
                prob = (powers * inv).astype(BF16)
                pbuf[b % 2, h] = prob
                outs.append(mm(prob, vs[:, cs]))
            p_out(b).start()
            context = jnp.concatenate(outs, axis=1).astype(BF16)
            ctx[r, :] = context
            att_s[r, :] = mm(context, flat(3), NT).astype(BF16)
            att_copy(b).start()
            @pl.when(b == 3)
            def _():
                near_g.start()

            for t, when in ((2, 0), (3, 2), (4, 4)):

                @pl.when(b == when)
                def _(t=t):
                    ag_tick(t)

            return carry

        lax.fori_loop(0, blocks, attend, 0)
        p_out(blocks - 2).wait()
        p_out(blocks - 1).wait()

    pl.run_scoped(attention, pltpu.VMEM(pshape, BF16))
    ag_tick(5)

    router_t = router_ref[:, 0:D]
    router_hi = router_t.astype(BF16)
    router_lo = (router_t - router_hi.astype(F32)).astype(BF16)
    task = task_ref[0]
    n_tasks = router_ref.shape[1] - D
    task_lanes = lax.broadcasted_iota(jnp.int32, (experts, n_tasks), 1)
    task_bias = jnp.sum(
        jnp.where(task_lanes == task, router_ref[:, D:], 0.0), axis=1, keepdims=True
    )
    row_id = lax.broadcasted_iota(jnp.int32, (experts, tb), 0)
    gates[0, experts : 2 * experts, :] = jnp.full((experts, rows_all), task.astype(F32), F32)

    def second_norm(rows, source, b, gb):
        att_copy(gb).wait_recv()
        rows_mid = (
            source[blk_rows(b), :].astype(F32)
            + att_s[rows, :].astype(F32)
            + att_r[rows, :].astype(F32)
        )
        mid[rows, :] = rows_mid
        unit, _ = row_stats(rows_mid)
        normed = (unit * gain2 + bias2).astype(BF16)
        x2[0, rows, :] = normed
        logits = mm(router_hi, normed, NT) + mm(router_lo, normed, NT) + task_bias
        chosen = row_id == routes_ref[0:1, rows]
        for k in range(1, TOP):
            chosen = jnp.logical_or(chosen, row_id == routes_ref[k : k + 1, rows])
        peak = jnp.max(jnp.where(chosen, logits, -jnp.inf), axis=0, keepdims=True)
        powers = jnp.where(chosen, jnp.exp(logits - peak), 0.0)
        share = powers / jnp.sum(powers, axis=0, keepdims=True)
        gates[0, 0:experts, rows] = share

    def second_own(b, carry):
        second_norm(own_rows(b), x_ref, b, m * own_blocks + b)
        near_x2(b).start()
        return carry

    def second_sib(b, carry):
        second_norm(sib_rows(b), x_sib, b, (1 - m) * own_blocks + b)
        return carry

    lax.fori_loop(0, own_blocks, second_own, 0)
    lax.fori_loop(0, own_blocks, second_sib, 0)
    near_gates.start()
    send_g.wait_recv()

    def clear(b, carry):
        r = blk_rows(b)
        for st in range(2):
            mix[st, r, :] = jnp.zeros((tb, D), F32)
            gsec[st, r, :] = jnp.zeros((tb, D), F32)
        return carry

    lax.fori_loop(0, blocks, clear, 0)
    wgt_t[...] = jnp.zeros(wgt_t.shape, F32)

    def gate_grad(st, share_all, rows):
        share = wgt_t[st, :, rows]
        grad_logits = share - share_all * jnp.sum(share, axis=0, keepdims=True)
        high = grad_logits.astype(BF16)
        low = (grad_logits - high.astype(F32)).astype(BF16)
        normed = x2[st, rows, :]
        rg = mm(high, normed) + mm(low, normed)
        tg = jnp.sum(grad_logits, axis=1, keepdims=True)
        return gsec[st, rows, :] + mm(high, router_hi, TN), rg, tg

    def pair_rows_in():
        near_gates.wait_recv()
        pass_g.wait_recv()

        def land(b, carry):
            pass_x2(b).wait_recv()
            return carry

        lax.fori_loop(0, own_blocks, land, 0)

    def pass_rows(b, carry):
        near_x2(b).wait_recv()
        pass_x2(b).start()
        return carry

    task_row = lax.broadcasted_iota(jnp.int32, (experts, 128), 1).astype(F32)

    def pair_rows_out():
        def keep(b, carry):
            rg, tg = carry
            rows = own_rows(b)
            upstream, more_rg, more_tg = gate_grad(1, gates[1, 0:experts, rows], rows)
            gsec[1, rows, :] = upstream
            return rg + more_rg, tg + more_tg

        def give(b, carry):
            rg, tg = carry
            rows = sib_rows(b)
            upstream, more_rg, more_tg = gate_grad(1, gates[1, 0:experts, rows], rows)
            pair_s[0, blk_rows(b), :] = upstream.astype(BF16)
            pair_s[1, blk_rows(b), :] = mix[1, rows, :].astype(BF16)
            return rg + more_rg, tg + more_tg

        zero = (jnp.zeros((experts, D), F32), jnp.zeros((experts, 1), F32))
        sums = lax.fori_loop(0, own_blocks, give, zero)
        start(pair_copies)
        rg, tg = lax.fori_loop(0, own_blocks, keep, sums)
        ar_s[0] = jnp.zeros(ar_s.shape[1:], F32)
        ar_s[0, 8:16, :] = rg
        pair_task = gates[1, experts : experts + 1, 0:128]
        ar_s[0, 16:24, 0:128] = jnp.where(task_row == pair_task, tg, 0.0)

    def pair_rows_back():
        arrive(pair_copies)

        def grads(b, carry):
            r = blk_rows(b)
            x_sib[r, :] = (gsec[1, own_rows(b), :] + pair_r[0, r, :].astype(F32)).astype(BF16)
            return carry

        def rows(b, carry):
            r = blk_rows(b)
            mix_s[r, :] = (mix[1, own_rows(b), :] + pair_r[1, r, :].astype(F32)).astype(BF16)
            return carry

        lax.fori_loop(0, own_blocks, grads, 0)
        back_copies[0].start()
        lax.fori_loop(0, own_blocks, rows, 0)
        back_copies[1].start()

    def all_experts(g_gate, hid, gpre):
        def segment(s, carry):
            pair = jnp.logical_and(s >= 2, s < 6)
            st = jnp.where(pair, 1, 0)
            i = s - jnp.where(s >= 6, 4, jnp.where(s >= 2, 2, 0))
            e = base + i
            first = jnp.logical_or(s < 2, jnp.logical_and(s >= 4, s < 6))

            @pl.when(first)
            def _():
                arrive(ag3(i))

            @pl.when(s == 1)
            def _():
                near_g.wait_recv()
                pass_g.start()
                lax.fori_loop(0, own_blocks, pass_rows, 0)

            @pl.when(s == 2)
            def _():
                pair_rows_in()

            @pl.when(s == 3)
            def _():
                start(rs1(0))

            @pl.when(s == 4)
            def _():
                start(rs1(1))
                rs_b(0)

            @pl.when(s == 5)
            def _():
                rs_b(1)
                rs_c(0)

            @pl.when(s == 6)
            def _():
                pair_rows_out()
                rs_c(1)
                rs_d(0)

            @pl.when(s == 7)
            def _():
                pair_rows_back()
                start(rs1(2))
                rs_d(1)

            def block(b, carry2):
                r = blk_rows(b)
                w_in = gw[0, i].reshape(D, hidden_width)
                w_out = gw[1, i].reshape(D, hidden_width)
                gate = gates[st, pl.ds(e, 1), r].T
                pre = mm(x2[st, r, :], w_in)
                incoming = (gate * g_all[st, r, :].astype(F32)).astype(BF16)
                g_gate[r, :] = incoming
                grad_hidden = mm(incoming, w_out)
                phi = 0.5 + 0.5 * lax.erf(pre * SQRT_HALF)
                density = jnp.exp2(pre * pre * (-0.5 * LOG2E)) * INV_SQRT_TWO_PI
                hidden = (pre * phi).astype(BF16)
                hid[r, :] = hidden
                grad_pre = (grad_hidden * (phi + pre * density)).astype(BF16)
                gpre[r, :] = grad_pre
                produced = mm(hidden, w_out, NT)
                mix[st, r, :] += gate * produced
                weight = jnp.sum(incoming.astype(F32) * produced, axis=1, keepdims=True)
                wgt_t[st, pl.ds(e, 1), r] = weight.T
                gsec[st, r, :] += mm(grad_pre, w_in, NT)
                return carry2

            lax.fori_loop(0, blocks, block, 0)

            def keep_sum(a, value):
                @pl.when(first)
                def _():
                    gd[a, i] = value.astype(BF16)

                @pl.when(jnp.logical_not(first))
                def _():
                    gd[a, i] = (gd[a, i].astype(F32) + value).astype(BF16)

            keep_sum(0, mm(x2[st], gpre[...], TN).reshape(wshape))
            keep_sum(1, mm(g_gate[...], hid[...], TN).reshape(wshape))
            return carry

        lax.fori_loop(0, 2 * local, segment, 0)

    pl.run_scoped(
        all_experts,
        pltpu.VMEM((rows_all, D), BF16),
        pltpu.VMEM((rows_all, hidden_width), BF16),
        pltpu.VMEM((rows_all, hidden_width), BF16),
    )
    start(rs1(3))
    rs_b(2)

    def gs_copy(b):
        r = blk_rows(b)
        return rcopy(att_s.at[r], gs_r.at[r], gs_ss.at[b], gs_rs.at[b], sib)

    for b in range(blocks):
        att_copy(b).wait_send()

    def gate_sib(b, carry):
        rg, tg = carry
        rows = sib_rows(b)
        upstream, more_rg, more_tg = gate_grad(0, gates[0, 0:experts, rows], rows)
        att_s[rows, :] = upstream.astype(BF16)
        gs_copy((1 - m) * own_blocks + b).start()
        return rg + more_rg, tg + more_tg

    def gate_own(b, carry):
        rg, tg = carry
        rows = own_rows(b)
        upstream, more_rg, more_tg = gate_grad(0, gates[0, 0:experts, rows], rows)
        att_s[rows, :] = (upstream + back_r[0, blk_rows(b), :].astype(F32)).astype(BF16)
        gs_copy(m * own_blocks + b).start()
        return rg + more_rg, tg + more_tg

    sums = (jnp.zeros((experts, D), F32), jnp.zeros((experts, 1), F32))
    sums = lax.fori_loop(0, own_blocks, gate_sib, sums)
    back_copies[0].wait_recv()
    rg, tg = lax.fori_loop(0, own_blocks, gate_own, sums)
    ar_s[0, 8:16, :] += rg
    ar_s[0, 16:24, 0:128] += jnp.where(task_row == task.astype(F32), tg, 0.0)

    sent(pair_copies)

    def mix_out(b, carry):
        pair_s[1, blk_rows(b), :] = mix[0, sib_rows(b), :].astype(BF16)
        return carry

    lax.fori_loop(0, own_blocks, mix_out, 0)
    send_mix.start()

    gml = att_r
    w_o = flat(3)

    def back_second(rows, gb):
        gs_copy(gb).wait_recv()
        grad_second = att_s[rows, :].astype(F32) + gs_r[rows, :].astype(F32)
        unit, inv_std = row_stats(mid[rows, :])
        back = row_back(grad_second, unit, inv_std, gain2)
        return grad_second, unit, back

    def back_own(b, carry):
        gain_sum, bias_sum = carry
        rows = own_rows(b)
        grad_second, unit, back = back_second(rows, m * own_blocks + b)
        grad_mid = igrad_ref[blk_rows(b), :] + back
        igrad_ref[blk_rows(b), :] = grad_mid
        grad_low = grad_mid.astype(BF16)
        gml[rows, :] = grad_low
        gctx[rows, :] = mm(grad_low, w_o).astype(BF16)
        gain_sum = gain_sum + jnp.sum(grad_second * unit, axis=0, keepdims=True)
        bias_sum = bias_sum + jnp.sum(grad_second, axis=0, keepdims=True)
        return gain_sum, bias_sum

    def back_sib(b, carry):
        rows = sib_rows(b)
        grad_second, unit, back = back_second(rows, (1 - m) * own_blocks + b)
        grad_low = (g_all[0, rows, :].astype(F32) + back).astype(BF16)
        gml[rows, :] = grad_low
        gctx[rows, :] = mm(grad_low, w_o).astype(BF16)
        return carry

    zero_row = jnp.zeros((1, D), F32)
    gain2_grad, bias2_grad = lax.fori_loop(0, own_blocks, back_own, (zero_row, zero_row))
    ar_s[0, 2:3, :] = gain2_grad
    ar_s[0, 3:4, :] = bias2_grad
    early.one()
    lax.fori_loop(0, own_blocks, back_sib, 0)
    gg[3] = mm(gml[...], ctx[...], TN).reshape(qshape).astype(BF16)

    pass_g.wait_send()

    def last_part(pbuf, keys_acc, values_acc):

        def p_in(b):
            return pltpu.make_async_copy(p_hbm.at[b], pbuf.at[b % 2], p_sem.at[b % 2])

        p_in(0).start()
        keys_acc[...] = jnp.zeros(keys_acc.shape, F32)
        values_acc[...] = jnp.zeros(values_acc.shape, F32)

        def attend_back(b, carry):
            r = blk_rows(b)

            @pl.when(b + 1 < blocks)
            def _():
                p_in(b + 1).start()

            p_in(b).wait()
            outs = []
            for h in range(heads):
                cs = slice(h * HD, (h + 1) * HD)
                grad_block = gctx[r, cs]
                inner = jnp.sum(
                    grad_block.astype(F32) * ctx[r, cs].astype(F32), axis=1, keepdims=True
                )
                grad_prob = mm(grad_block, vs[:, cs], NT)
                prob = pbuf[b % 2, h]
                grad_scores = (prob.astype(F32) * (grad_prob - inner)).astype(BF16)
                outs.append(mm(grad_scores, ks[:, cs]) * SCORE_SCALE)
                keys_acc[cs, :] += mm(qs[r, cs], grad_scores, TN)
                values_acc[cs, :] += mm(grad_block, prob, TN)
            g_all[1, r, 0:width] = jnp.concatenate(outs, axis=1).astype(BF16)

            @pl.when(b == 0)
            def _():
                rs_b(3)
                rs_c(2)

            @pl.when(b == 2)
            def _():
                rs_c(3)
                rs_d(2)
                early.two()

            @pl.when(b == 4)
            def _():
                rs_d(3)
                rs_e(0)
                rs_e(1)
                small_ref[...] = early.three()

            return carry

        lax.fori_loop(0, blocks, attend_back, 0)

        normed = x1[...]
        gg[0] = mm(normed, g_all[1, :, 0:width], TN).reshape(qshape).astype(BF16)
        gg[1] = mm(normed, keys_acc[...].astype(BF16), TT).reshape(qshape).astype(BF16)
        gg[2] = mm(normed, values_acc[...].astype(BF16), TT).reshape(qshape).astype(BF16)
        start(gr1)

        def grad_first(rows):
            return (
                mm(g_all[1, rows, 0:width], flat(0), NT)
                + mm(keys_acc[:, rows].astype(BF16), flat(1), TT)
                + mm(values_acc[:, rows].astype(BF16), flat(2), TT)
            )

        def first_back_sib(b, carry):
            pair_s[0, blk_rows(b), :] = grad_first(sib_rows(b)).astype(BF16)
            return carry

        def first_back_own(b, carry):
            gsec[0, blk_rows(b), :] = grad_first(own_rows(b))
            return carry

        lax.fori_loop(0, own_blocks, first_back_sib, 0)
        send_first.start()
        lax.fori_loop(0, own_blocks, first_back_own, 0)

    pl.run_scoped(
        last_part,
        pltpu.VMEM(pshape, BF16),
        pltpu.VMEM((width, rows_all), F32),
        pltpu.VMEM((width, rows_all), F32),
    )

    arrive(gr1)
    gg[0:2, :, y] = add_low(gg[0:2, :, y], q1[0])
    gg[2:4, :, :, x] = add_low(gg[2:4, :, :, x], q1[1])
    start(gr2)
    send_first.wait_recv()

    def back_first(b, carry):
        gain_sum, bias_sum = carry
        r = blk_rows(b)
        upstream = gsec[0, r, :] + gfirst_r[r, :].astype(F32)
        unit, inv_std = row_stats(x_ref[r, :].astype(F32))
        igrad_ref[r, :] += row_back(upstream, unit, inv_std, gain1)
        gain_sum = gain_sum + jnp.sum(upstream * unit, axis=0, keepdims=True)
        bias_sum = bias_sum + jnp.sum(upstream, axis=0, keepdims=True)
        return gain_sum, bias_sum

    gain1_grad, bias1_grad = lax.fori_loop(0, own_blocks, back_first, (zero_row, zero_row))
    la_s[0] = jnp.zeros(la_s.shape[1:], F32)
    la_s[0, 0:1, :] = gain1_grad
    la_s[0, 1:2, :] = bias1_grad

    arrive(gr2)
    gg[0:2, :, y, x] = add_low(gg[0:2, :, y, x], q2[0])
    gg[2:4, :, y, x] = add_low(gg[2:4, :, y, x], q2[1])
    start(gr3)

    send_mix.wait_recv()
    back_copies[1].wait_recv()

    def write_out(b, carry):
        r = blk_rows(b)
        rows = own_rows(b)
        out_ref[r, :] = (
            mid[rows, :]
            + mix[0, rows, :]
            + mix_r[r, :].astype(F32)
            + back_r[1, r, :].astype(F32)
        )
        return carry

    lax.fori_loop(0, own_blocks, write_out, 0)
    rs_e(2)
    rs_e(3)

    arrive(gr3)
    total = gg[:, z, y, x].astype(F32)
    for k in range(3):
        total = total + q3[k].astype(F32)
    redq_ref[...] = total

    def squares(e, acc):
        for a in range(2):
            acc = acc + jnp.sum(red_ref[a, e] * red_ref[a, e])
        return acc

    local_sum = lax.fori_loop(0, experts, squares, jnp.sum(total * total))
    la_s[0, 2:3, :] = jnp.full((1, D), local_sum, F32)
    late.one()
    late.two()
    late_ref[...] = late.three()

    sent(gq1 + gq2 + gq3 + gr1 + gr2 + gr3)
    early.done()
    late.done()
    sent([send_x, send_g, near_g, near_gates, send_mix, send_first] + back_copies)
    for i in range(local):
        sent(ag0(i) + ag1(i) + ag2(i) + ag3(i))
        sent(rs1(i) + rs2(i) + rs3(i) + rs4(i))

    def drain_rows(b, carry):
        gs_copy(b).wait_send()
        return carry

    def drain_own(b, carry):
        near_x2(b).wait_send()
        pass_x2(b).wait_send()
        return carry

    lax.fori_loop(0, blocks, drain_rows, 0)
    lax.fori_loop(0, own_blocks, drain_own, 0)


def step_call(x_rows, cotangent, task_ids, routes, norms, qkv, wo, router, win, wout):
    half = x_rows.shape[0]
    rows_all = 2 * half
    experts, shard, hidden = win.shape
    local = experts // 2
    width = wo.shape[1]
    blocks = rows_all // ROW_BLOCK
    own_blocks = half // ROW_BLOCK
    heads = width // HD
    vmem = pl.BlockSpec(memory_space=pltpu.VMEM)
    hbm = pl.BlockSpec(memory_space=pl.ANY)
    grid = (GRID_Z, GRID_Y, GRID_X)
    struct = jax.ShapeDtypeStruct
    dma = pltpu.SemaphoreType.DMA
    outs = (
        struct((half, D), F32),
        struct((half, D), F32),
        struct((2, experts, shard, hidden), F32),
        struct((4, shard, width), F32),
        struct((24, D), F32),
        struct((8, D), F32),
        struct((blocks, heads, ROW_BLOCK, rows_all), BF16),
    )
    scratch = [
        pltpu.VMEM((half, D), BF16),
        pltpu.VMEM((2, rows_all, D), BF16),
        pltpu.VMEM((rows_all, D), BF16),
        pltpu.VMEM((rows_all, width), BF16),
        pltpu.VMEM((rows_all, width), BF16),
        pltpu.VMEM((rows_all, width), BF16),
        pltpu.VMEM((rows_all, width), BF16),
        pltpu.VMEM((rows_all, D), BF16),
        pltpu.VMEM((rows_all, D), BF16),
        pltpu.VMEM((rows_all, D), F32),
        pltpu.VMEM((2, rows_all, D), BF16),
        pltpu.VMEM((2, 2 * experts, rows_all), F32),
        pltpu.VMEM((2, experts, rows_all), F32),
        pltpu.VMEM((2, rows_all, D), F32),
        pltpu.VMEM((2, rows_all, D), F32),
        pltpu.VMEM((rows_all, D), BF16),
        pltpu.VMEM((half, D), BF16),
        pltpu.VMEM((half, D), BF16),
        pltpu.VMEM((rows_all, width), BF16),
        pltpu.VMEM((half, D), BF16),
        pltpu.VMEM((2, half, D), BF16),
        pltpu.VMEM((2, half, D), BF16),
        pltpu.VMEM((2, half, D), BF16),
        pltpu.VMEM((2, local) + grid + (shard, hidden), BF16),
        pltpu.VMEM((2, local) + grid + (shard, hidden), BF16),
        pltpu.VMEM((2, local, shard, hidden), BF16),
        pltpu.VMEM((local, 2, 4, 2, shard, hidden), BF16),
        pltpu.VMEM((local, 2, 4, shard, hidden), BF16),
        pltpu.VMEM((local, 2, 2, shard, hidden), BF16),
        pltpu.VMEM((local, 2, shard, hidden), BF16),
        pltpu.VMEM((4,) + grid + (shard, width), BF16),
        pltpu.VMEM((4,) + grid + (shard, width), BF16),
        pltpu.VMEM((2, 2, 4, 2, shard, width), BF16),
        pltpu.VMEM((2, 2, 4, shard, width), BF16),
        pltpu.VMEM((3, 4, shard, width), BF16),
        pltpu.VMEM((2, 24, D), F32),
        pltpu.VMEM((8, 24, D), F32),
        pltpu.VMEM((4, 24, D), F32),
        pltpu.VMEM((2, 8, D), F32),
        pltpu.VMEM((8, 8, D), F32),
        pltpu.VMEM((4, 8, D), F32),
    ]
    for size in [
        (local, 6),
        (local, 6),
        (7,),
        (7,),
        (7,),
        (4,),
        (own_blocks,),
        (own_blocks,),
        (blocks,),
        (blocks,),
        (10,),
        (10,),
    ]:
        scratch += [dma(size), dma(size)]
    scratch += [dma((2,)), dma((3,))]
    return pl.pallas_call(
        step_kernel,
        out_shape=outs,
        in_specs=[vmem, hbm, pl.BlockSpec(memory_space=pltpu.SMEM)] + [vmem] * 5 + [hbm] * 2,
        out_specs=[vmem] * 6 + [hbm],
        scratch_shapes=scratch,
        compiler_params=pltpu.CompilerParams(
            collective_id=0, has_side_effects=True, vmem_limit_bytes=64 << 20
        ),
        name="step",
    )(
        x_rows,
        cotangent,
        task_ids,
        routes.T,
        norms,
        qkv,
        wo,
        router.T,
        win,
        wout,
    )


def adam_parts(weight, first, second, average, gradient, clip_scale, rate):
    clipped = clip_scale * gradient
    first_new = BETA_FIRST * first + (1.0 - BETA_FIRST) * clipped
    second_new = BETA_SECOND * second + (1.0 - BETA_SECOND) * clipped * clipped
    first_hat = first_new * (1.0 / (1.0 - BETA_FIRST**STEP))
    second_hat = second_new * (1.0 / (1.0 - BETA_SECOND**STEP))
    weight_new = weight - rate * (
        first_hat / (jnp.sqrt(second_hat) + ADAM_EPS) + WEIGHT_DECAY * weight
    )
    return weight_new, first_new, second_new, EMA_KEEP * average + (1.0 - EMA_KEEP) * weight_new


def adam_kernel(*refs):
    red, redq, small, late, rows_in, back_in = refs[:6]
    state = [refs[6 + 4 * k : 10 + 4 * k] for k in range(6)]
    norm_out, rows_out, back_out = refs[30:33]
    fresh = [refs[33 + 4 * k : 37 + 4 * k] for k in range(6)]
    step = pl.program_id(0)

    rows_out[...] = rows_in[...]
    back_out[...] = back_in[...]
    norm_grad = jnp.concatenate([late[0:2, :], small[2:4, :]], axis=0)
    router_grad = small[8:16, :]
    task_grad = small[16:24, 0:TASKS]
    total = (
        jnp.max(late[2:3, 0:1])
        + jnp.sum(norm_grad * norm_grad)
        + jnp.sum(router_grad * router_grad)
        + jnp.sum(task_grad * task_grad)
    )
    grad_norm = jnp.sqrt(jnp.full((1, 1), total, F32))
    clip = jnp.minimum(1.0, CLIP_LIMIT / (grad_norm + 1e-06))

    def update(k, gradient, rate, *index):
        new = adam_parts(*[r[index] for r in state[k]], gradient, clip, rate)
        for r, v in zip(fresh[k], new):
            r[index] = v

    @pl.when(step == 0)
    def _():
        norm_out[0] = jnp.max(grad_norm)
        update(0, norm_grad, NORM_RATE, slice(None))
        for c in range(3):
            update(1, redq[c], LEARN_RATE, c)
        update(2, redq[3], LEARN_RATE, slice(None))
        update(3, router_grad, LEARN_RATE, slice(None), slice(0, D))
        update(3, task_grad, LEARN_RATE, slice(None), slice(D, D + TASKS))

    update(4, red[0], LEARN_RATE, slice(None))
    update(5, red[1], LEARN_RATE, slice(None))


def adam_call(red, redq, small, late, output, input_grad, state):
    experts, shard, hidden = red.shape[1:]
    per = 2
    steps = experts // per

    def fixed(array):
        rank = len(array.shape)
        return pl.BlockSpec(array.shape, lambda s: (0,) * rank)

    rows = pl.BlockSpec((output.shape[0] // steps, D), lambda s: (s, 0))
    tile = pl.BlockSpec((per, shard, hidden), lambda s: (s, 0, 0))
    specs = []
    for k, group in enumerate(state):
        specs += [tile if k >= 4 else fixed(a) for a in group]
    flat = [a for group in state for a in group]
    struct = jax.ShapeDtypeStruct
    results = pl.pallas_call(
        adam_kernel,
        grid=(steps,),
        out_shape=[struct((1,), F32), struct(output.shape, F32), struct(output.shape, F32)]
        + [struct(a.shape, F32) for a in flat],
        in_specs=[
            pl.BlockSpec((2, per, shard, hidden), lambda s: (0, s, 0, 0)),
            fixed(redq),
            fixed(small),
            fixed(late),
            rows,
            rows,
        ]
        + specs,
        out_specs=[pl.BlockSpec(memory_space=pltpu.SMEM), rows, rows] + specs,
        compiler_params=pltpu.CompilerParams(vmem_limit_bytes=64 << 20),
        name="adam",
    )(red, redq, small, late, output, input_grad, *flat)
    fresh = [results[3 + 4 * k : 7 + 4 * k] for k in range(6)]
    return results[0], results[1], results[2], fresh


def shards(
    x_rows,
    cotangent,
    task_ids,
    routes,
    norm_params,
    norm_first,
    norm_second,
    norm_ema,
    qkv_weight,
    qkv_first,
    qkv_second,
    qkv_ema,
    out_weight,
    out_first,
    out_second,
    out_ema,
    router,
    router_first,
    router_second,
    router_ema,
    expert_in,
    expert_in_first,
    expert_in_second,
    expert_in_ema,
    expert_out,
    expert_out_first,
    expert_out_second,
    expert_out_ema,
):
    qkv_full, out_full, in_full, eout_full = (
        lax.all_gather(qkv_weight.astype(jnp.bfloat16), "dp", axis=1, tiled=True),
        lax.all_gather(out_weight.astype(jnp.bfloat16), "dp", axis=0, tiled=True),
        lax.all_gather(expert_in.astype(jnp.bfloat16), "dp", axis=1, tiled=True),
        lax.all_gather(expert_out.astype(jnp.bfloat16), "dp", axis=1, tiled=True),
    )
    local_width = qkv_full.shape[2]
    local_heads = local_width // HD
    x_float = x_rows.astype(jnp.float32)
    first_normed, first_unit, first_inv = norm_forward(x_float, norm_params[0], norm_params[1])
    first_all = lax.all_gather(first_normed.astype(jnp.bfloat16), "mp", axis=0, tiled=True)
    triple = jnp.einsum(
        "rd,cdh->crh", first_all, qkv_full, preferred_element_type=jnp.float32
    ).astype(jnp.bfloat16)
    heads = triple.reshape(3, IMGS, L, local_heads, HD)
    context_heads, log_total = lax.map(
        lambda member: attend_image(member[0], member[1], member[2], QB),
        (heads[0], heads[1], heads[2]),
    )
    context = context_heads.reshape(R, local_width)
    attended_part = jnp.einsum("rh,dh->rd", context, out_full, preferred_element_type=jnp.float32)
    attended = lax.psum_scatter(
        attended_part.astype(jnp.bfloat16), "mp", scatter_dimension=0, tiled=True
    ).astype(jnp.float32)
    mid = x_float + attended
    second_normed, second_unit, second_inv = norm_forward(mid, norm_params[2], norm_params[3])
    second_all = lax.all_gather(second_normed.astype(jnp.bfloat16), "mp", axis=0, tiled=True)
    second_float = second_all.astype(jnp.float32)
    task_onehot = (task_ids[:, None] == jnp.arange(TASKS, dtype=jnp.int32)[None, :]).astype(
        jnp.float32
    )
    task_bias = dense_exact(task_onehot, router[D:])
    logits = dense_exact(second_float, router[:D])
    logits = (logits.reshape(IMGS, L, E) + task_bias[:, None, :]).reshape(R, E)
    route_hot = (routes[:, :, None] == jnp.arange(E, dtype=jnp.int32)[None, None, :]).astype(
        jnp.float32
    )
    chosen = jnp.sum(route_hot * logits[:, None, :], axis=-1)
    gates = jax.nn.softmax(chosen, axis=-1)
    slots = slot_table(routes, E, CAP)
    pair_ids = jnp.arange(R * TOP, dtype=jnp.int32)
    slot_pair = jnp.full((E * CAP,), R * TOP, jnp.int32).at[slots].set(pair_ids)
    slot_token = (slot_pair // TOP).reshape(E, CAP)
    gate_padded = jnp.concatenate([gates.reshape(-1), jnp.zeros((1,), jnp.float32)])
    slot_gate = gate_padded[slot_pair].reshape(E, CAP)
    padded_rows = jnp.concatenate([second_all, jnp.zeros((1, D), jnp.bfloat16)], axis=0)

    def expert_forward(carry, member):
        weight_in, weight_out, owners, owner_gate = member
        dispatched = padded_rows[owners]
        pre = jnp.dot(dispatched, weight_in, preferred_element_type=jnp.float32)
        hidden = gelu_exact(pre).astype(jnp.bfloat16)
        produced = jnp.einsum("cf,df->cd", hidden, weight_out, preferred_element_type=jnp.float32)
        return (carry.at[owners].add(owner_gate[:, None] * produced), None)

    mixture_acc, unused = lax.scan(
        expert_forward,
        jnp.zeros((R + 1, D), jnp.float32),
        (in_full, eout_full, slot_token, slot_gate),
    )
    mixture = lax.psum_scatter(
        mixture_acc[:R].astype(jnp.bfloat16), "mp", scatter_dimension=0, tiled=True
    ).astype(jnp.float32)
    output = mid + mixture
    grad_low_all = lax.all_gather(cotangent.astype(jnp.bfloat16), "mp", axis=0, tiled=True)
    grad_padded = jnp.concatenate([grad_low_all, jnp.zeros((1, D), jnp.bfloat16)], axis=0)

    def expert_backward(carry, member):
        weight_in, weight_out, owners, owner_gate = member
        dispatched = padded_rows[owners]
        pre = jnp.dot(dispatched, weight_in, preferred_element_type=jnp.float32)
        hidden = gelu_exact(pre).astype(jnp.bfloat16)
        produced = jnp.einsum("cf,df->cd", hidden, weight_out, preferred_element_type=jnp.float32)
        incoming = grad_padded[owners].astype(jnp.float32)
        slot_grad_gate = jnp.sum(incoming * produced, axis=-1)
        grad_produced = (owner_gate[:, None] * incoming).astype(jnp.bfloat16)
        grad_hidden = jnp.dot(grad_produced, weight_out, preferred_element_type=jnp.float32)
        grad_pre = (grad_hidden * gelu_slope(pre)).astype(jnp.bfloat16)
        grad_weight_out = jnp.einsum(
            "cd,cf->df", grad_produced, hidden, preferred_element_type=jnp.float32
        )
        grad_weight_in = jnp.einsum(
            "cd,cf->df", dispatched, grad_pre, preferred_element_type=jnp.float32
        )
        grad_dispatched = jnp.einsum(
            "cf,df->cd", grad_pre, weight_in, preferred_element_type=jnp.float32
        )
        return (
            carry.at[owners].add(grad_dispatched),
            (grad_weight_in, grad_weight_out, slot_grad_gate),
        )

    expert_carry, expert_outs = lax.scan(
        expert_backward,
        jnp.zeros((R + 1, D), jnp.float32),
        (in_full, eout_full, slot_token, slot_gate),
    )
    grad_in_stack, grad_eout_stack, slot_grad_gate = expert_outs
    in_reduced, eout_reduced = (
        lax.psum_scatter(grad_in_stack, "dp", scatter_dimension=1, tiled=True),
        lax.psum_scatter(grad_eout_stack, "dp", scatter_dimension=1, tiled=True),
    )
    grad_gates = slot_grad_gate.reshape(-1)[slots].reshape(R, TOP)
    grad_chosen = gates * (grad_gates - jnp.sum(gates * grad_gates, axis=-1, keepdims=True))
    grad_logits = jnp.sum(route_hot * grad_chosen[:, :, None], axis=1)
    router_rows_grad = dense_exact(second_float.T, grad_logits)
    task_rows_grad = dense_exact(task_onehot.T, jnp.sum(grad_logits.reshape(IMGS, L, E), axis=1))
    router_grad_part = jnp.concatenate([router_rows_grad, task_rows_grad], axis=0)
    grad_second_part = expert_carry[:R] + dense_exact(grad_logits, router[:D].T)
    grad_second = lax.psum_scatter(
        grad_second_part.astype(jnp.bfloat16), "mp", scatter_dimension=0, tiled=True
    ).astype(jnp.float32)
    grad_mid_norm, gain_two_grad, shift_two_grad = norm_backward(
        grad_second, second_unit, second_inv, norm_params[2]
    )
    grad_mid = cotangent + grad_mid_norm
    grad_mid_all = lax.all_gather(grad_mid.astype(jnp.bfloat16), "mp", axis=0, tiled=True)
    grad_out_weight = jnp.einsum(
        "rd,rh->dh", grad_mid_all, context, preferred_element_type=jnp.float32
    )
    grad_context = jnp.dot(grad_mid_all, out_full, preferred_element_type=jnp.float32).astype(
        jnp.bfloat16
    )
    grad_context_heads = grad_context.reshape(IMGS, L, local_heads, HD)
    grad_queries, grad_keys, grad_values = lax.map(
        lambda member: attend_image_back(member[0], member[1], member[2], member[3], member[4], QB),
        (heads[0], heads[1], heads[2], log_total, grad_context_heads),
    )
    grad_triple = jnp.stack(
        [
            grad_queries.reshape(R, local_width),
            grad_keys.reshape(R, local_width),
            grad_values.reshape(R, local_width),
        ],
        axis=0,
    )
    grad_qkv_weight = jnp.einsum(
        "rd,crh->cdh", first_all, grad_triple, preferred_element_type=jnp.float32
    )
    grad_first_part = jnp.einsum(
        "crh,cdh->rd", grad_triple, qkv_full, preferred_element_type=jnp.float32
    )
    grad_first = lax.psum_scatter(
        grad_first_part.astype(jnp.bfloat16), "mp", scatter_dimension=0, tiled=True
    ).astype(jnp.float32)
    grad_x_norm, gain_one_grad, shift_one_grad = norm_backward(
        grad_first, first_unit, first_inv, norm_params[0]
    )
    input_grad = grad_mid + grad_x_norm
    norm_grad_part = jnp.stack(
        [gain_one_grad, shift_one_grad, gain_two_grad, shift_two_grad], axis=0
    )
    norm_grad, router_grad = lax.psum((norm_grad_part, router_grad_part), ("dp", "mp"))
    qkv_reduced, out_reduced = (
        lax.psum_scatter(grad_qkv_weight, "dp", scatter_dimension=1, tiled=True),
        lax.psum_scatter(grad_out_weight, "dp", scatter_dimension=0, tiled=True),
    )
    local_squares = (
        jnp.sum(qkv_reduced * qkv_reduced)
        + jnp.sum(out_reduced * out_reduced)
        + jnp.sum(in_reduced * in_reduced)
        + jnp.sum(eout_reduced * eout_reduced)
    )
    share = 1.0 / (lax.axis_size("dp") * lax.axis_size("mp"))
    small_squares = jnp.sum(norm_grad * norm_grad) + jnp.sum(router_grad * router_grad)
    total_squares = lax.psum(local_squares + share * small_squares, ("dp", "mp"))
    grad_norm = jnp.sqrt(total_squares)
    clip_scale = jnp.minimum(1.0, CLIP_LIMIT / (grad_norm + 1e-06))
    norm_new, norm_first_new, norm_second_new, norm_ema_new = adam_update(
        norm_params, norm_first, norm_second, norm_ema, norm_grad, clip_scale, NORM_RATE
    )
    qkv_new, qkv_first_new, qkv_second_new, qkv_ema_new = adam_update(
        qkv_weight, qkv_first, qkv_second, qkv_ema, qkv_reduced, clip_scale, LEARN_RATE
    )
    out_new, out_first_new, out_second_new, out_ema_new = adam_update(
        out_weight, out_first, out_second, out_ema, out_reduced, clip_scale, LEARN_RATE
    )
    router_new, router_first_new, router_second_new, router_ema_new = adam_update(
        router, router_first, router_second, router_ema, router_grad, clip_scale, LEARN_RATE
    )
    in_new, in_first_new, in_second_new, in_ema_new = adam_update(
        expert_in,
        expert_in_first,
        expert_in_second,
        expert_in_ema,
        in_reduced,
        clip_scale,
        LEARN_RATE,
    )
    eout_new, eout_first_new, eout_second_new, eout_ema_new = adam_update(
        expert_out,
        expert_out_first,
        expert_out_second,
        expert_out_ema,
        eout_reduced,
        clip_scale,
        LEARN_RATE,
    )
    return (
        output,
        input_grad,
        grad_norm.reshape(1),
        norm_new,
        norm_first_new,
        norm_second_new,
        norm_ema_new,
        qkv_new,
        qkv_first_new,
        qkv_second_new,
        qkv_ema_new,
        out_new,
        out_first_new,
        out_second_new,
        out_ema_new,
        router_new,
        router_first_new,
        router_second_new,
        router_ema_new,
        in_new,
        in_first_new,
        in_second_new,
        in_ema_new,
        eout_new,
        eout_first_new,
        eout_second_new,
        eout_ema_new,
    )


def shards_fused(
    x_rows,
    cotangent,
    task_ids,
    routes,
    norm_params,
    norm_first,
    norm_second,
    norm_ema,
    qkv_weight,
    qkv_first,
    qkv_second,
    qkv_ema,
    out_weight,
    out_first,
    out_second,
    out_ema,
    router,
    router_first,
    router_second,
    router_ema,
    expert_in,
    expert_in_first,
    expert_in_second,
    expert_in_ema,
    expert_out,
    expert_out_first,
    expert_out_second,
    expert_out_ema,
):
    output, input_grad, expert_red, qkvo_red, small, late, unused = step_call(
        x_rows,
        cotangent,
        task_ids,
        routes,
        norm_params,
        qkv_weight,
        out_weight,
        router,
        expert_in,
        expert_out,
    )
    state = [
        (norm_params, norm_first, norm_second, norm_ema),
        (qkv_weight, qkv_first, qkv_second, qkv_ema),
        (out_weight, out_first, out_second, out_ema),
        (router.T, router_first.T, router_second.T, router_ema.T),
        (expert_in, expert_in_first, expert_in_second, expert_in_ema),
        (expert_out, expert_out_first, expert_out_second, expert_out_ema),
    ]
    grad_norm, output, input_grad, fresh = adam_call(
        expert_red, qkvo_red, small, late, output, input_grad, state
    )
    fresh[3] = [a.T for a in fresh[3]]
    flat = [a for group in fresh for a in group]
    return (output, input_grad, grad_norm, *flat)


def solution(mesh):
    fused = mesh.shape["dp"] == GRID_Z * GRID_Y * GRID_X and mesh.shape["mp"] == 2
    return jax.shard_map(
        shards_fused if fused else shards,
        mesh=mesh,
        in_specs=(
            P(("dp", "mp"), None),
            P(("dp", "mp"), None),
            P("dp"),
            P("dp", None),
            P(),
            P(),
            P(),
            P(),
            P(None, "dp", "mp"),
            P(None, "dp", "mp"),
            P(None, "dp", "mp"),
            P(None, "dp", "mp"),
            P("dp", "mp"),
            P("dp", "mp"),
            P("dp", "mp"),
            P("dp", "mp"),
            P(),
            P(),
            P(),
            P(),
            P(None, "dp", "mp"),
            P(None, "dp", "mp"),
            P(None, "dp", "mp"),
            P(None, "dp", "mp"),
            P(None, "dp", "mp"),
            P(None, "dp", "mp"),
            P(None, "dp", "mp"),
            P(None, "dp", "mp"),
        ),
        out_specs=(
            P(("dp", "mp"), None),
            P(("dp", "mp"), None),
            P(),
            P(),
            P(),
            P(),
            P(),
            P(None, "dp", "mp"),
            P(None, "dp", "mp"),
            P(None, "dp", "mp"),
            P(None, "dp", "mp"),
            P("dp", "mp"),
            P("dp", "mp"),
            P("dp", "mp"),
            P("dp", "mp"),
            P(),
            P(),
            P(),
            P(),
            P(None, "dp", "mp"),
            P(None, "dp", "mp"),
            P(None, "dp", "mp"),
            P(None, "dp", "mp"),
            P(None, "dp", "mp"),
            P(None, "dp", "mp"),
            P(None, "dp", "mp"),
            P(None, "dp", "mp"),
        ),
        check_vma=False,
    )
```

```python
import jax
import jax.numpy as jnp
from jax import lax
from jax.experimental import pallas as pl
from jax.experimental.pallas import tpu as pltpu
from jax.sharding import PartitionSpec as P

D = 384
HD = 64
E = 8
TOP = 4
TASKS = 5
L = 1536
STEP = 10
IMGS = 1
R = 1536
QB = 512
CAP = 1536


NORM_EPS = 1e-06
SCORE_SCALE = 0.125
CLIP_LIMIT = 1.0
BETA_FIRST = 0.9
BETA_SECOND = 0.999
LEARN_RATE = 0.1
NORM_RATE = 0.5
WEIGHT_DECAY = 0.05
ADAM_EPS = 1e-08
EMA_KEEP = 0.6
SQRT_HALF = 0.7071067811865476
INV_SQRT_TWO_PI = 0.3989422804014327


def norm_forward(rows, gain, shift):
    row_mean = jnp.mean(rows, axis=-1, keepdims=True)
    centered = rows - row_mean
    inv_std = lax.rsqrt(jnp.mean(centered * centered, axis=-1, keepdims=True) + NORM_EPS)
    unit = centered * inv_std
    return (unit * gain + shift, unit, inv_std)


def norm_backward(upstream, unit, inv_std, gain):
    scaled = upstream * gain
    inner = jnp.mean(scaled * unit, axis=-1, keepdims=True)
    grad_rows = inv_std * (scaled - jnp.mean(scaled, axis=-1, keepdims=True) - unit * inner)
    return (grad_rows, jnp.sum(upstream * unit, axis=0), jnp.sum(upstream, axis=0))


def gelu_exact(values):
    return 0.5 * values * (1.0 + lax.erf(values * SQRT_HALF))


def gelu_slope(values):
    return 0.5 * (1.0 + lax.erf(values * SQRT_HALF)) + values * INV_SQRT_TWO_PI * jnp.exp(
        -0.5 * values * values
    )


def dense_exact(left, right):
    return jnp.dot(left, right, precision=lax.Precision.HIGHEST, preferred_element_type=jnp.float32)


def slot_table(route_rows, experts, capacity):
    flat_routes = route_rows.reshape(-1)
    one_hot = (flat_routes[:, None] == jnp.arange(experts, dtype=jnp.int32)[None, :]).astype(
        jnp.int32
    )
    earlier = jnp.cumsum(one_hot, axis=0) - one_hot
    position = jnp.sum(earlier * one_hot, axis=1)
    return flat_routes * capacity + position


def attend_image(queries, keys_img, values_img, block_rows):
    blended_parts = []
    total_parts = []
    for offset in range(0, queries.shape[0], block_rows):
        query_block = queries[offset : offset + block_rows]
        scores = (
            jnp.einsum("qhd,khd->hqk", query_block, keys_img, preferred_element_type=jnp.float32)
            * SCORE_SCALE
        )
        row_peak = jnp.max(scores, axis=-1, keepdims=True)
        powers = jnp.exp(scores - row_peak)
        row_total = jnp.sum(powers, axis=-1, keepdims=True)
        probability = (powers / row_total).astype(jnp.bfloat16)
        blended = jnp.einsum(
            "hqk,khd->qhd", probability, values_img, preferred_element_type=jnp.float32
        )
        blended_parts.append(blended.astype(jnp.bfloat16))
        total_parts.append((row_peak + jnp.log(row_total))[:, :, 0])
    return (jnp.concatenate(blended_parts, axis=0), jnp.concatenate(total_parts, axis=1))


def attend_image_back(queries, keys_img, values_img, log_total, grad_context, block_rows):
    query_parts = []
    grad_keys = jnp.zeros(keys_img.shape, jnp.float32)
    grad_values = jnp.zeros(values_img.shape, jnp.float32)
    for offset in range(0, queries.shape[0], block_rows):
        query_block = queries[offset : offset + block_rows]
        grad_block = grad_context[offset : offset + block_rows]
        scores = (
            jnp.einsum("qhd,khd->hqk", query_block, keys_img, preferred_element_type=jnp.float32)
            * SCORE_SCALE
        )
        probability = jnp.exp(scores - log_total[:, offset : offset + block_rows, None])
        prob_low = probability.astype(jnp.bfloat16)
        grad_prob = jnp.einsum(
            "qhd,khd->hqk", grad_block, values_img, preferred_element_type=jnp.float32
        )
        inner = jnp.sum(probability * grad_prob, axis=-1, keepdims=True)
        grad_scores = (probability * (grad_prob - inner)).astype(jnp.bfloat16)
        query_parts.append(
            jnp.einsum("hqk,khd->qhd", grad_scores, keys_img, preferred_element_type=jnp.float32)
            * SCORE_SCALE
        )
        grad_keys = (
            grad_keys
            + jnp.einsum(
                "hqk,qhd->khd", grad_scores, query_block, preferred_element_type=jnp.float32
            )
            * SCORE_SCALE
        )
        grad_values = grad_values + jnp.einsum(
            "hqk,qhd->khd", prob_low, grad_block, preferred_element_type=jnp.float32
        )
    grad_queries = jnp.concatenate(query_parts, axis=0)
    return (
        grad_queries.astype(jnp.bfloat16),
        grad_keys.astype(jnp.bfloat16),
        grad_values.astype(jnp.bfloat16),
    )


def adam_update(weight, first, second, average, gradient, clip_scale, rate):
    clipped = clip_scale * gradient
    first_new = BETA_FIRST * first + (1.0 - BETA_FIRST) * clipped
    second_new = BETA_SECOND * second + (1.0 - BETA_SECOND) * clipped * clipped
    first_hat = first_new / (1.0 - BETA_FIRST**STEP)
    second_hat = second_new / (1.0 - BETA_SECOND**STEP)
    weight_new = weight - rate * (
        first_hat / (jnp.sqrt(second_hat) + ADAM_EPS) + WEIGHT_DECAY * weight
    )
    average_new = EMA_KEEP * average + (1.0 - EMA_KEEP) * weight_new
    return (weight_new, first_new, second_new, average_new)


F32 = jnp.float32
BF16 = jnp.bfloat16
MESH = pl.DeviceIdType.MESH
LOG2E = 1.4426950408889634
NN = ((1,), (0,))
NT = ((1,), (1,))
TN = ((0,), (0,))
TT = ((0,), (1,))
GRID_Z, GRID_Y, GRID_X = 4, 2, 2
ROW_BLOCK = 256
EXPERT_BLOCK = 512


def mm(left, right, dims=NN):
    return lax.dot_general(left, right, (dims, ((), ())), preferred_element_type=F32)


def row_stats(rows):
    centered = rows - jnp.mean(rows, axis=-1, keepdims=True)
    inv_std = lax.rsqrt(jnp.mean(centered * centered, axis=-1, keepdims=True) + NORM_EPS)
    return centered * inv_std, inv_std


def row_back(upstream, unit, inv_std, gain):
    scaled = upstream * gain
    inner = jnp.mean(scaled * unit, axis=-1, keepdims=True)
    return inv_std * (scaled - jnp.mean(scaled, axis=-1, keepdims=True) - unit * inner)


def step_kernel(
    x_ref,
    cot_ref,
    task_ref,
    routes_ref,
    norm_ref,
    qkv_ref,
    wo_ref,
    router_ref,
    win_ref,
    wout_ref,
    out_ref,
    igrad_ref,
    red_ref,
    redq_ref,
    small_ref,
    late_ref,
    p_hbm,
    x_sib,
    g_all,
    x1,
    qs,
    ks,
    vs,
    ctx,
    att_s,
    att_r,
    mid,
    x2,
    gates,
    wgt_t,
    mix,
    gsec,
    gs_r,
    mix_s,
    mix_r,
    gctx,
    gfirst_r,
    pair_s,
    pair_r,
    back_r,
    gw,
    gd,
    wsend,
    r1,
    r2,
    r3,
    r4,
    gq,
    wq,
    gg,
    q1,
    q2,
    q3,
    ar_s,
    ar_g,
    ar_z,
    la_s,
    la_g,
    la_z,
    sc_s,
    sc_g,
    ag_ss,
    ag_rs,
    rs_ss,
    rs_rs,
    gq_ss,
    gq_rs,
    gr_ss,
    gr_rs,
    sib_ss,
    sib_rs,
    near_ss,
    near_rs,
    x2_ss,
    x2_rs,
    x2f_ss,
    x2f_rs,
    att_ss,
    att_rs,
    gs_ss,
    gs_rs,
    ar_ss,
    ar_rs,
    la_ss,
    la_rs,
    sc_ss,
    sc_rs,
    p_sem,
    in_sem,
):
    experts = win_ref.shape[0]
    local = experts // 2
    half = x_ref.shape[0]
    rows_all = 2 * half
    width = qs.shape[1]
    hidden_width = gw.shape[-1]
    heads = width // HD
    tb = ROW_BLOCK
    mb = EXPERT_BLOCK
    blocks = rows_all // tb
    own_blocks = half // tb
    pshape = (2, heads, tb, rows_all)
    wshape = gw.shape[2:]
    qshape = gg.shape[0:4] + (width,)
    low_lanes = slice(0, 2 * width)
    high_lanes = slice(2 * width, 4 * width)

    def part(c):
        return slice(c * width, (c + 1) * width)


    d = lax.axis_index("dp")
    m = lax.axis_index("mp")
    z = d // 4
    y = (d // 2) % 2
    x = d % 2
    zg = z // 2
    zl = z % 2
    zp = z + 1 - 2 * zl
    sib = (d, 1 - m)
    xn = (d + 1 - 2 * x, m)
    yn = (d + 2 - 4 * y, m)
    near = (zp * 4 + y * 2 + x, m)
    far = ((z + 2 - 4 * zg) * 4 + y * 2 + x, m)
    zs = [((z + k) % 4) for k in (1, 2, 3)]
    zn = [(zs[k] * 4 + y * 2 + x, m) for k in range(3)]
    base = zl * local
    other = (1 - zl) * local

    load_in = pltpu.make_async_copy(win_ref, red_ref.at[0], in_sem.at[0])
    load_out = pltpu.make_async_copy(wout_ref, red_ref.at[1], in_sem.at[1])
    load_cot = pltpu.make_async_copy(cot_ref, igrad_ref, in_sem.at[2])
    for c in [load_in, load_out, load_cot]:
        c.start()

    barrier = pltpu.get_barrier_semaphore()
    plane = [
        (
            z * 4 + (y + a * (1 - 2 * y)) * 2 + (x + b * (1 - 2 * x)),
            m + c * (1 - 2 * m),
        )
        for a in (0, 1)
        for b in (0, 1)
        for c in (0, 1)
        if a + b + c > 0
    ]
    everyone = [
        (
            zk * 4 + (y + a * (1 - 2 * y)) * 2 + (x + b * (1 - 2 * x)),
            m + c * (1 - 2 * m),
        )
        for k, zk in enumerate([z] + zs)
        for a in (0, 1)
        for b in (0, 1)
        for c in (0, 1)
        if k + a + b + c > 0
    ]
    for peer in everyone:
        pl.semaphore_signal(barrier, inc=1, device_id=peer, device_id_type=MESH)
    pl.semaphore_wait(barrier, len(everyone))

    def rcopy(src, dst, ss, rs, dev):
        return pltpu.make_async_remote_copy(
            src_ref=src, dst_ref=dst, send_sem=ss, recv_sem=rs, device_id=dev, device_id_type=MESH
        )

    def start(copies):
        for c in copies:
            c.start()

    def arrive(copies):
        for c in copies:
            c.wait_recv()

    def sent(copies):
        for c in copies:
            c.wait_send()

    def blk_rows(b):
        return pl.ds(pl.multiple_of(b * tb, tb), tb)

    def own_rows(b):
        return pl.ds(pl.multiple_of(m * half + b * tb, tb), tb)

    def sib_rows(b):
        return pl.ds(pl.multiple_of((1 - m) * half + b * tb, tb), tb)

    own_half = pl.ds(pl.multiple_of(m * half, half), half)

    zpair = pl.ds(zg * 2, 2)
    zaway = pl.ds((1 - zg) * 2, 2)

    def ag0(i):
        return [
            rcopy(wsend.at[:, i], gw.at[:, i, z, y, x], ag_ss.at[i, 0], ag_rs.at[i, 0], near)
        ]

    def ag1(i):
        part = gw.at[:, i, zpair, y, x]
        return [rcopy(part, part, ag_ss.at[i, 1], ag_rs.at[i, 1], far)]

    def ag2(i):
        return [
            rcopy(gw.at[0, i, :, y, x], gw.at[0, i, :, y, x], ag_ss.at[i, 2], ag_rs.at[i, 2], xn),
            rcopy(gw.at[1, i, :, y, x], gw.at[1, i, :, y, x], ag_ss.at[i, 3], ag_rs.at[i, 3], yn),
        ]

    def ag3(i):
        return [
            rcopy(gw.at[0, i, :, y], gw.at[0, i, :, y], ag_ss.at[i, 4], ag_rs.at[i, 4], yn),
            rcopy(gw.at[1, i, :, :, x], gw.at[1, i, :, :, x], ag_ss.at[i, 5], ag_rs.at[i, 5], xn),
        ]

    def ag_tick(t):
        if 0 <= t < local:
            arrive(ag0(t))
            start(ag1(t))
        if 0 <= t - 1 < local:
            arrive(ag1(t - 1))
            start(ag2(t - 1))
        if 0 <= t - 2 < local:
            arrive(ag2(t - 2))
            start(ag3(t - 2))

    def rs1(i):
        return [
            rcopy(gd.at[0, i, :, 1 - y], r1.at[i, 0], rs_ss.at[i, 0], rs_rs.at[i, 0], yn),
            rcopy(gd.at[1, i, :, :, 1 - x], r1.at[i, 1], rs_ss.at[i, 1], rs_rs.at[i, 1], xn),
        ]

    def rs2(i):
        return [
            rcopy(gd.at[0, i, :, y, 1 - x], r2.at[i, 0], rs_ss.at[i, 2], rs_rs.at[i, 2], xn),
            rcopy(gd.at[1, i, :, 1 - y, x], r2.at[i, 1], rs_ss.at[i, 3], rs_rs.at[i, 3], yn),
        ]

    def rs3(i):
        return [
            rcopy(gd.at[:, i, zaway, y, x], r3.at[i], rs_ss.at[i, 4], rs_rs.at[i, 4], far)
        ]

    def rs4(i):
        return [rcopy(gd.at[:, i, zp, y, x], r4.at[i], rs_ss.at[i, 5], rs_rs.at[i, 5], near)]

    def add_low(one, two):
        return (one.astype(F32) + two.astype(F32)).astype(BF16)

    def rs_b(i):
        arrive(rs1(i))
        gd[0, i, :, y] = add_low(gd[0, i, :, y], r1[i, 0])
        gd[1, i, :, :, x] = add_low(gd[1, i, :, :, x], r1[i, 1])
        start(rs2(i))

    def rs_c(i):
        arrive(rs2(i))
        for a in range(2):
            gd[a, i, :, y, x] = add_low(gd[a, i, :, y, x], r2[i, a])
        start(rs3(i))

    def rs_d(i):
        arrive(rs3(i))
        red_ref[:, base + i] = gd[:, i, z, y, x].astype(F32) + r3[i, :, zl].astype(F32)
        gd[:, i, zp, y, x] = add_low(gd[:, i, zp, y, x], r3[i, :, 1 - zl])
        start(rs4(i))

    def rs_e(i):
        arrive(rs4(i))
        red_ref[:, other + i] = r4[i].astype(F32)

    gq1 = [
        rcopy(gq.at[z, y, x], gq.at[z, y, x], gq_ss.at[k], gq_rs.at[k], zn[k]) for k in range(3)
    ]

    def same(ref, sems, k, peer):
        return rcopy(ref, ref, sems[0].at[k], sems[1].at[k], peer)

    gq_sems = (gq_ss, gq_rs)
    gq2 = [
        same(gq.at[:, y, x, :, low_lanes], gq_sems, 3, xn),
        same(gq.at[:, y, x, :, high_lanes], gq_sems, 4, yn),
    ]
    gq3 = [
        same(gq.at[:, y, :, :, low_lanes], gq_sems, 5, yn),
        same(gq.at[:, :, x, :, high_lanes], gq_sems, 6, xn),
    ]
    gr1 = [
        rcopy(gg.at[:, 1 - y, :, :, low_lanes], q1.at[0], gr_ss.at[0], gr_rs.at[0], yn),
        rcopy(gg.at[:, :, 1 - x, :, high_lanes], q1.at[1], gr_ss.at[1], gr_rs.at[1], xn),
    ]
    gr2 = [
        rcopy(gg.at[:, y, 1 - x, :, low_lanes], q2.at[0], gr_ss.at[2], gr_rs.at[2], xn),
        rcopy(gg.at[:, 1 - y, x, :, high_lanes], q2.at[1], gr_ss.at[3], gr_rs.at[3], yn),
    ]
    gr3 = [
        rcopy(gg.at[zs[k], y, x], q3.at[k], gr_ss.at[4 + k], gr_rs.at[4 + k], zn[k])
        for k in range(3)
    ]

    send_x = rcopy(x_ref, x_sib, sib_ss.at[0], sib_rs.at[0], sib)
    own_g = g_all.at[0, own_half]
    pair_g = g_all.at[1, own_half]
    send_g = rcopy(own_g, own_g, sib_ss.at[1], sib_rs.at[1], sib)
    near_g = rcopy(own_g, pair_g, near_ss.at[0], near_rs.at[0], near)
    pass_g = rcopy(pair_g, pair_g, sib_ss.at[2], sib_rs.at[2], sib)
    near_gates = rcopy(gates.at[0], gates.at[1], near_ss.at[1], near_rs.at[1], near)

    def near_x2(b):
        r = own_rows(b)
        return rcopy(x2.at[0, r], x2.at[1, r], x2_ss.at[b], x2_rs.at[b], near)

    def pass_x2(b):
        r = own_rows(b)
        return rcopy(x2.at[1, r], x2.at[1, r], x2f_ss.at[b], x2f_rs.at[b], sib)

    pair_copies = [
        rcopy(pair_s.at[k], pair_r.at[k], sib_ss.at[3 + k], sib_rs.at[3 + k], sib)
        for k in range(2)
    ]
    back_copies = [
        rcopy(x_sib, back_r.at[0], near_ss.at[2], near_rs.at[2], near),
        rcopy(mix_s, back_r.at[1], near_ss.at[3], near_rs.at[3], near),
    ]
    send_mix = rcopy(pair_s.at[1], mix_r, sib_ss.at[5], sib_rs.at[5], sib)
    send_first = rcopy(pair_s.at[0], gfirst_r, sib_ss.at[6], sib_rs.at[6], sib)

    place = (y * 2 + x) * 2 + m

    class SumAll:
        def __init__(self, src, group, line, ss, rs):
            self.src, self.group, self.line = src, group, line
            self.near = [
                rcopy(src.at[0], group.at[place], ss.at[k], rs.at[k], plane[k]) for k in range(7)
            ]
            self.along = [
                rcopy(src.at[1], line.at[z], ss.at[7 + k], rs.at[7 + k], zn[k]) for k in range(3)
            ]

        def one(self):
            start(self.near)
            self.group[place] = self.src[0]

        def two(self):
            arrive(self.near)
            total = self.group[0]
            for k in range(1, 8):
                total = total + self.group[k]
            self.src[1] = total
            start(self.along)
            self.line[z] = total

        def three(self):
            arrive(self.along)
            return (self.line[0] + self.line[1]) + (self.line[2] + self.line[3])

        def done(self):
            sent(self.near + self.along)

    early = SumAll(ar_s, ar_g, ar_z, ar_ss, ar_rs)
    late = SumAll(la_s, la_g, la_z, la_ss, la_rs)
    me = d * 2 + m
    last = [
        rcopy(sc_s, sc_g.at[me], sc_ss.at[k], sc_rs.at[k], peer)
        for k, peer in enumerate(everyone)
    ]

    send_x.start()
    for c in range(3):
        gq[z, y, x, :, part(c)] = qkv_ref[c].astype(BF16)
    gq[z, y, x, :, part(3)] = wo_ref[...].astype(BF16)
    start(gq1)

    load_in.wait()
    load_out.wait()

    def cast_weights(i, carry):
        for a in range(2):
            wsend[a, i] = red_ref[a, other + i].astype(BF16)
        start(ag0(i))
        for a in range(2):
            gw[a, i, z, y, x] = red_ref[a, base + i].astype(BF16)
        return carry

    lax.fori_loop(0, local, cast_weights, 0)

    gain1 = norm_ref[0:1, :]
    bias1 = norm_ref[1:2, :]
    gain2 = norm_ref[2:3, :]
    bias2 = norm_ref[3:4, :]

    def first_norm(rows, source, b):
        unit, _ = row_stats(source[blk_rows(b), :].astype(F32))
        x1[rows, :] = (unit * gain1 + bias1).astype(BF16)

    def first_own(b, carry):
        first_norm(own_rows(b), x_ref, b)
        return carry

    def first_sib(b, carry):
        first_norm(sib_rows(b), x_sib, b)
        return carry

    lax.fori_loop(0, own_blocks, first_own, 0)
    arrive(gq1)
    start(gq2)
    ag_tick(0)
    send_x.wait_recv()
    lax.fori_loop(0, own_blocks, first_sib, 0)
    arrive(gq2)
    start(gq3)

    def cast_cot(b, carry):
        g_all[0, own_rows(b), :] = igrad_ref[blk_rows(b), :].astype(BF16)
        return carry

    load_cot.wait()
    lax.fori_loop(0, own_blocks, cast_cot, 0)
    send_g.start()
    ag_tick(1)
    arrive(gq3)

    for c in range(4):
        wq[c] = gq[:, :, :, :, part(c)].reshape(D, width)

    def flat(c):
        return wq[c]

    def project(b, carry):
        r = blk_rows(b)
        normed = x1[r, :]
        qs[r, :] = (mm(normed, flat(0)).astype(BF16).astype(F32) * SCORE_SCALE).astype(BF16)
        ks[r, :] = mm(normed, flat(1)).astype(BF16)
        vs[r, :] = mm(normed, flat(2)).astype(BF16)
        return carry

    lax.fori_loop(0, blocks, project, 0)

    def att_copy(b):
        r = blk_rows(b)
        return rcopy(att_s.at[r], att_r.at[r], att_ss.at[b], att_rs.at[b], sib)

    def attention(pbuf):
        def p_out(b):
            return pltpu.make_async_copy(pbuf.at[b % 2], p_hbm.at[b], p_sem.at[b % 2])

        def attend(b, carry):
            r = blk_rows(b)

            @pl.when(b >= 2)
            def _():
                p_out(b - 2).wait()

            outs = []
            for h in range(heads):
                cs = slice(h * HD, (h + 1) * HD)
                s = mm(qs[r, cs], ks[:, cs], NT)
                powers = jnp.exp2((s - jnp.max(s, axis=1, keepdims=True)) * LOG2E)
                inv = 1.0 / jnp.sum(powers, axis=1, keepdims=True)
                prob = (powers * inv).astype(BF16)
                pbuf[b % 2, h] = prob
                outs.append(mm(prob, vs[:, cs]))
            p_out(b).start()
            context = jnp.concatenate(outs, axis=1).astype(BF16)
            ctx[r, :] = context
            att_s[r, :] = mm(context, flat(3), NT).astype(BF16)
            att_copy(b).start()
            @pl.when(b == 4)
            def _():
                near_g.start()

            for t, when in ((2, 1), (3, 3), (4, 5)):

                @pl.when(b == when)
                def _(t=t):
                    ag_tick(t)

            return carry

        lax.fori_loop(0, blocks, attend, 0)
        p_out(blocks - 2).wait()
        p_out(blocks - 1).wait()

    pl.run_scoped(attention, pltpu.VMEM(pshape, BF16))

    router_t = router_ref[:, 0:D]
    router_hi = router_t.astype(BF16)
    router_lo = (router_t - router_hi.astype(F32)).astype(BF16)
    task = task_ref[0]
    n_tasks = router_ref.shape[1] - D
    task_lanes = lax.broadcasted_iota(jnp.int32, (experts, n_tasks), 1)
    task_bias = jnp.sum(
        jnp.where(task_lanes == task, router_ref[:, D:], 0.0), axis=1, keepdims=True
    )
    row_id = lax.broadcasted_iota(jnp.int32, (experts, tb), 0)
    gates[0, experts : 2 * experts, :] = jnp.full((experts, rows_all), task.astype(F32), F32)

    def second_norm(rows, source, b, gb):
        att_copy(gb).wait_recv()
        rows_mid = (
            source[blk_rows(b), :].astype(F32)
            + att_s[rows, :].astype(F32)
            + att_r[rows, :].astype(F32)
        )
        mid[rows, :] = rows_mid
        unit, _ = row_stats(rows_mid)
        normed = (unit * gain2 + bias2).astype(BF16)
        x2[0, rows, :] = normed
        logits = mm(router_hi, normed, NT) + mm(router_lo, normed, NT) + task_bias
        chosen = row_id == routes_ref[0:1, rows]
        for k in range(1, TOP):
            chosen = jnp.logical_or(chosen, row_id == routes_ref[k : k + 1, rows])
        peak = jnp.max(jnp.where(chosen, logits, -jnp.inf), axis=0, keepdims=True)
        powers = jnp.where(chosen, jnp.exp(logits - peak), 0.0)
        share = powers / jnp.sum(powers, axis=0, keepdims=True)
        gates[0, 0:experts, rows] = share

    def second_own(b, carry):
        second_norm(own_rows(b), x_ref, b, m * own_blocks + b)
        near_x2(b).start()
        return carry

    def second_sib(b, carry):
        second_norm(sib_rows(b), x_sib, b, (1 - m) * own_blocks + b)
        return carry

    lax.fori_loop(0, own_blocks, second_own, 0)
    lax.fori_loop(0, own_blocks, second_sib, 0)
    near_gates.start()
    send_g.wait_recv()

    def clear(b, carry):
        r = blk_rows(b)
        for st in range(2):
            mix[st, r, :] = jnp.zeros((tb, D), F32)
            gsec[st, r, :] = jnp.zeros((tb, D), F32)
        return carry

    lax.fori_loop(0, blocks, clear, 0)
    wgt_t[...] = jnp.zeros(wgt_t.shape, F32)

    def gate_grad(st, share_all, rows):
        share = wgt_t[st, :, rows]
        grad_logits = share - share_all * jnp.sum(share, axis=0, keepdims=True)
        high = grad_logits.astype(BF16)
        low = (grad_logits - high.astype(F32)).astype(BF16)
        normed = x2[st, rows, :]
        rg = mm(high, normed) + mm(low, normed)
        tg = jnp.sum(grad_logits, axis=1, keepdims=True)
        return gsec[st, rows, :] + mm(high, router_hi, TN), rg, tg

    def pair_rows_in():
        near_gates.wait_recv()
        pass_g.wait_recv()

        def land(b, carry):
            pass_x2(b).wait_recv()
            return carry

        lax.fori_loop(0, own_blocks, land, 0)

    def pass_rows(b, carry):
        near_x2(b).wait_recv()
        pass_x2(b).start()
        return carry

    task_row = lax.broadcasted_iota(jnp.int32, (experts, 128), 1).astype(F32)

    def pair_rows_out():
        def keep(b, carry):
            rg, tg = carry
            rows = own_rows(b)
            upstream, more_rg, more_tg = gate_grad(1, gates[1, 0:experts, rows], rows)
            gsec[1, rows, :] = upstream
            return rg + more_rg, tg + more_tg

        def give(b, carry):
            rg, tg = carry
            rows = sib_rows(b)
            upstream, more_rg, more_tg = gate_grad(1, gates[1, 0:experts, rows], rows)
            pair_s[0, blk_rows(b), :] = upstream.astype(BF16)
            pair_s[1, blk_rows(b), :] = mix[1, rows, :].astype(BF16)
            return rg + more_rg, tg + more_tg

        zero = (jnp.zeros((experts, D), F32), jnp.zeros((experts, 1), F32))
        sums = lax.fori_loop(0, own_blocks, give, zero)
        start(pair_copies)
        rg, tg = lax.fori_loop(0, own_blocks, keep, sums)
        ar_s[0] = jnp.zeros(ar_s.shape[1:], F32)
        ar_s[0, 8:16, :] = rg
        pair_task = gates[1, experts : experts + 1, 0:128]
        ar_s[0, 16:24, 0:128] = jnp.where(task_row == pair_task, tg, 0.0)

    def pair_grads_back():
        pair_copies[0].wait_recv()

        def grads(b, carry):
            r = blk_rows(b)
            x_sib[r, :] = (gsec[1, own_rows(b), :] + pair_r[0, r, :].astype(F32)).astype(BF16)
            return carry

        lax.fori_loop(0, own_blocks, grads, 0)
        back_copies[0].start()

    def pair_mix_back():
        pair_copies[1].wait_recv()

        def rows(b, carry):
            r = blk_rows(b)
            mix_s[r, :] = (mix[1, own_rows(b), :] + pair_r[1, r, :].astype(F32)).astype(BF16)
            return carry

        lax.fori_loop(0, own_blocks, rows, 0)
        back_copies[1].start()

    def all_experts(g_gate, hid, gpre):
        def segment(s, carry):
            pair = jnp.logical_and(s >= 2, s < 6)
            st = jnp.where(pair, 1, 0)
            i = s - jnp.where(s >= 6, 4, jnp.where(s >= 2, 2, 0))
            e = base + i
            first = jnp.logical_or(s < 2, jnp.logical_and(s >= 4, s < 6))

            @pl.when(first)
            def _():
                arrive(ag3(i))

            @pl.when(s == 1)
            def _():
                ag_tick(5)
                near_g.wait_recv()
                pass_g.start()
                lax.fori_loop(0, own_blocks, pass_rows, 0)

            @pl.when(s == 2)
            def _():
                pair_rows_in()

            @pl.when(s == 3)
            def _():
                start(rs1(0))

            @pl.when(s == 4)
            def _():
                start(rs1(1))
                rs_b(0)

            @pl.when(s == 5)
            def _():
                rs_b(1)
                rs_c(0)

            @pl.when(s == 6)
            def _():
                pair_rows_out()
                rs_c(1)
                rs_d(0)

            @pl.when(s == 7)
            def _():
                start(rs1(2))
                rs_d(1)

            def block(b, carry2):
                r = pl.ds(pl.multiple_of(b * mb, mb), mb)
                w_in = gw[0, i].reshape(D, hidden_width)
                w_out = gw[1, i].reshape(D, hidden_width)
                gate = gates[st, pl.ds(e, 1), r].T
                pre = mm(x2[st, r, :], w_in)
                incoming = (gate * g_all[st, r, :].astype(F32)).astype(BF16)
                g_gate[r, :] = incoming
                grad_hidden = mm(incoming, w_out)
                phi = 0.5 + 0.5 * lax.erf(pre * SQRT_HALF)
                density = jnp.exp2(pre * pre * (-0.5 * LOG2E)) * INV_SQRT_TWO_PI
                hidden = (pre * phi).astype(BF16)
                hid[r, :] = hidden
                grad_pre = (grad_hidden * (phi + pre * density)).astype(BF16)
                gpre[r, :] = grad_pre
                produced = mm(hidden, w_out, NT)
                mix[st, r, :] += gate * produced
                weight = jnp.sum(incoming.astype(F32) * produced, axis=1, keepdims=True)
                wgt_t[st, pl.ds(e, 1), r] = weight.T
                gsec[st, r, :] += mm(grad_pre, w_in, NT)
                return carry2

            lax.fori_loop(0, rows_all // mb, block, 0)

            @pl.when(s == 6)
            def _():
                pair_grads_back()


            def keep_sum(a, value):
                @pl.when(first)
                def _():
                    gd[a, i] = value.astype(BF16)

                @pl.when(jnp.logical_not(first))
                def _():
                    gd[a, i] = (gd[a, i].astype(F32) + value).astype(BF16)

            keep_sum(0, mm(x2[st], gpre[...], TN).reshape(wshape))
            keep_sum(1, mm(g_gate[...], hid[...], TN).reshape(wshape))
            return carry

        lax.fori_loop(0, 2 * local, segment, 0)

    pl.run_scoped(
        all_experts,
        pltpu.VMEM((rows_all, D), BF16),
        pltpu.VMEM((rows_all, hidden_width), BF16),
        pltpu.VMEM((rows_all, hidden_width), BF16),
    )
    start(rs1(3))
    rs_b(2)

    def gs_copy(b):
        r = blk_rows(b)
        return rcopy(att_s.at[r], gs_r.at[r], gs_ss.at[b], gs_rs.at[b], sib)

    for b in range(blocks):
        att_copy(b).wait_send()

    def gate_sib(b, carry):
        rg, tg = carry
        rows = sib_rows(b)
        upstream, more_rg, more_tg = gate_grad(0, gates[0, 0:experts, rows], rows)
        att_s[rows, :] = upstream.astype(BF16)
        gs_copy((1 - m) * own_blocks + b).start()
        return rg + more_rg, tg + more_tg

    def gate_own(b, carry):
        rg, tg = carry
        rows = own_rows(b)
        upstream, more_rg, more_tg = gate_grad(0, gates[0, 0:experts, rows], rows)
        att_s[rows, :] = (upstream + back_r[0, blk_rows(b), :].astype(F32)).astype(BF16)
        gs_copy(m * own_blocks + b).start()
        return rg + more_rg, tg + more_tg

    sums = (jnp.zeros((experts, D), F32), jnp.zeros((experts, 1), F32))
    sums = lax.fori_loop(0, own_blocks, gate_sib, sums)
    back_copies[0].wait_recv()
    rg, tg = lax.fori_loop(0, own_blocks, gate_own, sums)
    ar_s[0, 8:16, :] += rg
    ar_s[0, 16:24, 0:128] += jnp.where(task_row == task.astype(F32), tg, 0.0)

    sent(pair_copies)

    def mix_out(b, carry):
        pair_s[1, blk_rows(b), :] = mix[0, sib_rows(b), :].astype(BF16)
        return carry

    lax.fori_loop(0, own_blocks, mix_out, 0)
    send_mix.start()

    gml = att_r
    w_o = flat(3)

    def back_second(rows, gb):
        gs_copy(gb).wait_recv()
        grad_second = att_s[rows, :].astype(F32) + gs_r[rows, :].astype(F32)
        unit, inv_std = row_stats(mid[rows, :])
        back = row_back(grad_second, unit, inv_std, gain2)
        return grad_second, unit, back

    def back_own(b, carry):
        gain_sum, bias_sum = carry
        rows = own_rows(b)
        grad_second, unit, back = back_second(rows, m * own_blocks + b)
        grad_mid = igrad_ref[blk_rows(b), :] + back
        igrad_ref[blk_rows(b), :] = grad_mid
        grad_low = grad_mid.astype(BF16)
        gml[rows, :] = grad_low
        gctx[rows, :] = mm(grad_low, w_o).astype(BF16)
        gain_sum = gain_sum + jnp.sum(grad_second * unit, axis=0, keepdims=True)
        bias_sum = bias_sum + jnp.sum(grad_second, axis=0, keepdims=True)
        return gain_sum, bias_sum

    def back_sib(b, carry):
        rows = sib_rows(b)
        grad_second, unit, back = back_second(rows, (1 - m) * own_blocks + b)
        grad_low = (g_all[0, rows, :].astype(F32) + back).astype(BF16)
        gml[rows, :] = grad_low
        gctx[rows, :] = mm(grad_low, w_o).astype(BF16)
        return carry

    zero_row = jnp.zeros((1, D), F32)
    gain2_grad, bias2_grad = lax.fori_loop(0, own_blocks, back_own, (zero_row, zero_row))
    ar_s[0, 2:3, :] = gain2_grad
    ar_s[0, 3:4, :] = bias2_grad
    early.one()
    lax.fori_loop(0, own_blocks, back_sib, 0)
    gg[:, :, :, :, part(3)] = mm(gml[...], ctx[...], TN).reshape(qshape).astype(BF16)

    pass_g.wait_send()

    def last_part(pbuf, keys_acc, values_acc):

        def p_in(b):
            return pltpu.make_async_copy(p_hbm.at[b], pbuf.at[b % 2], p_sem.at[b % 2])

        p_in(0).start()
        keys_acc[...] = jnp.zeros(keys_acc.shape, F32)
        values_acc[...] = jnp.zeros(values_acc.shape, F32)

        def attend_back(b, carry):
            r = blk_rows(b)

            @pl.when(b + 1 < blocks)
            def _():
                p_in(b + 1).start()

            p_in(b).wait()
            outs = []
            for h in range(heads):
                cs = slice(h * HD, (h + 1) * HD)
                grad_block = gctx[r, cs]
                inner = jnp.sum(
                    grad_block.astype(F32) * ctx[r, cs].astype(F32), axis=1, keepdims=True
                )
                grad_prob = mm(grad_block, vs[:, cs], NT)
                prob = pbuf[b % 2, h]
                grad_scores = (prob.astype(F32) * (grad_prob - inner)).astype(BF16)
                outs.append(mm(grad_scores, ks[:, cs]) * SCORE_SCALE)
                keys_acc[cs, :] += mm(qs[r, cs], grad_scores, TN)
                values_acc[cs, :] += mm(grad_block, prob, TN)
            g_all[1, r, 0:width] = jnp.concatenate(outs, axis=1).astype(BF16)

            @pl.when(b == 0)
            def _():
                rs_b(3)
                rs_c(2)

            @pl.when(b == 1)
            def _():
                pair_mix_back()

            @pl.when(b == 3)
            def _():
                rs_c(3)
                rs_d(2)
                early.two()

            @pl.when(b == 5)
            def _():
                rs_d(3)
                rs_e(0)
                rs_e(1)
                small_ref[...] = early.three()

            return carry

        lax.fori_loop(0, blocks, attend_back, 0)

        normed = x1[...]
        gg[:, :, :, :, part(0)] = mm(normed, g_all[1, :, 0:width], TN).reshape(qshape).astype(BF16)
        gg[:, :, :, :, part(1)] = mm(normed, keys_acc[...].astype(BF16), TT).reshape(qshape).astype(BF16)
        gg[:, :, :, :, part(2)] = mm(normed, values_acc[...].astype(BF16), TT).reshape(qshape).astype(BF16)
        start(gr1)

        def grad_first(rows):
            return (
                mm(g_all[1, rows, 0:width], flat(0), NT)
                + mm(keys_acc[:, rows].astype(BF16), flat(1), TT)
                + mm(values_acc[:, rows].astype(BF16), flat(2), TT)
            )

        def first_back_sib(b, carry):
            pair_s[0, blk_rows(b), :] = grad_first(sib_rows(b)).astype(BF16)
            return carry

        def first_back_own(b, carry):
            gsec[0, blk_rows(b), :] = grad_first(own_rows(b))
            return carry

        lax.fori_loop(0, own_blocks, first_back_sib, 0)
        send_first.start()
        lax.fori_loop(0, own_blocks, first_back_own, 0)

    pl.run_scoped(
        last_part,
        pltpu.VMEM(pshape, BF16),
        pltpu.VMEM((width, rows_all), F32),
        pltpu.VMEM((width, rows_all), F32),
    )

    arrive(gr1)
    gg[:, y, :, :, low_lanes] = add_low(gg[:, y, :, :, low_lanes], q1[0])
    gg[:, :, x, :, high_lanes] = add_low(gg[:, :, x, :, high_lanes], q1[1])
    start(gr2)
    send_first.wait_recv()

    def back_first(b, carry):
        gain_sum, bias_sum = carry
        r = blk_rows(b)
        upstream = gsec[0, r, :] + gfirst_r[r, :].astype(F32)
        unit, inv_std = row_stats(x_ref[r, :].astype(F32))
        igrad_ref[r, :] += row_back(upstream, unit, inv_std, gain1)
        gain_sum = gain_sum + jnp.sum(upstream * unit, axis=0, keepdims=True)
        bias_sum = bias_sum + jnp.sum(upstream, axis=0, keepdims=True)
        return gain_sum, bias_sum

    gain1_grad, bias1_grad = lax.fori_loop(0, own_blocks, back_first, (zero_row, zero_row))
    la_s[0] = jnp.zeros(la_s.shape[1:], F32)
    la_s[0, 0:1, :] = gain1_grad
    la_s[0, 1:2, :] = bias1_grad

    late.one()

    send_mix.wait_recv()
    back_copies[1].wait_recv()

    def write_out(b, carry):
        r = blk_rows(b)
        rows = own_rows(b)
        out_ref[r, :] = (
            mid[rows, :]
            + mix[0, rows, :]
            + mix_r[r, :].astype(F32)
            + back_r[1, r, :].astype(F32)
        )
        return carry

    lax.fori_loop(0, own_blocks, write_out, 0)

    arrive(gr2)
    gg[:, y, x, :, low_lanes] = add_low(gg[:, y, x, :, low_lanes], q2[0])
    gg[:, y, x, :, high_lanes] = add_low(gg[:, y, x, :, high_lanes], q2[1])
    start(gr3)
    rs_e(2)
    rs_e(3)

    def squares(e, acc):
        for a in range(2):
            acc = acc + jnp.sum(red_ref[a, e] * red_ref[a, e], axis=0, keepdims=True)
        return acc

    columns = lax.fori_loop(0, experts, squares, jnp.zeros((1, hidden_width), F32))
    late.two()

    arrive(gr3)
    total = gg[z, y, x].astype(F32)
    for k in range(3):
        total = total + q3[k].astype(F32)
    redq_ref[...] = total
    columns = columns + jnp.sum(total * total, axis=0, keepdims=True)
    sc_s[...] = jnp.full(sc_s.shape, jnp.sum(columns), F32)
    start(last)
    sc_g[me] = sc_s[...]
    late_ref[0:2, :] = late.three()[0:2]
    arrive(last)
    total = sc_g[0]
    for k in range(1, len(everyone) + 1):
        total = total + sc_g[k]
    late_ref[2:8, :] = jnp.broadcast_to(total[0:1, 0:1], (6, D))

    sent(gq1 + gq2 + gq3 + gr1 + gr2 + gr3)
    early.done()
    late.done()
    sent(last)
    sent([send_x, send_g, near_g, near_gates, send_mix, send_first] + back_copies)
    for i in range(local):
        sent(ag0(i) + ag1(i) + ag2(i) + ag3(i))
        sent(rs1(i) + rs2(i) + rs3(i) + rs4(i))

    def drain_rows(b, carry):
        gs_copy(b).wait_send()
        return carry

    def drain_own(b, carry):
        near_x2(b).wait_send()
        pass_x2(b).wait_send()
        return carry

    lax.fori_loop(0, blocks, drain_rows, 0)
    lax.fori_loop(0, own_blocks, drain_own, 0)


def step_call(x_rows, cotangent, task_ids, routes, norms, qkv, wo, router, win, wout):
    half = x_rows.shape[0]
    rows_all = 2 * half
    experts, shard, hidden = win.shape
    local = experts // 2
    width = wo.shape[1]
    blocks = rows_all // ROW_BLOCK
    own_blocks = half // ROW_BLOCK
    heads = width // HD
    vmem = pl.BlockSpec(memory_space=pltpu.VMEM)
    hbm = pl.BlockSpec(memory_space=pl.ANY)
    grid = (GRID_Z, GRID_Y, GRID_X)
    struct = jax.ShapeDtypeStruct
    dma = pltpu.SemaphoreType.DMA
    outs = (
        struct((half, D), F32),
        struct((half, D), F32),
        struct((2, experts, shard, hidden), F32),
        struct((shard, 4 * width), F32),
        struct((24, D), F32),
        struct((8, D), F32),
        struct((blocks, heads, ROW_BLOCK, rows_all), BF16),
    )
    scratch = [
        pltpu.VMEM((half, D), BF16),
        pltpu.VMEM((2, rows_all, D), BF16),
        pltpu.VMEM((rows_all, D), BF16),
        pltpu.VMEM((rows_all, width), BF16),
        pltpu.VMEM((rows_all, width), BF16),
        pltpu.VMEM((rows_all, width), BF16),
        pltpu.VMEM((rows_all, width), BF16),
        pltpu.VMEM((rows_all, D), BF16),
        pltpu.VMEM((rows_all, D), BF16),
        pltpu.VMEM((rows_all, D), F32),
        pltpu.VMEM((2, rows_all, D), BF16),
        pltpu.VMEM((2, 2 * experts, rows_all), F32),
        pltpu.VMEM((2, experts, rows_all), F32),
        pltpu.VMEM((2, rows_all, D), F32),
        pltpu.VMEM((2, rows_all, D), F32),
        pltpu.VMEM((rows_all, D), BF16),
        pltpu.VMEM((half, D), BF16),
        pltpu.VMEM((half, D), BF16),
        pltpu.VMEM((rows_all, width), BF16),
        pltpu.VMEM((half, D), BF16),
        pltpu.VMEM((2, half, D), BF16),
        pltpu.VMEM((2, half, D), BF16),
        pltpu.VMEM((2, half, D), BF16),
        pltpu.VMEM((2, local) + grid + (shard, hidden), BF16),
        pltpu.VMEM((2, local) + grid + (shard, hidden), BF16),
        pltpu.VMEM((2, local, shard, hidden), BF16),
        pltpu.VMEM((local, 2, 4, 2, shard, hidden), BF16),
        pltpu.VMEM((local, 2, 4, shard, hidden), BF16),
        pltpu.VMEM((local, 2, 2, shard, hidden), BF16),
        pltpu.VMEM((local, 2, shard, hidden), BF16),
        pltpu.VMEM(grid + (shard, 4 * width), BF16),
        pltpu.VMEM((4, D, width), BF16),
        pltpu.VMEM(grid + (shard, 4 * width), BF16),
        pltpu.VMEM((2, 4, 2, shard, 2 * width), BF16),
        pltpu.VMEM((2, 4, shard, 2 * width), BF16),
        pltpu.VMEM((3, shard, 4 * width), BF16),
        pltpu.VMEM((2, 24, D), F32),
        pltpu.VMEM((8, 24, D), F32),
        pltpu.VMEM((4, 24, D), F32),
        pltpu.VMEM((2, 8, D), F32),
        pltpu.VMEM((8, 8, D), F32),
        pltpu.VMEM((4, 8, D), F32),
        pltpu.VMEM((8, 128), F32),
        pltpu.VMEM((32, 8, 128), F32),
    ]
    for size in [
        (local, 6),
        (local, 6),
        (7,),
        (7,),
        (7,),
        (4,),
        (own_blocks,),
        (own_blocks,),
        (blocks,),
        (blocks,),
        (10,),
        (10,),
        (31,),
    ]:
        scratch += [dma(size), dma(size)]
    scratch += [dma((2,)), dma((3,))]
    return pl.pallas_call(
        step_kernel,
        out_shape=outs,
        in_specs=[vmem, hbm, pl.BlockSpec(memory_space=pltpu.SMEM)] + [vmem] * 5 + [hbm] * 2,
        out_specs=[vmem] * 6 + [hbm],
        scratch_shapes=scratch,
        compiler_params=pltpu.CompilerParams(
            collective_id=0, has_side_effects=True, vmem_limit_bytes=64 << 20
        ),
        name="step",
    )(
        x_rows,
        cotangent,
        task_ids,
        routes.T,
        norms,
        qkv,
        wo,
        router.T,
        win,
        wout,
    )


def adam_parts(weight, first, second, average, gradient, clip_scale, rate):
    clipped = clip_scale * gradient
    first_new = BETA_FIRST * first + (1.0 - BETA_FIRST) * clipped
    second_new = BETA_SECOND * second + (1.0 - BETA_SECOND) * clipped * clipped
    first_hat = first_new * (1.0 / (1.0 - BETA_FIRST**STEP))
    second_hat = second_new * (1.0 / (1.0 - BETA_SECOND**STEP))
    weight_new = weight - rate * (
        first_hat / (jnp.sqrt(second_hat) + ADAM_EPS) + WEIGHT_DECAY * weight
    )
    return weight_new, first_new, second_new, EMA_KEEP * average + (1.0 - EMA_KEEP) * weight_new


def adam_kernel(*refs):
    red, redq, small, late, rows_in, back_in = refs[:6]
    state = [refs[6 + 4 * k : 10 + 4 * k] for k in range(6)]
    norm_out, rows_out, back_out = refs[30:33]
    fresh = [refs[33 + 4 * k : 37 + 4 * k] for k in range(6)]
    step = pl.program_id(0)
    width = redq.shape[1] // 4

    rows_out[...] = rows_in[...]
    back_out[...] = back_in[...]
    norm_grad = jnp.concatenate([late[0:2, :], small[2:4, :]], axis=0)
    router_grad = small[8:16, :]
    task_grad = small[16:24, 0:TASKS]
    total = (
        jnp.max(late[2:3, 0:1])
        + jnp.sum(norm_grad * norm_grad)
        + jnp.sum(router_grad * router_grad)
        + jnp.sum(task_grad * task_grad)
    )
    grad_norm = jnp.sqrt(jnp.full((1, 1), total, F32))
    clip = jnp.minimum(1.0, CLIP_LIMIT / (grad_norm + 1e-06))

    def update(k, gradient, rate, *index):
        new = adam_parts(*[r[index] for r in state[k]], gradient, clip, rate)
        for r, v in zip(fresh[k], new):
            r[index] = v

    @pl.when(step == 0)
    def _():
        norm_out[0] = jnp.max(grad_norm)
        update(0, norm_grad, NORM_RATE, slice(None))
        for c in range(3):
            update(1, redq[:, c * width : (c + 1) * width], LEARN_RATE, c)
        update(2, redq[:, 3 * width :], LEARN_RATE, slice(None))
        update(3, router_grad, LEARN_RATE, slice(None), slice(0, D))
        update(3, task_grad, LEARN_RATE, slice(None), slice(D, D + TASKS))

    update(4, red[0], LEARN_RATE, slice(None))
    update(5, red[1], LEARN_RATE, slice(None))


def adam_call(red, redq, small, late, output, input_grad, state):
    experts, shard, hidden = red.shape[1:]
    per = 2
    steps = experts // per

    def fixed(array):
        rank = len(array.shape)
        return pl.BlockSpec(array.shape, lambda s: (0,) * rank)

    rows = pl.BlockSpec((output.shape[0] // steps, D), lambda s: (s, 0))
    tile = pl.BlockSpec((per, shard, hidden), lambda s: (s, 0, 0))
    specs = []
    for k, group in enumerate(state):
        specs += [tile if k >= 4 else fixed(a) for a in group]
    flat = [a for group in state for a in group]
    struct = jax.ShapeDtypeStruct
    results = pl.pallas_call(
        adam_kernel,
        grid=(steps,),
        out_shape=[struct((1,), F32), struct(output.shape, F32), struct(output.shape, F32)]
        + [struct(a.shape, F32) for a in flat],
        in_specs=[
            pl.BlockSpec((2, per, shard, hidden), lambda s: (0, s, 0, 0)),
            fixed(redq),
            fixed(small),
            fixed(late),
            rows,
            rows,
        ]
        + specs,
        out_specs=[pl.BlockSpec(memory_space=pltpu.SMEM), rows, rows] + specs,
        compiler_params=pltpu.CompilerParams(vmem_limit_bytes=64 << 20),
        name="adam",
    )(red, redq, small, late, output, input_grad, *flat)
    fresh = [results[3 + 4 * k : 7 + 4 * k] for k in range(6)]
    return results[0], results[1], results[2], fresh


def shards(
    x_rows,
    cotangent,
    task_ids,
    routes,
    norm_params,
    norm_first,
    norm_second,
    norm_ema,
    qkv_weight,
    qkv_first,
    qkv_second,
    qkv_ema,
    out_weight,
    out_first,
    out_second,
    out_ema,
    router,
    router_first,
    router_second,
    router_ema,
    expert_in,
    expert_in_first,
    expert_in_second,
    expert_in_ema,
    expert_out,
    expert_out_first,
    expert_out_second,
    expert_out_ema,
):
    qkv_full, out_full, in_full, eout_full = (
        lax.all_gather(qkv_weight.astype(jnp.bfloat16), "dp", axis=1, tiled=True),
        lax.all_gather(out_weight.astype(jnp.bfloat16), "dp", axis=0, tiled=True),
        lax.all_gather(expert_in.astype(jnp.bfloat16), "dp", axis=1, tiled=True),
        lax.all_gather(expert_out.astype(jnp.bfloat16), "dp", axis=1, tiled=True),
    )
    local_width = qkv_full.shape[2]
    local_heads = local_width // HD
    x_float = x_rows.astype(jnp.float32)
    first_normed, first_unit, first_inv = norm_forward(x_float, norm_params[0], norm_params[1])
    first_all = lax.all_gather(first_normed.astype(jnp.bfloat16), "mp", axis=0, tiled=True)
    triple = jnp.einsum(
        "rd,cdh->crh", first_all, qkv_full, preferred_element_type=jnp.float32
    ).astype(jnp.bfloat16)
    heads = triple.reshape(3, IMGS, L, local_heads, HD)
    context_heads, log_total = lax.map(
        lambda member: attend_image(member[0], member[1], member[2], QB),
        (heads[0], heads[1], heads[2]),
    )
    context = context_heads.reshape(R, local_width)
    attended_part = jnp.einsum("rh,dh->rd", context, out_full, preferred_element_type=jnp.float32)
    attended = lax.psum_scatter(
        attended_part.astype(jnp.bfloat16), "mp", scatter_dimension=0, tiled=True
    ).astype(jnp.float32)
    mid = x_float + attended
    second_normed, second_unit, second_inv = norm_forward(mid, norm_params[2], norm_params[3])
    second_all = lax.all_gather(second_normed.astype(jnp.bfloat16), "mp", axis=0, tiled=True)
    second_float = second_all.astype(jnp.float32)
    task_onehot = (task_ids[:, None] == jnp.arange(TASKS, dtype=jnp.int32)[None, :]).astype(
        jnp.float32
    )
    task_bias = dense_exact(task_onehot, router[D:])
    logits = dense_exact(second_float, router[:D])
    logits = (logits.reshape(IMGS, L, E) + task_bias[:, None, :]).reshape(R, E)
    route_hot = (routes[:, :, None] == jnp.arange(E, dtype=jnp.int32)[None, None, :]).astype(
        jnp.float32
    )
    chosen = jnp.sum(route_hot * logits[:, None, :], axis=-1)
    gates = jax.nn.softmax(chosen, axis=-1)
    slots = slot_table(routes, E, CAP)
    pair_ids = jnp.arange(R * TOP, dtype=jnp.int32)
    slot_pair = jnp.full((E * CAP,), R * TOP, jnp.int32).at[slots].set(pair_ids)
    slot_token = (slot_pair // TOP).reshape(E, CAP)
    gate_padded = jnp.concatenate([gates.reshape(-1), jnp.zeros((1,), jnp.float32)])
    slot_gate = gate_padded[slot_pair].reshape(E, CAP)
    padded_rows = jnp.concatenate([second_all, jnp.zeros((1, D), jnp.bfloat16)], axis=0)

    def expert_forward(carry, member):
        weight_in, weight_out, owners, owner_gate = member
        dispatched = padded_rows[owners]
        pre = jnp.dot(dispatched, weight_in, preferred_element_type=jnp.float32)
        hidden = gelu_exact(pre).astype(jnp.bfloat16)
        produced = jnp.einsum("cf,df->cd", hidden, weight_out, preferred_element_type=jnp.float32)
        return (carry.at[owners].add(owner_gate[:, None] * produced), None)

    mixture_acc, unused = lax.scan(
        expert_forward,
        jnp.zeros((R + 1, D), jnp.float32),
        (in_full, eout_full, slot_token, slot_gate),
    )
    mixture = lax.psum_scatter(
        mixture_acc[:R].astype(jnp.bfloat16), "mp", scatter_dimension=0, tiled=True
    ).astype(jnp.float32)
    output = mid + mixture
    grad_low_all = lax.all_gather(cotangent.astype(jnp.bfloat16), "mp", axis=0, tiled=True)
    grad_padded = jnp.concatenate([grad_low_all, jnp.zeros((1, D), jnp.bfloat16)], axis=0)

    def expert_backward(carry, member):
        weight_in, weight_out, owners, owner_gate = member
        dispatched = padded_rows[owners]
        pre = jnp.dot(dispatched, weight_in, preferred_element_type=jnp.float32)
        hidden = gelu_exact(pre).astype(jnp.bfloat16)
        produced = jnp.einsum("cf,df->cd", hidden, weight_out, preferred_element_type=jnp.float32)
        incoming = grad_padded[owners].astype(jnp.float32)
        slot_grad_gate = jnp.sum(incoming * produced, axis=-1)
        grad_produced = (owner_gate[:, None] * incoming).astype(jnp.bfloat16)
        grad_hidden = jnp.dot(grad_produced, weight_out, preferred_element_type=jnp.float32)
        grad_pre = (grad_hidden * gelu_slope(pre)).astype(jnp.bfloat16)
        grad_weight_out = jnp.einsum(
            "cd,cf->df", grad_produced, hidden, preferred_element_type=jnp.float32
        )
        grad_weight_in = jnp.einsum(
            "cd,cf->df", dispatched, grad_pre, preferred_element_type=jnp.float32
        )
        grad_dispatched = jnp.einsum(
            "cf,df->cd", grad_pre, weight_in, preferred_element_type=jnp.float32
        )
        return (
            carry.at[owners].add(grad_dispatched),
            (grad_weight_in, grad_weight_out, slot_grad_gate),
        )

    expert_carry, expert_outs = lax.scan(
        expert_backward,
        jnp.zeros((R + 1, D), jnp.float32),
        (in_full, eout_full, slot_token, slot_gate),
    )
    grad_in_stack, grad_eout_stack, slot_grad_gate = expert_outs
    in_reduced, eout_reduced = (
        lax.psum_scatter(grad_in_stack, "dp", scatter_dimension=1, tiled=True),
        lax.psum_scatter(grad_eout_stack, "dp", scatter_dimension=1, tiled=True),
    )
    grad_gates = slot_grad_gate.reshape(-1)[slots].reshape(R, TOP)
    grad_chosen = gates * (grad_gates - jnp.sum(gates * grad_gates, axis=-1, keepdims=True))
    grad_logits = jnp.sum(route_hot * grad_chosen[:, :, None], axis=1)
    router_rows_grad = dense_exact(second_float.T, grad_logits)
    task_rows_grad = dense_exact(task_onehot.T, jnp.sum(grad_logits.reshape(IMGS, L, E), axis=1))
    router_grad_part = jnp.concatenate([router_rows_grad, task_rows_grad], axis=0)
    grad_second_part = expert_carry[:R] + dense_exact(grad_logits, router[:D].T)
    grad_second = lax.psum_scatter(
        grad_second_part.astype(jnp.bfloat16), "mp", scatter_dimension=0, tiled=True
    ).astype(jnp.float32)
    grad_mid_norm, gain_two_grad, shift_two_grad = norm_backward(
        grad_second, second_unit, second_inv, norm_params[2]
    )
    grad_mid = cotangent + grad_mid_norm
    grad_mid_all = lax.all_gather(grad_mid.astype(jnp.bfloat16), "mp", axis=0, tiled=True)
    grad_out_weight = jnp.einsum(
        "rd,rh->dh", grad_mid_all, context, preferred_element_type=jnp.float32
    )
    grad_context = jnp.dot(grad_mid_all, out_full, preferred_element_type=jnp.float32).astype(
        jnp.bfloat16
    )
    grad_context_heads = grad_context.reshape(IMGS, L, local_heads, HD)
    grad_queries, grad_keys, grad_values = lax.map(
        lambda member: attend_image_back(member[0], member[1], member[2], member[3], member[4], QB),
        (heads[0], heads[1], heads[2], log_total, grad_context_heads),
    )
    grad_triple = jnp.stack(
        [
            grad_queries.reshape(R, local_width),
            grad_keys.reshape(R, local_width),
            grad_values.reshape(R, local_width),
        ],
        axis=0,
    )
    grad_qkv_weight = jnp.einsum(
        "rd,crh->cdh", first_all, grad_triple, preferred_element_type=jnp.float32
    )
    grad_first_part = jnp.einsum(
        "crh,cdh->rd", grad_triple, qkv_full, preferred_element_type=jnp.float32
    )
    grad_first = lax.psum_scatter(
        grad_first_part.astype(jnp.bfloat16), "mp", scatter_dimension=0, tiled=True
    ).astype(jnp.float32)
    grad_x_norm, gain_one_grad, shift_one_grad = norm_backward(
        grad_first, first_unit, first_inv, norm_params[0]
    )
    input_grad = grad_mid + grad_x_norm
    norm_grad_part = jnp.stack(
        [gain_one_grad, shift_one_grad, gain_two_grad, shift_two_grad], axis=0
    )
    norm_grad, router_grad = lax.psum((norm_grad_part, router_grad_part), ("dp", "mp"))
    qkv_reduced, out_reduced = (
        lax.psum_scatter(grad_qkv_weight, "dp", scatter_dimension=1, tiled=True),
        lax.psum_scatter(grad_out_weight, "dp", scatter_dimension=0, tiled=True),
    )
    local_squares = (
        jnp.sum(qkv_reduced * qkv_reduced)
        + jnp.sum(out_reduced * out_reduced)
        + jnp.sum(in_reduced * in_reduced)
        + jnp.sum(eout_reduced * eout_reduced)
    )
    share = 1.0 / (lax.axis_size("dp") * lax.axis_size("mp"))
    small_squares = jnp.sum(norm_grad * norm_grad) + jnp.sum(router_grad * router_grad)
    total_squares = lax.psum(local_squares + share * small_squares, ("dp", "mp"))
    grad_norm = jnp.sqrt(total_squares)
    clip_scale = jnp.minimum(1.0, CLIP_LIMIT / (grad_norm + 1e-06))
    norm_new, norm_first_new, norm_second_new, norm_ema_new = adam_update(
        norm_params, norm_first, norm_second, norm_ema, norm_grad, clip_scale, NORM_RATE
    )
    qkv_new, qkv_first_new, qkv_second_new, qkv_ema_new = adam_update(
        qkv_weight, qkv_first, qkv_second, qkv_ema, qkv_reduced, clip_scale, LEARN_RATE
    )
    out_new, out_first_new, out_second_new, out_ema_new = adam_update(
        out_weight, out_first, out_second, out_ema, out_reduced, clip_scale, LEARN_RATE
    )
    router_new, router_first_new, router_second_new, router_ema_new = adam_update(
        router, router_first, router_second, router_ema, router_grad, clip_scale, LEARN_RATE
    )
    in_new, in_first_new, in_second_new, in_ema_new = adam_update(
        expert_in,
        expert_in_first,
        expert_in_second,
        expert_in_ema,
        in_reduced,
        clip_scale,
        LEARN_RATE,
    )
    eout_new, eout_first_new, eout_second_new, eout_ema_new = adam_update(
        expert_out,
        expert_out_first,
        expert_out_second,
        expert_out_ema,
        eout_reduced,
        clip_scale,
        LEARN_RATE,
    )
    return (
        output,
        input_grad,
        grad_norm.reshape(1),
        norm_new,
        norm_first_new,
        norm_second_new,
        norm_ema_new,
        qkv_new,
        qkv_first_new,
        qkv_second_new,
        qkv_ema_new,
        out_new,
        out_first_new,
        out_second_new,
        out_ema_new,
        router_new,
        router_first_new,
        router_second_new,
        router_ema_new,
        in_new,
        in_first_new,
        in_second_new,
        in_ema_new,
        eout_new,
        eout_first_new,
        eout_second_new,
        eout_ema_new,
    )


def shards_fused(
    x_rows,
    cotangent,
    task_ids,
    routes,
    norm_params,
    norm_first,
    norm_second,
    norm_ema,
    qkv_weight,
    qkv_first,
    qkv_second,
    qkv_ema,
    out_weight,
    out_first,
    out_second,
    out_ema,
    router,
    router_first,
    router_second,
    router_ema,
    expert_in,
    expert_in_first,
    expert_in_second,
    expert_in_ema,
    expert_out,
    expert_out_first,
    expert_out_second,
    expert_out_ema,
):
    output, input_grad, expert_red, qkvo_red, small, late, unused = step_call(
        x_rows,
        cotangent,
        task_ids,
        routes,
        norm_params,
        qkv_weight,
        out_weight,
        router,
        expert_in,
        expert_out,
    )
    state = [
        (norm_params, norm_first, norm_second, norm_ema),
        (qkv_weight, qkv_first, qkv_second, qkv_ema),
        (out_weight, out_first, out_second, out_ema),
        (router.T, router_first.T, router_second.T, router_ema.T),
        (expert_in, expert_in_first, expert_in_second, expert_in_ema),
        (expert_out, expert_out_first, expert_out_second, expert_out_ema),
    ]
    grad_norm, output, input_grad, fresh = adam_call(
        expert_red, qkvo_red, small, late, output, input_grad, state
    )
    fresh[3] = [a.T for a in fresh[3]]
    flat = [a for group in fresh for a in group]
    return (output, input_grad, grad_norm, *flat)


def solution(mesh):
    fused = mesh.shape["dp"] == GRID_Z * GRID_Y * GRID_X and mesh.shape["mp"] == 2
    return jax.shard_map(
        shards_fused if fused else shards,
        mesh=mesh,
        in_specs=(
            P(("dp", "mp"), None),
            P(("dp", "mp"), None),
            P("dp"),
            P("dp", None),
            P(),
            P(),
            P(),
            P(),
            P(None, "dp", "mp"),
            P(None, "dp", "mp"),
            P(None, "dp", "mp"),
            P(None, "dp", "mp"),
            P("dp", "mp"),
            P("dp", "mp"),
            P("dp", "mp"),
            P("dp", "mp"),
            P(),
            P(),
            P(),
            P(),
            P(None, "dp", "mp"),
            P(None, "dp", "mp"),
            P(None, "dp", "mp"),
            P(None, "dp", "mp"),
            P(None, "dp", "mp"),
            P(None, "dp", "mp"),
            P(None, "dp", "mp"),
            P(None, "dp", "mp"),
        ),
        out_specs=(
            P(("dp", "mp"), None),
            P(("dp", "mp"), None),
            P(),
            P(),
            P(),
            P(),
            P(),
            P(None, "dp", "mp"),
            P(None, "dp", "mp"),
            P(None, "dp", "mp"),
            P(None, "dp", "mp"),
            P("dp", "mp"),
            P("dp", "mp"),
            P("dp", "mp"),
            P("dp", "mp"),
            P(),
            P(),
            P(),
            P(),
            P(None, "dp", "mp"),
            P(None, "dp", "mp"),
            P(None, "dp", "mp"),
            P(None, "dp", "mp"),
            P(None, "dp", "mp"),
            P(None, "dp", "mp"),
            P(None, "dp", "mp"),
            P(None, "dp", "mp"),
        ),
        check_vma=False,
    )
```

```python
import jax
import jax.numpy as jnp
from jax import lax
from jax.experimental import pallas as pl
from jax.experimental.pallas import tpu as pltpu
from jax.sharding import PartitionSpec as P

D = 384
HD = 64
E = 8
TOP = 4
TASKS = 5
L = 1536
STEP = 10
IMGS = 1
R = 1536
QB = 512
CAP = 1536


NORM_EPS = 1e-06
SCORE_SCALE = 0.125
CLIP_LIMIT = 1.0
BETA_FIRST = 0.9
BETA_SECOND = 0.999
LEARN_RATE = 0.1
NORM_RATE = 0.5
WEIGHT_DECAY = 0.05
ADAM_EPS = 1e-08
EMA_KEEP = 0.6
SQRT_HALF = 0.7071067811865476
INV_SQRT_TWO_PI = 0.3989422804014327


def norm_forward(rows, gain, shift):
    row_mean = jnp.mean(rows, axis=-1, keepdims=True)
    centered = rows - row_mean
    inv_std = lax.rsqrt(jnp.mean(centered * centered, axis=-1, keepdims=True) + NORM_EPS)
    unit = centered * inv_std
    return (unit * gain + shift, unit, inv_std)


def norm_backward(upstream, unit, inv_std, gain):
    scaled = upstream * gain
    inner = jnp.mean(scaled * unit, axis=-1, keepdims=True)
    grad_rows = inv_std * (scaled - jnp.mean(scaled, axis=-1, keepdims=True) - unit * inner)
    return (grad_rows, jnp.sum(upstream * unit, axis=0), jnp.sum(upstream, axis=0))


def gelu_exact(values):
    return 0.5 * values * (1.0 + lax.erf(values * SQRT_HALF))


def gelu_slope(values):
    return 0.5 * (1.0 + lax.erf(values * SQRT_HALF)) + values * INV_SQRT_TWO_PI * jnp.exp(
        -0.5 * values * values
    )


def dense_exact(left, right):
    return jnp.dot(left, right, precision=lax.Precision.HIGHEST, preferred_element_type=jnp.float32)


def slot_table(route_rows, experts, capacity):
    flat_routes = route_rows.reshape(-1)
    one_hot = (flat_routes[:, None] == jnp.arange(experts, dtype=jnp.int32)[None, :]).astype(
        jnp.int32
    )
    earlier = jnp.cumsum(one_hot, axis=0) - one_hot
    position = jnp.sum(earlier * one_hot, axis=1)
    return flat_routes * capacity + position


def attend_image(queries, keys_img, values_img, block_rows):
    blended_parts = []
    total_parts = []
    for offset in range(0, queries.shape[0], block_rows):
        query_block = queries[offset : offset + block_rows]
        scores = (
            jnp.einsum("qhd,khd->hqk", query_block, keys_img, preferred_element_type=jnp.float32)
            * SCORE_SCALE
        )
        row_peak = jnp.max(scores, axis=-1, keepdims=True)
        powers = jnp.exp(scores - row_peak)
        row_total = jnp.sum(powers, axis=-1, keepdims=True)
        probability = (powers / row_total).astype(jnp.bfloat16)
        blended = jnp.einsum(
            "hqk,khd->qhd", probability, values_img, preferred_element_type=jnp.float32
        )
        blended_parts.append(blended.astype(jnp.bfloat16))
        total_parts.append((row_peak + jnp.log(row_total))[:, :, 0])
    return (jnp.concatenate(blended_parts, axis=0), jnp.concatenate(total_parts, axis=1))


def attend_image_back(queries, keys_img, values_img, log_total, grad_context, block_rows):
    query_parts = []
    grad_keys = jnp.zeros(keys_img.shape, jnp.float32)
    grad_values = jnp.zeros(values_img.shape, jnp.float32)
    for offset in range(0, queries.shape[0], block_rows):
        query_block = queries[offset : offset + block_rows]
        grad_block = grad_context[offset : offset + block_rows]
        scores = (
            jnp.einsum("qhd,khd->hqk", query_block, keys_img, preferred_element_type=jnp.float32)
            * SCORE_SCALE
        )
        probability = jnp.exp(scores - log_total[:, offset : offset + block_rows, None])
        prob_low = probability.astype(jnp.bfloat16)
        grad_prob = jnp.einsum(
            "qhd,khd->hqk", grad_block, values_img, preferred_element_type=jnp.float32
        )
        inner = jnp.sum(probability * grad_prob, axis=-1, keepdims=True)
        grad_scores = (probability * (grad_prob - inner)).astype(jnp.bfloat16)
        query_parts.append(
            jnp.einsum("hqk,khd->qhd", grad_scores, keys_img, preferred_element_type=jnp.float32)
            * SCORE_SCALE
        )
        grad_keys = (
            grad_keys
            + jnp.einsum(
                "hqk,qhd->khd", grad_scores, query_block, preferred_element_type=jnp.float32
            )
            * SCORE_SCALE
        )
        grad_values = grad_values + jnp.einsum(
            "hqk,qhd->khd", prob_low, grad_block, preferred_element_type=jnp.float32
        )
    grad_queries = jnp.concatenate(query_parts, axis=0)
    return (
        grad_queries.astype(jnp.bfloat16),
        grad_keys.astype(jnp.bfloat16),
        grad_values.astype(jnp.bfloat16),
    )


def adam_update(weight, first, second, average, gradient, clip_scale, rate):
    clipped = clip_scale * gradient
    first_new = BETA_FIRST * first + (1.0 - BETA_FIRST) * clipped
    second_new = BETA_SECOND * second + (1.0 - BETA_SECOND) * clipped * clipped
    first_hat = first_new / (1.0 - BETA_FIRST**STEP)
    second_hat = second_new / (1.0 - BETA_SECOND**STEP)
    weight_new = weight - rate * (
        first_hat / (jnp.sqrt(second_hat) + ADAM_EPS) + WEIGHT_DECAY * weight
    )
    average_new = EMA_KEEP * average + (1.0 - EMA_KEEP) * weight_new
    return (weight_new, first_new, second_new, average_new)


F32 = jnp.float32
BF16 = jnp.bfloat16
MESH = pl.DeviceIdType.MESH
LOG2E = 1.4426950408889634
NN = ((1,), (0,))
NT = ((1,), (1,))
TN = ((0,), (0,))
TT = ((0,), (1,))
GRID_Z, GRID_Y, GRID_X = 4, 2, 2
ROW_BLOCK = 256
EXPERT_BLOCK = 512


def mm(left, right, dims=NN):
    return lax.dot_general(left, right, (dims, ((), ())), preferred_element_type=F32)


def row_stats(rows):
    centered = rows - jnp.mean(rows, axis=-1, keepdims=True)
    inv_std = lax.rsqrt(jnp.mean(centered * centered, axis=-1, keepdims=True) + NORM_EPS)
    return centered * inv_std, inv_std


def row_back(upstream, unit, inv_std, gain):
    scaled = upstream * gain
    inner = jnp.mean(scaled * unit, axis=-1, keepdims=True)
    return inv_std * (scaled - jnp.mean(scaled, axis=-1, keepdims=True) - unit * inner)


def step_kernel(
    x_ref,
    cot_ref,
    task_ref,
    routes_ref,
    norm_ref,
    qkv_ref,
    wo_ref,
    router_ref,
    win_ref,
    wout_ref,
    out_ref,
    igrad_ref,
    red_ref,
    redq_ref,
    small_ref,
    late_ref,
    p_hbm,
    x_sib,
    g_all,
    x1,
    qs,
    ks,
    vs,
    ctx,
    att_s,
    att_r,
    mid,
    x2,
    gates,
    wgt_t,
    mix,
    gsec,
    gs_r,
    mix_s,
    mix_r,
    gctx,
    gfirst_r,
    pair_s,
    pair_r,
    back_r,
    gw,
    gd,
    wsend,
    r1,
    r2,
    r3,
    r4,
    gq,
    wq,
    gg,
    q1,
    q2,
    q3,
    ar_s,
    ar_g,
    ar_z,
    la_s,
    la_g,
    la_z,
    sc_s,
    sc_g,
    ag_ss,
    ag_rs,
    rs_ss,
    rs_rs,
    gq_ss,
    gq_rs,
    gr_ss,
    gr_rs,
    sib_ss,
    sib_rs,
    near_ss,
    near_rs,
    x2_ss,
    x2_rs,
    x2f_ss,
    x2f_rs,
    att_ss,
    att_rs,
    gs_ss,
    gs_rs,
    ar_ss,
    ar_rs,
    la_ss,
    la_rs,
    sc_ss,
    sc_rs,
    p_sem,
    in_sem,
):
    experts = win_ref.shape[0]
    local = experts // 2
    half = x_ref.shape[0]
    rows_all = 2 * half
    width = qs.shape[1]
    hidden_width = gw.shape[-1]
    heads = width // HD
    tb = ROW_BLOCK
    mb = EXPERT_BLOCK
    blocks = rows_all // tb
    own_blocks = half // tb
    pshape = (2, heads, tb, rows_all)
    wshape = gw.shape[2:]
    qshape = gg.shape[0:4] + (width,)
    low_lanes = slice(0, 2 * width)
    high_lanes = slice(2 * width, 4 * width)

    def part(c):
        return slice(c * width, (c + 1) * width)


    d = lax.axis_index("dp")
    m = lax.axis_index("mp")
    z = d // 4
    y = (d // 2) % 2
    x = d % 2
    zg = z // 2
    zl = z % 2
    zp = z + 1 - 2 * zl
    sib = (d, 1 - m)
    xn = (d + 1 - 2 * x, m)
    yn = (d + 2 - 4 * y, m)
    near = (zp * 4 + y * 2 + x, m)
    far = ((z + 2 - 4 * zg) * 4 + y * 2 + x, m)
    zs = [((z + k) % 4) for k in (1, 2, 3)]
    zn = [(zs[k] * 4 + y * 2 + x, m) for k in range(3)]
    base = zl * local
    other = (1 - zl) * local

    load_in = pltpu.make_async_copy(win_ref, red_ref.at[0], in_sem.at[0])
    load_out = pltpu.make_async_copy(wout_ref, red_ref.at[1], in_sem.at[1])
    load_cot = pltpu.make_async_copy(cot_ref, igrad_ref, in_sem.at[2])
    for c in [load_in, load_out, load_cot]:
        c.start()

    barrier = pltpu.get_barrier_semaphore()
    plane = [
        (
            z * 4 + (y + a * (1 - 2 * y)) * 2 + (x + b * (1 - 2 * x)),
            m + c * (1 - 2 * m),
        )
        for a in (0, 1)
        for b in (0, 1)
        for c in (0, 1)
        if a + b + c > 0
    ]
    everyone = [
        (
            zk * 4 + (y + a * (1 - 2 * y)) * 2 + (x + b * (1 - 2 * x)),
            m + c * (1 - 2 * m),
        )
        for k, zk in enumerate([z] + zs)
        for a in (0, 1)
        for b in (0, 1)
        for c in (0, 1)
        if k + a + b + c > 0
    ]
    for peer in everyone:
        pl.semaphore_signal(barrier, inc=1, device_id=peer, device_id_type=MESH)
    pl.semaphore_wait(barrier, len(everyone))

    def rcopy(src, dst, ss, rs, dev):
        return pltpu.make_async_remote_copy(
            src_ref=src, dst_ref=dst, send_sem=ss, recv_sem=rs, device_id=dev, device_id_type=MESH
        )

    def start(copies):
        for c in copies:
            c.start()

    def arrive(copies):
        for c in copies:
            c.wait_recv()

    def sent(copies):
        for c in copies:
            c.wait_send()

    def blk_rows(b):
        return pl.ds(pl.multiple_of(b * tb, tb), tb)

    def own_rows(b):
        return pl.ds(pl.multiple_of(m * half + b * tb, tb), tb)

    def sib_rows(b):
        return pl.ds(pl.multiple_of((1 - m) * half + b * tb, tb), tb)

    own_half = pl.ds(pl.multiple_of(m * half, half), half)

    zpair = pl.ds(zg * 2, 2)
    zaway = pl.ds((1 - zg) * 2, 2)

    def ag0(i):
        return [
            rcopy(wsend.at[:, i], gw.at[:, i, z, y, x], ag_ss.at[i, 0], ag_rs.at[i, 0], near)
        ]

    def ag1(i):
        part = gw.at[:, i, zpair, y, x]
        return [rcopy(part, part, ag_ss.at[i, 1], ag_rs.at[i, 1], far)]

    def ag2(i):
        return [
            rcopy(gw.at[0, i, :, y, x], gw.at[0, i, :, y, x], ag_ss.at[i, 2], ag_rs.at[i, 2], xn),
            rcopy(gw.at[1, i, :, y, x], gw.at[1, i, :, y, x], ag_ss.at[i, 3], ag_rs.at[i, 3], yn),
        ]

    def ag3(i):
        return [
            rcopy(gw.at[0, i, :, y], gw.at[0, i, :, y], ag_ss.at[i, 4], ag_rs.at[i, 4], yn),
            rcopy(gw.at[1, i, :, :, x], gw.at[1, i, :, :, x], ag_ss.at[i, 5], ag_rs.at[i, 5], xn),
        ]

    def ag_tick(t):
        if 0 <= t < local:
            arrive(ag0(t))
            start(ag1(t))
        if 0 <= t - 1 < local:
            arrive(ag1(t - 1))
            start(ag2(t - 1))
        if 0 <= t - 2 < local:
            arrive(ag2(t - 2))
            start(ag3(t - 2))

    def rs1(i):
        return [
            rcopy(gd.at[0, i, :, 1 - y], r1.at[i, 0], rs_ss.at[i, 0], rs_rs.at[i, 0], yn),
            rcopy(gd.at[1, i, :, :, 1 - x], r1.at[i, 1], rs_ss.at[i, 1], rs_rs.at[i, 1], xn),
        ]

    def rs2(i):
        return [
            rcopy(gd.at[0, i, :, y, 1 - x], r2.at[i, 0], rs_ss.at[i, 2], rs_rs.at[i, 2], xn),
            rcopy(gd.at[1, i, :, 1 - y, x], r2.at[i, 1], rs_ss.at[i, 3], rs_rs.at[i, 3], yn),
        ]

    def rs3(i):
        return [
            rcopy(gd.at[:, i, zaway, y, x], r3.at[i], rs_ss.at[i, 4], rs_rs.at[i, 4], far)
        ]

    def rs4(i):
        return [rcopy(gd.at[:, i, zp, y, x], r4.at[i], rs_ss.at[i, 5], rs_rs.at[i, 5], near)]

    def add_low(one, two):
        return (one.astype(F32) + two.astype(F32)).astype(BF16)

    def rs_b(i):
        arrive(rs1(i))
        gd[0, i, :, y] = add_low(gd[0, i, :, y], r1[i, 0])
        gd[1, i, :, :, x] = add_low(gd[1, i, :, :, x], r1[i, 1])
        start(rs2(i))

    def rs_c(i):
        arrive(rs2(i))
        for a in range(2):
            gd[a, i, :, y, x] = add_low(gd[a, i, :, y, x], r2[i, a])
        start(rs3(i))

    def rs_d(i):
        arrive(rs3(i))
        red_ref[:, base + i] = gd[:, i, z, y, x].astype(F32) + r3[i, :, zl].astype(F32)
        gd[:, i, zp, y, x] = add_low(gd[:, i, zp, y, x], r3[i, :, 1 - zl])
        start(rs4(i))

    def rs_e(i):
        arrive(rs4(i))
        red_ref[:, other + i] = r4[i].astype(F32)

    gq1 = [
        rcopy(gq.at[z, y, x], gq.at[z, y, x], gq_ss.at[k], gq_rs.at[k], zn[k]) for k in range(3)
    ]

    def same(ref, sems, k, peer):
        return rcopy(ref, ref, sems[0].at[k], sems[1].at[k], peer)

    gq_sems = (gq_ss, gq_rs)
    gq2 = [
        same(gq.at[:, y, x, :, low_lanes], gq_sems, 3, xn),
        same(gq.at[:, y, x, :, high_lanes], gq_sems, 4, yn),
    ]
    gq3 = [
        same(gq.at[:, y, :, :, low_lanes], gq_sems, 5, yn),
        same(gq.at[:, :, x, :, high_lanes], gq_sems, 6, xn),
    ]
    gr1 = [
        rcopy(gg.at[:, 1 - y, :, :, low_lanes], q1.at[0], gr_ss.at[0], gr_rs.at[0], yn),
        rcopy(gg.at[:, :, 1 - x, :, high_lanes], q1.at[1], gr_ss.at[1], gr_rs.at[1], xn),
    ]
    gr2 = [
        rcopy(gg.at[:, y, 1 - x, :, low_lanes], q2.at[0], gr_ss.at[2], gr_rs.at[2], xn),
        rcopy(gg.at[:, 1 - y, x, :, high_lanes], q2.at[1], gr_ss.at[3], gr_rs.at[3], yn),
    ]
    gr3 = [
        rcopy(gg.at[zs[k], y, x], q3.at[k], gr_ss.at[4 + k], gr_rs.at[4 + k], zn[k])
        for k in range(3)
    ]

    send_x = rcopy(x_ref, x_sib, sib_ss.at[0], sib_rs.at[0], sib)
    own_g = g_all.at[0, own_half]
    pair_g = g_all.at[1, own_half]
    send_g = rcopy(own_g, own_g, sib_ss.at[1], sib_rs.at[1], sib)
    near_g = rcopy(own_g, pair_g, near_ss.at[0], near_rs.at[0], near)
    pass_g = rcopy(pair_g, pair_g, sib_ss.at[2], sib_rs.at[2], sib)
    near_gates = rcopy(gates.at[0], gates.at[1], near_ss.at[1], near_rs.at[1], near)

    def near_x2(b):
        r = own_rows(b)
        return rcopy(x2.at[0, r], x2.at[1, r], x2_ss.at[b], x2_rs.at[b], near)

    def pass_x2(b):
        r = own_rows(b)
        return rcopy(x2.at[1, r], x2.at[1, r], x2f_ss.at[b], x2f_rs.at[b], sib)

    pair_copies = [
        rcopy(pair_s.at[k], pair_r.at[k], sib_ss.at[3 + k], sib_rs.at[3 + k], sib)
        for k in range(2)
    ]
    back_copies = [
        rcopy(x_sib, back_r.at[0], near_ss.at[2], near_rs.at[2], near),
        rcopy(mix_s, back_r.at[1], near_ss.at[3], near_rs.at[3], near),
    ]
    send_mix = rcopy(pair_s.at[1], mix_r, sib_ss.at[5], sib_rs.at[5], sib)
    send_first = rcopy(pair_s.at[0], gfirst_r, sib_ss.at[6], sib_rs.at[6], sib)

    place = (y * 2 + x) * 2 + m

    class SumAll:
        def __init__(self, src, group, line, ss, rs):
            self.src, self.group, self.line = src, group, line
            self.near = [
                rcopy(src.at[0], group.at[place], ss.at[k], rs.at[k], plane[k]) for k in range(7)
            ]
            self.along = [
                rcopy(src.at[1], line.at[z], ss.at[7 + k], rs.at[7 + k], zn[k]) for k in range(3)
            ]

        def one(self):
            start(self.near)
            self.group[place] = self.src[0]

        def two(self):
            arrive(self.near)
            total = self.group[0]
            for k in range(1, 8):
                total = total + self.group[k]
            self.src[1] = total
            start(self.along)
            self.line[z] = total

        def three(self):
            arrive(self.along)
            return (self.line[0] + self.line[1]) + (self.line[2] + self.line[3])

        def done(self):
            sent(self.near + self.along)

    early = SumAll(ar_s, ar_g, ar_z, ar_ss, ar_rs)
    late = SumAll(la_s, la_g, la_z, la_ss, la_rs)
    me = d * 2 + m
    last = [
        rcopy(sc_s, sc_g.at[me], sc_ss.at[k], sc_rs.at[k], peer)
        for k, peer in enumerate(everyone)
    ]

    send_x.start()
    for c in range(3):
        gq[z, y, x, :, part(c)] = qkv_ref[c].astype(BF16)
    gq[z, y, x, :, part(3)] = wo_ref[...].astype(BF16)
    start(gq1)

    load_in.wait()
    load_out.wait()

    def cast_weights(i, carry):
        for a in range(2):
            wsend[a, i] = red_ref[a, other + i].astype(BF16)
        start(ag0(i))
        for a in range(2):
            gw[a, i, z, y, x] = red_ref[a, base + i].astype(BF16)
        return carry

    lax.fori_loop(0, local, cast_weights, 0)

    gain1 = norm_ref[0:1, :]
    bias1 = norm_ref[1:2, :]
    gain2 = norm_ref[2:3, :]
    bias2 = norm_ref[3:4, :]

    def first_norm(rows, source, b):
        unit, _ = row_stats(source[blk_rows(b), :].astype(F32))
        x1[rows, :] = (unit * gain1 + bias1).astype(BF16)

    def first_own(b, carry):
        first_norm(own_rows(b), x_ref, b)
        return carry

    def first_sib(b, carry):
        first_norm(sib_rows(b), x_sib, b)
        return carry

    lax.fori_loop(0, own_blocks, first_own, 0)
    arrive(gq1)
    start(gq2)
    ag_tick(0)
    send_x.wait_recv()
    lax.fori_loop(0, own_blocks, first_sib, 0)
    arrive(gq2)
    start(gq3)

    def cast_cot(b, carry):
        g_all[0, own_rows(b), :] = igrad_ref[blk_rows(b), :].astype(BF16)
        return carry

    load_cot.wait()
    lax.fori_loop(0, own_blocks, cast_cot, 0)
    send_g.start()
    def clear(b, carry):
        r = blk_rows(b)
        for st in range(2):
            mix[st, r, :] = jnp.zeros((tb, D), F32)
            gsec[st, r, :] = jnp.zeros((tb, D), F32)
        return carry

    lax.fori_loop(0, blocks, clear, 0)
    wgt_t[...] = jnp.zeros(wgt_t.shape, F32)
    arrive(gq3)

    for c in range(4):
        wq[c] = gq[:, :, :, :, part(c)].reshape(D, width)

    def flat(c):
        return wq[c]

    def project(b, carry):
        r = blk_rows(b)
        normed = x1[r, :]
        qs[r, :] = (mm(normed, flat(0)).astype(BF16).astype(F32) * SCORE_SCALE).astype(BF16)
        ks[r, :] = mm(normed, flat(1)).astype(BF16)
        vs[r, :] = mm(normed, flat(2)).astype(BF16)
        return carry

    lax.fori_loop(0, blocks, project, 0)
    ag_tick(1)
    near_g.start()

    def att_copy(b):
        r = blk_rows(b)
        return rcopy(att_s.at[r], att_r.at[r], att_ss.at[b], att_rs.at[b], sib)

    def attention(pbuf):
        def p_out(b):
            return pltpu.make_async_copy(pbuf.at[b % 2], p_hbm.at[b], p_sem.at[b % 2])

        def attend(b, carry):
            r = blk_rows(b)

            @pl.when(b >= 2)
            def _():
                p_out(b - 2).wait()

            outs = []
            for h in range(heads):
                cs = slice(h * HD, (h + 1) * HD)
                s = mm(qs[r, cs], ks[:, cs], NT)
                powers = jnp.exp2((s - jnp.max(s, axis=1, keepdims=True)) * LOG2E)
                inv = 1.0 / jnp.sum(powers, axis=1, keepdims=True)
                prob = (powers * inv).astype(BF16)
                pbuf[b % 2, h] = prob
                outs.append(mm(prob, vs[:, cs]))
            p_out(b).start()
            context = jnp.concatenate(outs, axis=1).astype(BF16)
            ctx[r, :] = context
            att_s[r, :] = mm(context, flat(3), NT).astype(BF16)
            att_copy(b).start()
            @pl.when(b == 2)
            def _():
                ag_tick(2)

            return carry

        lax.fori_loop(0, blocks, attend, 0)
        p_out(blocks - 2).wait()
        p_out(blocks - 1).wait()

    pl.run_scoped(attention, pltpu.VMEM(pshape, BF16))

    ag_tick(3)

    router_t = router_ref[:, 0:D]
    router_hi = router_t.astype(BF16)
    router_lo = (router_t - router_hi.astype(F32)).astype(BF16)
    task = task_ref[0]
    n_tasks = router_ref.shape[1] - D
    task_lanes = lax.broadcasted_iota(jnp.int32, (experts, n_tasks), 1)
    task_bias = jnp.sum(
        jnp.where(task_lanes == task, router_ref[:, D:], 0.0), axis=1, keepdims=True
    )
    row_id = lax.broadcasted_iota(jnp.int32, (experts, tb), 0)
    gates[0, experts : 2 * experts, :] = jnp.full((experts, rows_all), task.astype(F32), F32)

    def second_norm(rows, source, b, gb):
        att_copy(gb).wait_recv()
        rows_mid = (
            source[blk_rows(b), :].astype(F32)
            + att_s[rows, :].astype(F32)
            + att_r[rows, :].astype(F32)
        )
        mid[rows, :] = rows_mid
        unit, _ = row_stats(rows_mid)
        normed = (unit * gain2 + bias2).astype(BF16)
        x2[0, rows, :] = normed
        logits = mm(router_hi, normed, NT) + mm(router_lo, normed, NT) + task_bias
        chosen = row_id == routes_ref[0:1, rows]
        for k in range(1, TOP):
            chosen = jnp.logical_or(chosen, row_id == routes_ref[k : k + 1, rows])
        peak = jnp.max(jnp.where(chosen, logits, -jnp.inf), axis=0, keepdims=True)
        powers = jnp.where(chosen, jnp.exp(logits - peak), 0.0)
        share = powers / jnp.sum(powers, axis=0, keepdims=True)
        gates[0, 0:experts, rows] = share

    def second_own(b, carry):
        second_norm(own_rows(b), x_ref, b, m * own_blocks + b)
        near_x2(b).start()
        return carry

    def second_sib(b, carry):
        second_norm(sib_rows(b), x_sib, b, (1 - m) * own_blocks + b)
        return carry

    lax.fori_loop(0, own_blocks, second_own, 0)
    lax.fori_loop(0, own_blocks, second_sib, 0)
    near_gates.start()
    send_g.wait_recv()

    def gate_grad(st, share_all, rows):
        share = wgt_t[st, :, rows]
        grad_logits = share - share_all * jnp.sum(share, axis=0, keepdims=True)
        high = grad_logits.astype(BF16)
        low = (grad_logits - high.astype(F32)).astype(BF16)
        normed = x2[st, rows, :]
        rg = mm(high, normed) + mm(low, normed)
        tg = jnp.sum(grad_logits, axis=1, keepdims=True)
        return gsec[st, rows, :] + mm(high, router_hi, TN), rg, tg

    def pair_rows_in():
        near_gates.wait_recv()
        pass_g.wait_recv()

        def land(b, carry):
            pass_x2(b).wait_recv()
            return carry

        lax.fori_loop(0, own_blocks, land, 0)

    def pass_rows(b, carry):
        near_x2(b).wait_recv()
        pass_x2(b).start()
        return carry

    task_row = lax.broadcasted_iota(jnp.int32, (experts, 128), 1).astype(F32)

    def pair_rows_out():
        def keep(b, carry):
            rg, tg = carry
            rows = own_rows(b)
            upstream, more_rg, more_tg = gate_grad(1, gates[1, 0:experts, rows], rows)
            gsec[1, rows, :] = upstream
            return rg + more_rg, tg + more_tg

        def give(b, carry):
            rg, tg = carry
            rows = sib_rows(b)
            upstream, more_rg, more_tg = gate_grad(1, gates[1, 0:experts, rows], rows)
            pair_s[0, blk_rows(b), :] = upstream.astype(BF16)
            pair_s[1, blk_rows(b), :] = mix[1, rows, :].astype(BF16)
            return rg + more_rg, tg + more_tg

        zero = (jnp.zeros((experts, D), F32), jnp.zeros((experts, 1), F32))
        sums = lax.fori_loop(0, own_blocks, give, zero)
        start(pair_copies)
        rg, tg = lax.fori_loop(0, own_blocks, keep, sums)
        ar_s[0] = jnp.zeros(ar_s.shape[1:], F32)
        ar_s[0, 8:16, :] = rg
        pair_task = gates[1, experts : experts + 1, 0:128]
        ar_s[0, 16:24, 0:128] = jnp.where(task_row == pair_task, tg, 0.0)

    def pair_grads_back():
        pair_copies[0].wait_recv()

        def grads(b, carry):
            r = blk_rows(b)
            x_sib[r, :] = (gsec[1, own_rows(b), :] + pair_r[0, r, :].astype(F32)).astype(BF16)
            return carry

        lax.fori_loop(0, own_blocks, grads, 0)
        back_copies[0].start()

    def pair_mix_back():
        pair_copies[1].wait_recv()

        def rows(b, carry):
            r = blk_rows(b)
            mix_s[r, :] = (mix[1, own_rows(b), :] + pair_r[1, r, :].astype(F32)).astype(BF16)
            return carry

        lax.fori_loop(0, own_blocks, rows, 0)
        back_copies[1].start()

    def all_experts(g_gate, hid, gpre):
        def segment(s, carry):
            pair = jnp.logical_and(s >= 2, s < 6)
            st = jnp.where(pair, 1, 0)
            i = s - jnp.where(s >= 6, 4, jnp.where(s >= 2, 2, 0))
            e = base + i
            first = jnp.logical_or(s < 2, jnp.logical_and(s >= 4, s < 6))

            @pl.when(first)
            def _():
                arrive(ag3(i))

            @pl.when(s == 1)
            def _():
                ag_tick(4)
                near_g.wait_recv()
                pass_g.start()

            @pl.when(s == 2)
            def _():
                pair_rows_in()
                ag_tick(5)

            @pl.when(s == 3)
            def _():
                start(rs1(0))

            @pl.when(s == 4)
            def _():
                start(rs1(1))

            @pl.when(s == 5)
            def _():
                rs_b(0)

            @pl.when(s == 6)
            def _():
                pair_rows_out()
                rs_b(1)
                rs_c(0)
                pair_grads_back()

            @pl.when(s == 7)
            def _():
                start(rs1(2))
                rs_c(1)
                rs_d(0)

            def block(b, carry2):
                r = pl.ds(pl.multiple_of(b * mb, mb), mb)
                w_in = gw[0, i].reshape(D, hidden_width)
                w_out = gw[1, i].reshape(D, hidden_width)
                gate = gates[st, pl.ds(e, 1), r].T
                pre = mm(x2[st, r, :], w_in)
                incoming = (gate * g_all[st, r, :].astype(F32)).astype(BF16)
                g_gate[r, :] = incoming
                grad_hidden = mm(incoming, w_out)
                phi = 0.5 + 0.5 * lax.erf(pre * SQRT_HALF)
                density = jnp.exp2(pre * pre * (-0.5 * LOG2E)) * INV_SQRT_TWO_PI
                hidden = (pre * phi).astype(BF16)
                hid[r, :] = hidden
                grad_pre = (grad_hidden * (phi + pre * density)).astype(BF16)
                gpre[r, :] = grad_pre
                produced = mm(hidden, w_out, NT)
                mix[st, r, :] += gate * produced
                weight = jnp.sum(incoming.astype(F32) * produced, axis=1, keepdims=True)
                wgt_t[st, pl.ds(e, 1), r] = weight.T
                gsec[st, r, :] += mm(grad_pre, w_in, NT)
                return carry2

            lax.fori_loop(0, rows_all // mb, block, 0)

            @pl.when(s == 1)
            def _():
                lax.fori_loop(0, own_blocks, pass_rows, 0)


            def keep_sum(a, value):
                @pl.when(first)
                def _():
                    gd[a, i] = value.astype(BF16)

                @pl.when(jnp.logical_not(first))
                def _():
                    gd[a, i] = (gd[a, i].astype(F32) + value).astype(BF16)

            keep_sum(0, mm(x2[st], gpre[...], TN).reshape(wshape))
            keep_sum(1, mm(g_gate[...], hid[...], TN).reshape(wshape))
            return carry

        lax.fori_loop(0, 2 * local, segment, 0)

    pl.run_scoped(
        all_experts,
        pltpu.VMEM((rows_all, D), BF16),
        pltpu.VMEM((rows_all, hidden_width), BF16),
        pltpu.VMEM((rows_all, hidden_width), BF16),
    )
    start(rs1(3))

    def gs_copy(b):
        r = blk_rows(b)
        return rcopy(att_s.at[r], gs_r.at[r], gs_ss.at[b], gs_rs.at[b], sib)

    for b in range(blocks):
        att_copy(b).wait_send()

    def gate_sib(b, carry):
        rg, tg = carry
        rows = sib_rows(b)
        upstream, more_rg, more_tg = gate_grad(0, gates[0, 0:experts, rows], rows)
        att_s[rows, :] = upstream.astype(BF16)
        gs_copy((1 - m) * own_blocks + b).start()
        return rg + more_rg, tg + more_tg

    def gate_own(b, carry):
        rg, tg = carry
        rows = own_rows(b)
        upstream, more_rg, more_tg = gate_grad(0, gates[0, 0:experts, rows], rows)
        att_s[rows, :] = (upstream + back_r[0, blk_rows(b), :].astype(F32)).astype(BF16)
        gs_copy(m * own_blocks + b).start()
        return rg + more_rg, tg + more_tg

    sums = (jnp.zeros((experts, D), F32), jnp.zeros((experts, 1), F32))
    sums = lax.fori_loop(0, own_blocks, gate_sib, sums)
    back_copies[0].wait_recv()
    rg, tg = lax.fori_loop(0, own_blocks, gate_own, sums)
    ar_s[0, 8:16, :] += rg
    ar_s[0, 16:24, 0:128] += jnp.where(task_row == task.astype(F32), tg, 0.0)

    rs_b(2)
    rs_d(1)
    pair_mix_back()
    sent(pair_copies)

    def mix_out(b, carry):
        pair_s[1, blk_rows(b), :] = mix[0, sib_rows(b), :].astype(BF16)
        return carry

    lax.fori_loop(0, own_blocks, mix_out, 0)
    send_mix.start()

    gml = att_r
    w_o = flat(3)

    def back_second(rows, gb):
        gs_copy(gb).wait_recv()
        grad_second = att_s[rows, :].astype(F32) + gs_r[rows, :].astype(F32)
        unit, inv_std = row_stats(mid[rows, :])
        back = row_back(grad_second, unit, inv_std, gain2)
        return grad_second, unit, back

    def back_own(b, carry):
        gain_sum, bias_sum = carry
        rows = own_rows(b)
        grad_second, unit, back = back_second(rows, m * own_blocks + b)
        grad_mid = igrad_ref[blk_rows(b), :] + back
        igrad_ref[blk_rows(b), :] = grad_mid
        grad_low = grad_mid.astype(BF16)
        gml[rows, :] = grad_low
        gctx[rows, :] = mm(grad_low, w_o).astype(BF16)
        gain_sum = gain_sum + jnp.sum(grad_second * unit, axis=0, keepdims=True)
        bias_sum = bias_sum + jnp.sum(grad_second, axis=0, keepdims=True)
        return gain_sum, bias_sum

    def back_sib(b, carry):
        rows = sib_rows(b)
        grad_second, unit, back = back_second(rows, (1 - m) * own_blocks + b)
        grad_low = (g_all[0, rows, :].astype(F32) + back).astype(BF16)
        gml[rows, :] = grad_low
        gctx[rows, :] = mm(grad_low, w_o).astype(BF16)
        return carry

    zero_row = jnp.zeros((1, D), F32)
    gain2_grad, bias2_grad = lax.fori_loop(0, own_blocks, back_own, (zero_row, zero_row))
    ar_s[0, 2:3, :] = gain2_grad
    ar_s[0, 3:4, :] = bias2_grad
    early.one()
    lax.fori_loop(0, own_blocks, back_sib, 0)
    gg[:, :, :, :, part(3)] = mm(gml[...], ctx[...], TN).reshape(qshape).astype(BF16)

    rs_b(3)
    rs_c(2)
    pass_g.wait_send()

    def last_part(pbuf, keys_acc, values_acc):

        def p_in(b):
            return pltpu.make_async_copy(p_hbm.at[b], pbuf.at[b % 2], p_sem.at[b % 2])

        p_in(0).start()
        keys_acc[...] = jnp.zeros(keys_acc.shape, F32)
        values_acc[...] = jnp.zeros(values_acc.shape, F32)

        def attend_back(b, carry):
            r = blk_rows(b)

            @pl.when(b + 1 < blocks)
            def _():
                p_in(b + 1).start()

            p_in(b).wait()
            outs = []
            for h in range(heads):
                cs = slice(h * HD, (h + 1) * HD)
                grad_block = gctx[r, cs]
                inner = jnp.sum(
                    grad_block.astype(F32) * ctx[r, cs].astype(F32), axis=1, keepdims=True
                )
                grad_prob = mm(grad_block, vs[:, cs], NT)
                prob = pbuf[b % 2, h]
                grad_scores = (prob.astype(F32) * (grad_prob - inner)).astype(BF16)
                outs.append(mm(grad_scores, ks[:, cs]) * SCORE_SCALE)
                keys_acc[cs, :] += mm(qs[r, cs], grad_scores, TN)
                values_acc[cs, :] += mm(grad_block, prob, TN)
            g_all[1, r, 0:width] = jnp.concatenate(outs, axis=1).astype(BF16)

            @pl.when(b == 2)
            def _():
                rs_c(3)

            @pl.when(b == 3)
            def _():
                rs_d(2)
                early.two()

            @pl.when(b == 5)
            def _():
                rs_d(3)
                rs_e(0)
                rs_e(1)

            return carry

        lax.fori_loop(0, blocks, attend_back, 0)

        normed = x1[...]
        gg[:, :, :, :, part(0)] = mm(normed, g_all[1, :, 0:width], TN).reshape(qshape).astype(BF16)
        gg[:, :, :, :, part(1)] = mm(normed, keys_acc[...].astype(BF16), TT).reshape(qshape).astype(BF16)
        gg[:, :, :, :, part(2)] = mm(normed, values_acc[...].astype(BF16), TT).reshape(qshape).astype(BF16)
        start(gr1)
        small_ref[...] = early.three()

        def grad_first(rows):
            return (
                mm(g_all[1, rows, 0:width], flat(0), NT)
                + mm(keys_acc[:, rows].astype(BF16), flat(1), TT)
                + mm(values_acc[:, rows].astype(BF16), flat(2), TT)
            )

        def first_back_sib(b, carry):
            pair_s[0, blk_rows(b), :] = grad_first(sib_rows(b)).astype(BF16)
            return carry

        def first_back_own(b, carry):
            gsec[0, blk_rows(b), :] = grad_first(own_rows(b))
            return carry

        lax.fori_loop(0, own_blocks, first_back_sib, 0)
        send_first.start()
        lax.fori_loop(0, own_blocks, first_back_own, 0)

    pl.run_scoped(
        last_part,
        pltpu.VMEM(pshape, BF16),
        pltpu.VMEM((width, rows_all), F32),
        pltpu.VMEM((width, rows_all), F32),
    )

    arrive(gr1)
    gg[:, y, :, :, low_lanes] = add_low(gg[:, y, :, :, low_lanes], q1[0])
    gg[:, :, x, :, high_lanes] = add_low(gg[:, :, x, :, high_lanes], q1[1])
    start(gr2)
    send_first.wait_recv()

    def back_first(b, carry):
        gain_sum, bias_sum = carry
        r = blk_rows(b)
        upstream = gsec[0, r, :] + gfirst_r[r, :].astype(F32)
        unit, inv_std = row_stats(x_ref[r, :].astype(F32))
        igrad_ref[r, :] += row_back(upstream, unit, inv_std, gain1)
        gain_sum = gain_sum + jnp.sum(upstream * unit, axis=0, keepdims=True)
        bias_sum = bias_sum + jnp.sum(upstream, axis=0, keepdims=True)
        return gain_sum, bias_sum

    gain1_grad, bias1_grad = lax.fori_loop(0, own_blocks, back_first, (zero_row, zero_row))
    la_s[0] = jnp.zeros(la_s.shape[1:], F32)
    la_s[0, 0:1, :] = gain1_grad
    la_s[0, 1:2, :] = bias1_grad

    late.one()

    send_mix.wait_recv()
    back_copies[1].wait_recv()

    def write_out(b, carry):
        r = blk_rows(b)
        rows = own_rows(b)
        out_ref[r, :] = (
            mid[rows, :]
            + mix[0, rows, :]
            + mix_r[r, :].astype(F32)
            + back_r[1, r, :].astype(F32)
        )
        return carry

    lax.fori_loop(0, own_blocks, write_out, 0)

    arrive(gr2)
    gg[:, y, x, :, low_lanes] = add_low(gg[:, y, x, :, low_lanes], q2[0])
    gg[:, y, x, :, high_lanes] = add_low(gg[:, y, x, :, high_lanes], q2[1])
    start(gr3)
    rs_e(2)
    rs_e(3)

    def squares(e, acc):
        for a in range(2):
            acc = acc + jnp.sum(red_ref[a, e] * red_ref[a, e], axis=0, keepdims=True)
        return acc

    columns = lax.fori_loop(0, experts, squares, jnp.zeros((1, hidden_width), F32))
    late.two()

    arrive(gr3)
    total = gg[z, y, x].astype(F32)
    for k in range(3):
        total = total + q3[k].astype(F32)
    redq_ref[...] = total
    columns = columns + jnp.sum(total * total, axis=0, keepdims=True)
    sc_s[...] = jnp.full(sc_s.shape, jnp.sum(columns), F32)
    start(last)
    sc_g[me] = sc_s[...]
    late_ref[0:2, :] = late.three()[0:2]
    arrive(last)
    total = sc_g[0]
    for k in range(1, len(everyone) + 1):
        total = total + sc_g[k]
    late_ref[2:8, :] = jnp.broadcast_to(total[0:1, 0:1], (6, D))

    sent(gq1 + gq2 + gq3 + gr1 + gr2 + gr3)
    early.done()
    late.done()
    sent(last)
    sent([send_x, send_g, near_g, near_gates, send_mix, send_first] + back_copies)
    for i in range(local):
        sent(ag0(i) + ag1(i) + ag2(i) + ag3(i))
        sent(rs1(i) + rs2(i) + rs3(i) + rs4(i))

    def drain_rows(b, carry):
        gs_copy(b).wait_send()
        return carry

    def drain_own(b, carry):
        near_x2(b).wait_send()
        pass_x2(b).wait_send()
        return carry

    lax.fori_loop(0, blocks, drain_rows, 0)
    lax.fori_loop(0, own_blocks, drain_own, 0)


def step_call(x_rows, cotangent, task_ids, routes, norms, qkv, wo, router, win, wout):
    half = x_rows.shape[0]
    rows_all = 2 * half
    experts, shard, hidden = win.shape
    local = experts // 2
    width = wo.shape[1]
    blocks = rows_all // ROW_BLOCK
    own_blocks = half // ROW_BLOCK
    heads = width // HD
    vmem = pl.BlockSpec(memory_space=pltpu.VMEM)
    hbm = pl.BlockSpec(memory_space=pl.ANY)
    grid = (GRID_Z, GRID_Y, GRID_X)
    struct = jax.ShapeDtypeStruct
    dma = pltpu.SemaphoreType.DMA
    outs = (
        struct((half, D), F32),
        struct((half, D), F32),
        struct((2, experts, shard, hidden), F32),
        struct((shard, 4 * width), F32),
        struct((24, D), F32),
        struct((8, D), F32),
        struct((blocks, heads, ROW_BLOCK, rows_all), BF16),
    )
    scratch = [
        pltpu.VMEM((half, D), BF16),
        pltpu.VMEM((2, rows_all, D), BF16),
        pltpu.VMEM((rows_all, D), BF16),
        pltpu.VMEM((rows_all, width), BF16),
        pltpu.VMEM((rows_all, width), BF16),
        pltpu.VMEM((rows_all, width), BF16),
        pltpu.VMEM((rows_all, width), BF16),
        pltpu.VMEM((rows_all, D), BF16),
        pltpu.VMEM((rows_all, D), BF16),
        pltpu.VMEM((rows_all, D), F32),
        pltpu.VMEM((2, rows_all, D), BF16),
        pltpu.VMEM((2, 2 * experts, rows_all), F32),
        pltpu.VMEM((2, experts, rows_all), F32),
        pltpu.VMEM((2, rows_all, D), F32),
        pltpu.VMEM((2, rows_all, D), F32),
        pltpu.VMEM((rows_all, D), BF16),
        pltpu.VMEM((half, D), BF16),
        pltpu.VMEM((half, D), BF16),
        pltpu.VMEM((rows_all, width), BF16),
        pltpu.VMEM((half, D), BF16),
        pltpu.VMEM((2, half, D), BF16),
        pltpu.VMEM((2, half, D), BF16),
        pltpu.VMEM((2, half, D), BF16),
        pltpu.VMEM((2, local) + grid + (shard, hidden), BF16),
        pltpu.VMEM((2, local) + grid + (shard, hidden), BF16),
        pltpu.VMEM((2, local, shard, hidden), BF16),
        pltpu.VMEM((local, 2, 4, 2, shard, hidden), BF16),
        pltpu.VMEM((local, 2, 4, shard, hidden), BF16),
        pltpu.VMEM((local, 2, 2, shard, hidden), BF16),
        pltpu.VMEM((local, 2, shard, hidden), BF16),
        pltpu.VMEM(grid + (shard, 4 * width), BF16),
        pltpu.VMEM((4, D, width), BF16),
        pltpu.VMEM(grid + (shard, 4 * width), BF16),
        pltpu.VMEM((2, 4, 2, shard, 2 * width), BF16),
        pltpu.VMEM((2, 4, shard, 2 * width), BF16),
        pltpu.VMEM((3, shard, 4 * width), BF16),
        pltpu.VMEM((2, 24, D), F32),
        pltpu.VMEM((8, 24, D), F32),
        pltpu.VMEM((4, 24, D), F32),
        pltpu.VMEM((2, 8, D), F32),
        pltpu.VMEM((8, 8, D), F32),
        pltpu.VMEM((4, 8, D), F32),
        pltpu.VMEM((8, 128), F32),
        pltpu.VMEM((32, 8, 128), F32),
    ]
    for size in [
        (local, 6),
        (local, 6),
        (7,),
        (7,),
        (7,),
        (4,),
        (own_blocks,),
        (own_blocks,),
        (blocks,),
        (blocks,),
        (10,),
        (10,),
        (31,),
    ]:
        scratch += [dma(size), dma(size)]
    scratch += [dma((2,)), dma((3,))]
    return pl.pallas_call(
        step_kernel,
        out_shape=outs,
        in_specs=[vmem, hbm, pl.BlockSpec(memory_space=pltpu.SMEM)] + [vmem] * 5 + [hbm] * 2,
        out_specs=[vmem] * 6 + [hbm],
        scratch_shapes=scratch,
        compiler_params=pltpu.CompilerParams(
            collective_id=0, has_side_effects=True, vmem_limit_bytes=64 << 20
        ),
        name="step",
    )(
        x_rows,
        cotangent,
        task_ids,
        routes.T,
        norms,
        qkv,
        wo,
        router.T,
        win,
        wout,
    )


def adam_parts(weight, first, second, average, gradient, clip_scale, rate):
    clipped = clip_scale * gradient
    first_new = BETA_FIRST * first + (1.0 - BETA_FIRST) * clipped
    second_new = BETA_SECOND * second + (1.0 - BETA_SECOND) * clipped * clipped
    first_hat = first_new * (1.0 / (1.0 - BETA_FIRST**STEP))
    second_hat = second_new * (1.0 / (1.0 - BETA_SECOND**STEP))
    weight_new = weight - rate * (
        first_hat / (jnp.sqrt(second_hat) + ADAM_EPS) + WEIGHT_DECAY * weight
    )
    return weight_new, first_new, second_new, EMA_KEEP * average + (1.0 - EMA_KEEP) * weight_new


def adam_kernel(*refs):
    red, redq, small, late, rows_in, back_in = refs[:6]
    state = [refs[6 + 4 * k : 10 + 4 * k] for k in range(6)]
    norm_out, rows_out, back_out = refs[30:33]
    fresh = [refs[33 + 4 * k : 37 + 4 * k] for k in range(6)]
    step = pl.program_id(0)
    width = redq.shape[1] // 4

    rows_out[...] = rows_in[...]
    back_out[...] = back_in[...]
    norm_grad = jnp.concatenate([late[0:2, :], small[2:4, :]], axis=0)
    router_grad = small[8:16, :]
    task_grad = small[16:24, 0:TASKS]
    total = (
        jnp.max(late[2:3, 0:1])
        + jnp.sum(norm_grad * norm_grad)
        + jnp.sum(router_grad * router_grad)
        + jnp.sum(task_grad * task_grad)
    )
    grad_norm = jnp.sqrt(jnp.full((1, 1), total, F32))
    clip = jnp.minimum(1.0, CLIP_LIMIT / (grad_norm + 1e-06))

    def update(k, gradient, rate, *index):
        new = adam_parts(*[r[index] for r in state[k]], gradient, clip, rate)
        for r, v in zip(fresh[k], new):
            r[index] = v

    @pl.when(step == 0)
    def _():
        norm_out[0] = jnp.max(grad_norm)
        update(0, norm_grad, NORM_RATE, slice(None))
        for c in range(3):
            update(1, redq[:, c * width : (c + 1) * width], LEARN_RATE, c)
        update(2, redq[:, 3 * width :], LEARN_RATE, slice(None))
        update(3, router_grad, LEARN_RATE, slice(None), slice(0, D))
        update(3, task_grad, LEARN_RATE, slice(None), slice(D, D + TASKS))

    update(4, red[0], LEARN_RATE, slice(None))
    update(5, red[1], LEARN_RATE, slice(None))


def adam_call(red, redq, small, late, output, input_grad, state):
    experts, shard, hidden = red.shape[1:]
    per = 2
    steps = experts // per

    def fixed(array):
        rank = len(array.shape)
        return pl.BlockSpec(array.shape, lambda s: (0,) * rank)

    rows = pl.BlockSpec((output.shape[0] // steps, D), lambda s: (s, 0))
    tile = pl.BlockSpec((per, shard, hidden), lambda s: (s, 0, 0))
    specs = []
    for k, group in enumerate(state):
        specs += [tile if k >= 4 else fixed(a) for a in group]
    flat = [a for group in state for a in group]
    struct = jax.ShapeDtypeStruct
    results = pl.pallas_call(
        adam_kernel,
        grid=(steps,),
        out_shape=[struct((1,), F32), struct(output.shape, F32), struct(output.shape, F32)]
        + [struct(a.shape, F32) for a in flat],
        in_specs=[
            pl.BlockSpec((2, per, shard, hidden), lambda s: (0, s, 0, 0)),
            fixed(redq),
            fixed(small),
            fixed(late),
            rows,
            rows,
        ]
        + specs,
        out_specs=[pl.BlockSpec(memory_space=pltpu.SMEM), rows, rows] + specs,
        compiler_params=pltpu.CompilerParams(vmem_limit_bytes=64 << 20),
        name="adam",
    )(red, redq, small, late, output, input_grad, *flat)
    fresh = [results[3 + 4 * k : 7 + 4 * k] for k in range(6)]
    return results[0], results[1], results[2], fresh


def shards(
    x_rows,
    cotangent,
    task_ids,
    routes,
    norm_params,
    norm_first,
    norm_second,
    norm_ema,
    qkv_weight,
    qkv_first,
    qkv_second,
    qkv_ema,
    out_weight,
    out_first,
    out_second,
    out_ema,
    router,
    router_first,
    router_second,
    router_ema,
    expert_in,
    expert_in_first,
    expert_in_second,
    expert_in_ema,
    expert_out,
    expert_out_first,
    expert_out_second,
    expert_out_ema,
):
    qkv_full, out_full, in_full, eout_full = (
        lax.all_gather(qkv_weight.astype(jnp.bfloat16), "dp", axis=1, tiled=True),
        lax.all_gather(out_weight.astype(jnp.bfloat16), "dp", axis=0, tiled=True),
        lax.all_gather(expert_in.astype(jnp.bfloat16), "dp", axis=1, tiled=True),
        lax.all_gather(expert_out.astype(jnp.bfloat16), "dp", axis=1, tiled=True),
    )
    local_width = qkv_full.shape[2]
    local_heads = local_width // HD
    x_float = x_rows.astype(jnp.float32)
    first_normed, first_unit, first_inv = norm_forward(x_float, norm_params[0], norm_params[1])
    first_all = lax.all_gather(first_normed.astype(jnp.bfloat16), "mp", axis=0, tiled=True)
    triple = jnp.einsum(
        "rd,cdh->crh", first_all, qkv_full, preferred_element_type=jnp.float32
    ).astype(jnp.bfloat16)
    heads = triple.reshape(3, IMGS, L, local_heads, HD)
    context_heads, log_total = lax.map(
        lambda member: attend_image(member[0], member[1], member[2], QB),
        (heads[0], heads[1], heads[2]),
    )
    context = context_heads.reshape(R, local_width)
    attended_part = jnp.einsum("rh,dh->rd", context, out_full, preferred_element_type=jnp.float32)
    attended = lax.psum_scatter(
        attended_part.astype(jnp.bfloat16), "mp", scatter_dimension=0, tiled=True
    ).astype(jnp.float32)
    mid = x_float + attended
    second_normed, second_unit, second_inv = norm_forward(mid, norm_params[2], norm_params[3])
    second_all = lax.all_gather(second_normed.astype(jnp.bfloat16), "mp", axis=0, tiled=True)
    second_float = second_all.astype(jnp.float32)
    task_onehot = (task_ids[:, None] == jnp.arange(TASKS, dtype=jnp.int32)[None, :]).astype(
        jnp.float32
    )
    task_bias = dense_exact(task_onehot, router[D:])
    logits = dense_exact(second_float, router[:D])
    logits = (logits.reshape(IMGS, L, E) + task_bias[:, None, :]).reshape(R, E)
    route_hot = (routes[:, :, None] == jnp.arange(E, dtype=jnp.int32)[None, None, :]).astype(
        jnp.float32
    )
    chosen = jnp.sum(route_hot * logits[:, None, :], axis=-1)
    gates = jax.nn.softmax(chosen, axis=-1)
    slots = slot_table(routes, E, CAP)
    pair_ids = jnp.arange(R * TOP, dtype=jnp.int32)
    slot_pair = jnp.full((E * CAP,), R * TOP, jnp.int32).at[slots].set(pair_ids)
    slot_token = (slot_pair // TOP).reshape(E, CAP)
    gate_padded = jnp.concatenate([gates.reshape(-1), jnp.zeros((1,), jnp.float32)])
    slot_gate = gate_padded[slot_pair].reshape(E, CAP)
    padded_rows = jnp.concatenate([second_all, jnp.zeros((1, D), jnp.bfloat16)], axis=0)

    def expert_forward(carry, member):
        weight_in, weight_out, owners, owner_gate = member
        dispatched = padded_rows[owners]
        pre = jnp.dot(dispatched, weight_in, preferred_element_type=jnp.float32)
        hidden = gelu_exact(pre).astype(jnp.bfloat16)
        produced = jnp.einsum("cf,df->cd", hidden, weight_out, preferred_element_type=jnp.float32)
        return (carry.at[owners].add(owner_gate[:, None] * produced), None)

    mixture_acc, unused = lax.scan(
        expert_forward,
        jnp.zeros((R + 1, D), jnp.float32),
        (in_full, eout_full, slot_token, slot_gate),
    )
    mixture = lax.psum_scatter(
        mixture_acc[:R].astype(jnp.bfloat16), "mp", scatter_dimension=0, tiled=True
    ).astype(jnp.float32)
    output = mid + mixture
    grad_low_all = lax.all_gather(cotangent.astype(jnp.bfloat16), "mp", axis=0, tiled=True)
    grad_padded = jnp.concatenate([grad_low_all, jnp.zeros((1, D), jnp.bfloat16)], axis=0)

    def expert_backward(carry, member):
        weight_in, weight_out, owners, owner_gate = member
        dispatched = padded_rows[owners]
        pre = jnp.dot(dispatched, weight_in, preferred_element_type=jnp.float32)
        hidden = gelu_exact(pre).astype(jnp.bfloat16)
        produced = jnp.einsum("cf,df->cd", hidden, weight_out, preferred_element_type=jnp.float32)
        incoming = grad_padded[owners].astype(jnp.float32)
        slot_grad_gate = jnp.sum(incoming * produced, axis=-1)
        grad_produced = (owner_gate[:, None] * incoming).astype(jnp.bfloat16)
        grad_hidden = jnp.dot(grad_produced, weight_out, preferred_element_type=jnp.float32)
        grad_pre = (grad_hidden * gelu_slope(pre)).astype(jnp.bfloat16)
        grad_weight_out = jnp.einsum(
            "cd,cf->df", grad_produced, hidden, preferred_element_type=jnp.float32
        )
        grad_weight_in = jnp.einsum(
            "cd,cf->df", dispatched, grad_pre, preferred_element_type=jnp.float32
        )
        grad_dispatched = jnp.einsum(
            "cf,df->cd", grad_pre, weight_in, preferred_element_type=jnp.float32
        )
        return (
            carry.at[owners].add(grad_dispatched),
            (grad_weight_in, grad_weight_out, slot_grad_gate),
        )

    expert_carry, expert_outs = lax.scan(
        expert_backward,
        jnp.zeros((R + 1, D), jnp.float32),
        (in_full, eout_full, slot_token, slot_gate),
    )
    grad_in_stack, grad_eout_stack, slot_grad_gate = expert_outs
    in_reduced, eout_reduced = (
        lax.psum_scatter(grad_in_stack, "dp", scatter_dimension=1, tiled=True),
        lax.psum_scatter(grad_eout_stack, "dp", scatter_dimension=1, tiled=True),
    )
    grad_gates = slot_grad_gate.reshape(-1)[slots].reshape(R, TOP)
    grad_chosen = gates * (grad_gates - jnp.sum(gates * grad_gates, axis=-1, keepdims=True))
    grad_logits = jnp.sum(route_hot * grad_chosen[:, :, None], axis=1)
    router_rows_grad = dense_exact(second_float.T, grad_logits)
    task_rows_grad = dense_exact(task_onehot.T, jnp.sum(grad_logits.reshape(IMGS, L, E), axis=1))
    router_grad_part = jnp.concatenate([router_rows_grad, task_rows_grad], axis=0)
    grad_second_part = expert_carry[:R] + dense_exact(grad_logits, router[:D].T)
    grad_second = lax.psum_scatter(
        grad_second_part.astype(jnp.bfloat16), "mp", scatter_dimension=0, tiled=True
    ).astype(jnp.float32)
    grad_mid_norm, gain_two_grad, shift_two_grad = norm_backward(
        grad_second, second_unit, second_inv, norm_params[2]
    )
    grad_mid = cotangent + grad_mid_norm
    grad_mid_all = lax.all_gather(grad_mid.astype(jnp.bfloat16), "mp", axis=0, tiled=True)
    grad_out_weight = jnp.einsum(
        "rd,rh->dh", grad_mid_all, context, preferred_element_type=jnp.float32
    )
    grad_context = jnp.dot(grad_mid_all, out_full, preferred_element_type=jnp.float32).astype(
        jnp.bfloat16
    )
    grad_context_heads = grad_context.reshape(IMGS, L, local_heads, HD)
    grad_queries, grad_keys, grad_values = lax.map(
        lambda member: attend_image_back(member[0], member[1], member[2], member[3], member[4], QB),
        (heads[0], heads[1], heads[2], log_total, grad_context_heads),
    )
    grad_triple = jnp.stack(
        [
            grad_queries.reshape(R, local_width),
            grad_keys.reshape(R, local_width),
            grad_values.reshape(R, local_width),
        ],
        axis=0,
    )
    grad_qkv_weight = jnp.einsum(
        "rd,crh->cdh", first_all, grad_triple, preferred_element_type=jnp.float32
    )
    grad_first_part = jnp.einsum(
        "crh,cdh->rd", grad_triple, qkv_full, preferred_element_type=jnp.float32
    )
    grad_first = lax.psum_scatter(
        grad_first_part.astype(jnp.bfloat16), "mp", scatter_dimension=0, tiled=True
    ).astype(jnp.float32)
    grad_x_norm, gain_one_grad, shift_one_grad = norm_backward(
        grad_first, first_unit, first_inv, norm_params[0]
    )
    input_grad = grad_mid + grad_x_norm
    norm_grad_part = jnp.stack(
        [gain_one_grad, shift_one_grad, gain_two_grad, shift_two_grad], axis=0
    )
    norm_grad, router_grad = lax.psum((norm_grad_part, router_grad_part), ("dp", "mp"))
    qkv_reduced, out_reduced = (
        lax.psum_scatter(grad_qkv_weight, "dp", scatter_dimension=1, tiled=True),
        lax.psum_scatter(grad_out_weight, "dp", scatter_dimension=0, tiled=True),
    )
    local_squares = (
        jnp.sum(qkv_reduced * qkv_reduced)
        + jnp.sum(out_reduced * out_reduced)
        + jnp.sum(in_reduced * in_reduced)
        + jnp.sum(eout_reduced * eout_reduced)
    )
    share = 1.0 / (lax.axis_size("dp") * lax.axis_size("mp"))
    small_squares = jnp.sum(norm_grad * norm_grad) + jnp.sum(router_grad * router_grad)
    total_squares = lax.psum(local_squares + share * small_squares, ("dp", "mp"))
    grad_norm = jnp.sqrt(total_squares)
    clip_scale = jnp.minimum(1.0, CLIP_LIMIT / (grad_norm + 1e-06))
    norm_new, norm_first_new, norm_second_new, norm_ema_new = adam_update(
        norm_params, norm_first, norm_second, norm_ema, norm_grad, clip_scale, NORM_RATE
    )
    qkv_new, qkv_first_new, qkv_second_new, qkv_ema_new = adam_update(
        qkv_weight, qkv_first, qkv_second, qkv_ema, qkv_reduced, clip_scale, LEARN_RATE
    )
    out_new, out_first_new, out_second_new, out_ema_new = adam_update(
        out_weight, out_first, out_second, out_ema, out_reduced, clip_scale, LEARN_RATE
    )
    router_new, router_first_new, router_second_new, router_ema_new = adam_update(
        router, router_first, router_second, router_ema, router_grad, clip_scale, LEARN_RATE
    )
    in_new, in_first_new, in_second_new, in_ema_new = adam_update(
        expert_in,
        expert_in_first,
        expert_in_second,
        expert_in_ema,
        in_reduced,
        clip_scale,
        LEARN_RATE,
    )
    eout_new, eout_first_new, eout_second_new, eout_ema_new = adam_update(
        expert_out,
        expert_out_first,
        expert_out_second,
        expert_out_ema,
        eout_reduced,
        clip_scale,
        LEARN_RATE,
    )
    return (
        output,
        input_grad,
        grad_norm.reshape(1),
        norm_new,
        norm_first_new,
        norm_second_new,
        norm_ema_new,
        qkv_new,
        qkv_first_new,
        qkv_second_new,
        qkv_ema_new,
        out_new,
        out_first_new,
        out_second_new,
        out_ema_new,
        router_new,
        router_first_new,
        router_second_new,
        router_ema_new,
        in_new,
        in_first_new,
        in_second_new,
        in_ema_new,
        eout_new,
        eout_first_new,
        eout_second_new,
        eout_ema_new,
    )


def shards_fused(
    x_rows,
    cotangent,
    task_ids,
    routes,
    norm_params,
    norm_first,
    norm_second,
    norm_ema,
    qkv_weight,
    qkv_first,
    qkv_second,
    qkv_ema,
    out_weight,
    out_first,
    out_second,
    out_ema,
    router,
    router_first,
    router_second,
    router_ema,
    expert_in,
    expert_in_first,
    expert_in_second,
    expert_in_ema,
    expert_out,
    expert_out_first,
    expert_out_second,
    expert_out_ema,
):
    output, input_grad, expert_red, qkvo_red, small, late, unused = step_call(
        x_rows,
        cotangent,
        task_ids,
        routes,
        norm_params,
        qkv_weight,
        out_weight,
        router,
        expert_in,
        expert_out,
    )
    state = [
        (norm_params, norm_first, norm_second, norm_ema),
        (qkv_weight, qkv_first, qkv_second, qkv_ema),
        (out_weight, out_first, out_second, out_ema),
        (router.T, router_first.T, router_second.T, router_ema.T),
        (expert_in, expert_in_first, expert_in_second, expert_in_ema),
        (expert_out, expert_out_first, expert_out_second, expert_out_ema),
    ]
    grad_norm, output, input_grad, fresh = adam_call(
        expert_red, qkvo_red, small, late, output, input_grad, state
    )
    fresh[3] = [a.T for a in fresh[3]]
    flat = [a for group in fresh for a in group]
    return (output, input_grad, grad_norm, *flat)


def solution(mesh):
    fused = mesh.shape["dp"] == GRID_Z * GRID_Y * GRID_X and mesh.shape["mp"] == 2
    return jax.shard_map(
        shards_fused if fused else shards,
        mesh=mesh,
        in_specs=(
            P(("dp", "mp"), None),
            P(("dp", "mp"), None),
            P("dp"),
            P("dp", None),
            P(),
            P(),
            P(),
            P(),
            P(None, "dp", "mp"),
            P(None, "dp", "mp"),
            P(None, "dp", "mp"),
            P(None, "dp", "mp"),
            P("dp", "mp"),
            P("dp", "mp"),
            P("dp", "mp"),
            P("dp", "mp"),
            P(),
            P(),
            P(),
            P(),
            P(None, "dp", "mp"),
            P(None, "dp", "mp"),
            P(None, "dp", "mp"),
            P(None, "dp", "mp"),
            P(None, "dp", "mp"),
            P(None, "dp", "mp"),
            P(None, "dp", "mp"),
            P(None, "dp", "mp"),
        ),
        out_specs=(
            P(("dp", "mp"), None),
            P(("dp", "mp"), None),
            P(),
            P(),
            P(),
            P(),
            P(),
            P(None, "dp", "mp"),
            P(None, "dp", "mp"),
            P(None, "dp", "mp"),
            P(None, "dp", "mp"),
            P("dp", "mp"),
            P("dp", "mp"),
            P("dp", "mp"),
            P("dp", "mp"),
            P(),
            P(),
            P(),
            P(),
            P(None, "dp", "mp"),
            P(None, "dp", "mp"),
            P(None, "dp", "mp"),
            P(None, "dp", "mp"),
            P(None, "dp", "mp"),
            P(None, "dp", "mp"),
            P(None, "dp", "mp"),
            P(None, "dp", "mp"),
        ),
        check_vma=False,
    )
```

```python
import jax
import jax.numpy as jnp
from jax import lax
from jax.experimental import pallas as pl
from jax.experimental.pallas import tpu as pltpu
from jax.sharding import PartitionSpec as P

D = 384
HD = 64
E = 8
TOP = 4
TASKS = 5
L = 1536
STEP = 10
IMGS = 1
R = 1536
QB = 512
CAP = 1536


NORM_EPS = 1e-06
SCORE_SCALE = 0.125
CLIP_LIMIT = 1.0
BETA_FIRST = 0.9
BETA_SECOND = 0.999
LEARN_RATE = 0.1
NORM_RATE = 0.5
WEIGHT_DECAY = 0.05
ADAM_EPS = 1e-08
EMA_KEEP = 0.6
SQRT_HALF = 0.7071067811865476
INV_SQRT_TWO_PI = 0.3989422804014327


def norm_forward(rows, gain, shift):
    row_mean = jnp.mean(rows, axis=-1, keepdims=True)
    centered = rows - row_mean
    inv_std = lax.rsqrt(jnp.mean(centered * centered, axis=-1, keepdims=True) + NORM_EPS)
    unit = centered * inv_std
    return (unit * gain + shift, unit, inv_std)


def norm_backward(upstream, unit, inv_std, gain):
    scaled = upstream * gain
    inner = jnp.mean(scaled * unit, axis=-1, keepdims=True)
    grad_rows = inv_std * (scaled - jnp.mean(scaled, axis=-1, keepdims=True) - unit * inner)
    return (grad_rows, jnp.sum(upstream * unit, axis=0), jnp.sum(upstream, axis=0))


def gelu_exact(values):
    return 0.5 * values * (1.0 + lax.erf(values * SQRT_HALF))


def gelu_slope(values):
    return 0.5 * (1.0 + lax.erf(values * SQRT_HALF)) + values * INV_SQRT_TWO_PI * jnp.exp(
        -0.5 * values * values
    )


def dense_exact(left, right):
    return jnp.dot(left, right, precision=lax.Precision.HIGHEST, preferred_element_type=jnp.float32)


def slot_table(route_rows, experts, capacity):
    flat_routes = route_rows.reshape(-1)
    one_hot = (flat_routes[:, None] == jnp.arange(experts, dtype=jnp.int32)[None, :]).astype(
        jnp.int32
    )
    earlier = jnp.cumsum(one_hot, axis=0) - one_hot
    position = jnp.sum(earlier * one_hot, axis=1)
    return flat_routes * capacity + position


def attend_image(queries, keys_img, values_img, block_rows):
    blended_parts = []
    total_parts = []
    for offset in range(0, queries.shape[0], block_rows):
        query_block = queries[offset : offset + block_rows]
        scores = (
            jnp.einsum("qhd,khd->hqk", query_block, keys_img, preferred_element_type=jnp.float32)
            * SCORE_SCALE
        )
        row_peak = jnp.max(scores, axis=-1, keepdims=True)
        powers = jnp.exp(scores - row_peak)
        row_total = jnp.sum(powers, axis=-1, keepdims=True)
        probability = (powers / row_total).astype(jnp.bfloat16)
        blended = jnp.einsum(
            "hqk,khd->qhd", probability, values_img, preferred_element_type=jnp.float32
        )
        blended_parts.append(blended.astype(jnp.bfloat16))
        total_parts.append((row_peak + jnp.log(row_total))[:, :, 0])
    return (jnp.concatenate(blended_parts, axis=0), jnp.concatenate(total_parts, axis=1))


def attend_image_back(queries, keys_img, values_img, log_total, grad_context, block_rows):
    query_parts = []
    grad_keys = jnp.zeros(keys_img.shape, jnp.float32)
    grad_values = jnp.zeros(values_img.shape, jnp.float32)
    for offset in range(0, queries.shape[0], block_rows):
        query_block = queries[offset : offset + block_rows]
        grad_block = grad_context[offset : offset + block_rows]
        scores = (
            jnp.einsum("qhd,khd->hqk", query_block, keys_img, preferred_element_type=jnp.float32)
            * SCORE_SCALE
        )
        probability = jnp.exp(scores - log_total[:, offset : offset + block_rows, None])
        prob_low = probability.astype(jnp.bfloat16)
        grad_prob = jnp.einsum(
            "qhd,khd->hqk", grad_block, values_img, preferred_element_type=jnp.float32
        )
        inner = jnp.sum(probability * grad_prob, axis=-1, keepdims=True)
        grad_scores = (probability * (grad_prob - inner)).astype(jnp.bfloat16)
        query_parts.append(
            jnp.einsum("hqk,khd->qhd", grad_scores, keys_img, preferred_element_type=jnp.float32)
            * SCORE_SCALE
        )
        grad_keys = (
            grad_keys
            + jnp.einsum(
                "hqk,qhd->khd", grad_scores, query_block, preferred_element_type=jnp.float32
            )
            * SCORE_SCALE
        )
        grad_values = grad_values + jnp.einsum(
            "hqk,qhd->khd", prob_low, grad_block, preferred_element_type=jnp.float32
        )
    grad_queries = jnp.concatenate(query_parts, axis=0)
    return (
        grad_queries.astype(jnp.bfloat16),
        grad_keys.astype(jnp.bfloat16),
        grad_values.astype(jnp.bfloat16),
    )


def adam_update(weight, first, second, average, gradient, clip_scale, rate):
    clipped = clip_scale * gradient
    first_new = BETA_FIRST * first + (1.0 - BETA_FIRST) * clipped
    second_new = BETA_SECOND * second + (1.0 - BETA_SECOND) * clipped * clipped
    first_hat = first_new / (1.0 - BETA_FIRST**STEP)
    second_hat = second_new / (1.0 - BETA_SECOND**STEP)
    weight_new = weight - rate * (
        first_hat / (jnp.sqrt(second_hat) + ADAM_EPS) + WEIGHT_DECAY * weight
    )
    average_new = EMA_KEEP * average + (1.0 - EMA_KEEP) * weight_new
    return (weight_new, first_new, second_new, average_new)


F32 = jnp.float32
BF16 = jnp.bfloat16
MESH = pl.DeviceIdType.MESH
LOG2E = 1.4426950408889634
NN = ((1,), (0,))
NT = ((1,), (1,))
TN = ((0,), (0,))
TT = ((0,), (1,))
GRID_Z, GRID_Y, GRID_X = 4, 2, 2
ROW_BLOCK = 256
EXPERT_BLOCK = 512


def mm(left, right, dims=NN):
    return lax.dot_general(left, right, (dims, ((), ())), preferred_element_type=F32)


def row_stats(rows):
    centered = rows - jnp.mean(rows, axis=-1, keepdims=True)
    inv_std = lax.rsqrt(jnp.mean(centered * centered, axis=-1, keepdims=True) + NORM_EPS)
    return centered * inv_std, inv_std


def row_back(upstream, unit, inv_std, gain):
    scaled = upstream * gain
    inner = jnp.mean(scaled * unit, axis=-1, keepdims=True)
    return inv_std * (scaled - jnp.mean(scaled, axis=-1, keepdims=True) - unit * inner)


def step_kernel(
    x_ref,
    cot_ref,
    task_ref,
    routes_ref,
    norm_ref,
    qkv_ref,
    wo_ref,
    router_ref,
    win_ref,
    wout_ref,
    out_ref,
    igrad_ref,
    red_ref,
    redq_ref,
    small_ref,
    late_ref,
    p_hbm,
    x_sib,
    g_all,
    x1,
    qs,
    ks,
    vs,
    ctx,
    att_s,
    att_r,
    mid,
    x2,
    gates,
    wgt_t,
    mix,
    gsec,
    gs_r,
    mix_s,
    mix_r,
    gctx,
    gfirst_r,
    pair_s,
    pair_r,
    back_r,
    gw,
    gd,
    wsend,
    r1,
    r2,
    r3,
    r4,
    gq,
    wq,
    gg,
    q1,
    q2,
    q3,
    ar_s,
    ar_g,
    ar_z,
    la_s,
    la_g,
    la_z,
    sc_s,
    sc_g,
    ag_ss,
    ag_rs,
    rs_ss,
    rs_rs,
    gq_ss,
    gq_rs,
    gr_ss,
    gr_rs,
    sib_ss,
    sib_rs,
    near_ss,
    near_rs,
    x2_ss,
    x2_rs,
    x2f_ss,
    x2f_rs,
    att_ss,
    att_rs,
    gs_ss,
    gs_rs,
    ar_ss,
    ar_rs,
    la_ss,
    la_rs,
    sc_ss,
    sc_rs,
    p_sem,
    in_sem,
):
    experts = win_ref.shape[0]
    local = experts // 2
    half = x_ref.shape[0]
    rows_all = 2 * half
    width = qs.shape[1]
    hidden_width = gw.shape[-1]
    heads = width // HD
    tb = ROW_BLOCK
    mb = EXPERT_BLOCK
    blocks = rows_all // tb
    own_blocks = half // tb
    pshape = (2, heads, tb, rows_all)
    wshape = gw.shape[2:]
    qshape = gg.shape[0:4] + (width,)
    low_lanes = slice(0, 2 * width)
    high_lanes = slice(2 * width, 4 * width)

    def part(c):
        return slice(c * width, (c + 1) * width)


    d = lax.axis_index("dp")
    m = lax.axis_index("mp")
    z = d // 4
    y = (d // 2) % 2
    x = d % 2
    zg = z // 2
    zl = z % 2
    zp = z + 1 - 2 * zl
    sib = (d, 1 - m)
    xn = (d + 1 - 2 * x, m)
    yn = (d + 2 - 4 * y, m)
    near = (zp * 4 + y * 2 + x, m)
    far = ((z + 2 - 4 * zg) * 4 + y * 2 + x, m)
    zs = [((z + k) % 4) for k in (1, 2, 3)]
    zn = [(zs[k] * 4 + y * 2 + x, m) for k in range(3)]
    base = zl * local
    other = (1 - zl) * local

    load_in = pltpu.make_async_copy(win_ref, red_ref.at[0], in_sem.at[0])
    load_out = pltpu.make_async_copy(wout_ref, red_ref.at[1], in_sem.at[1])
    load_cot = pltpu.make_async_copy(cot_ref, igrad_ref, in_sem.at[2])
    for c in [load_in, load_out, load_cot]:
        c.start()

    barrier = pltpu.get_barrier_semaphore()
    plane = [
        (
            z * 4 + (y + a * (1 - 2 * y)) * 2 + (x + b * (1 - 2 * x)),
            m + c * (1 - 2 * m),
        )
        for a in (0, 1)
        for b in (0, 1)
        for c in (0, 1)
        if a + b + c > 0
    ]
    everyone = [
        (
            zk * 4 + (y + a * (1 - 2 * y)) * 2 + (x + b * (1 - 2 * x)),
            m + c * (1 - 2 * m),
        )
        for k, zk in enumerate([z] + zs)
        for a in (0, 1)
        for b in (0, 1)
        for c in (0, 1)
        if k + a + b + c > 0
    ]
    for peer in everyone:
        pl.semaphore_signal(barrier, inc=1, device_id=peer, device_id_type=MESH)
    pl.semaphore_wait(barrier, len(everyone))

    def rcopy(src, dst, ss, rs, dev):
        return pltpu.make_async_remote_copy(
            src_ref=src, dst_ref=dst, send_sem=ss, recv_sem=rs, device_id=dev, device_id_type=MESH
        )

    def start(copies):
        for c in copies:
            c.start()

    def arrive(copies):
        for c in copies:
            c.wait_recv()

    def sent(copies):
        for c in copies:
            c.wait_send()

    def blk_rows(b):
        return pl.ds(pl.multiple_of(b * tb, tb), tb)

    def own_rows(b):
        return pl.ds(pl.multiple_of(m * half + b * tb, tb), tb)

    def sib_rows(b):
        return pl.ds(pl.multiple_of((1 - m) * half + b * tb, tb), tb)

    own_half = pl.ds(pl.multiple_of(m * half, half), half)

    zpair = pl.ds(zg * 2, 2)
    zaway = pl.ds((1 - zg) * 2, 2)

    def ag0(i):
        return [
            rcopy(wsend.at[:, i], gw.at[:, i, z, y, x], ag_ss.at[i, 0], ag_rs.at[i, 0], near)
        ]

    def ag1(i):
        part = gw.at[:, i, zpair, y, x]
        return [rcopy(part, part, ag_ss.at[i, 1], ag_rs.at[i, 1], far)]

    def ag2(i):
        return [
            rcopy(gw.at[0, i, :, y, x], gw.at[0, i, :, y, x], ag_ss.at[i, 2], ag_rs.at[i, 2], xn),
            rcopy(gw.at[1, i, :, y, x], gw.at[1, i, :, y, x], ag_ss.at[i, 3], ag_rs.at[i, 3], yn),
        ]

    def ag3(i):
        return [
            rcopy(gw.at[0, i, :, y], gw.at[0, i, :, y], ag_ss.at[i, 4], ag_rs.at[i, 4], yn),
            rcopy(gw.at[1, i, :, :, x], gw.at[1, i, :, :, x], ag_ss.at[i, 5], ag_rs.at[i, 5], xn),
        ]

    def ag_tick(t):
        if 0 <= t < local:
            arrive(ag0(t))
            start(ag1(t))
        if 0 <= t - 1 < local:
            arrive(ag1(t - 1))
            start(ag2(t - 1))
        if 0 <= t - 2 < local:
            arrive(ag2(t - 2))
            start(ag3(t - 2))

    def rs1(i):
        return [
            rcopy(gd.at[0, i, :, 1 - y], r1.at[i, 0], rs_ss.at[i, 0], rs_rs.at[i, 0], yn),
            rcopy(gd.at[1, i, :, :, 1 - x], r1.at[i, 1], rs_ss.at[i, 1], rs_rs.at[i, 1], xn),
        ]

    def rs2(i):
        return [
            rcopy(gd.at[0, i, :, y, 1 - x], r2.at[i, 0], rs_ss.at[i, 2], rs_rs.at[i, 2], xn),
            rcopy(gd.at[1, i, :, 1 - y, x], r2.at[i, 1], rs_ss.at[i, 3], rs_rs.at[i, 3], yn),
        ]

    def rs3(i):
        return [
            rcopy(gd.at[:, i, zaway, y, x], r3.at[i], rs_ss.at[i, 4], rs_rs.at[i, 4], far)
        ]

    def rs4(i):
        return [rcopy(gd.at[:, i, zp, y, x], r4.at[i], rs_ss.at[i, 5], rs_rs.at[i, 5], near)]

    def add_low(one, two):
        return (one.astype(F32) + two.astype(F32)).astype(BF16)

    def rs_b(i):
        arrive(rs1(i))
        gd[0, i, :, y] = add_low(gd[0, i, :, y], r1[i, 0])
        gd[1, i, :, :, x] = add_low(gd[1, i, :, :, x], r1[i, 1])
        start(rs2(i))

    def rs_c(i):
        arrive(rs2(i))
        for a in range(2):
            gd[a, i, :, y, x] = add_low(gd[a, i, :, y, x], r2[i, a])
        start(rs3(i))

    def rs_d(i):
        arrive(rs3(i))
        red_ref[:, base + i] = gd[:, i, z, y, x].astype(F32) + r3[i, :, zl].astype(F32)
        gd[:, i, zp, y, x] = add_low(gd[:, i, zp, y, x], r3[i, :, 1 - zl])
        start(rs4(i))

    def rs_e(i):
        arrive(rs4(i))
        red_ref[:, other + i] = r4[i].astype(F32)

    gq1 = [
        rcopy(gq.at[z, y, x], gq.at[z, y, x], gq_ss.at[k], gq_rs.at[k], zn[k]) for k in range(3)
    ]

    def same(ref, sems, k, peer):
        return rcopy(ref, ref, sems[0].at[k], sems[1].at[k], peer)

    gq_sems = (gq_ss, gq_rs)
    gq2 = [
        same(gq.at[:, y, x, :, low_lanes], gq_sems, 3, xn),
        same(gq.at[:, y, x, :, high_lanes], gq_sems, 4, yn),
    ]
    gq3 = [
        same(gq.at[:, y, :, :, low_lanes], gq_sems, 5, yn),
        same(gq.at[:, :, x, :, high_lanes], gq_sems, 6, xn),
    ]
    gr1 = [
        rcopy(gg.at[:, 1 - y, :, :, low_lanes], q1.at[0], gr_ss.at[0], gr_rs.at[0], yn),
        rcopy(gg.at[:, :, 1 - x, :, high_lanes], q1.at[1], gr_ss.at[1], gr_rs.at[1], xn),
    ]
    gr2 = [
        rcopy(gg.at[:, y, 1 - x, :, low_lanes], q2.at[0], gr_ss.at[2], gr_rs.at[2], xn),
        rcopy(gg.at[:, 1 - y, x, :, high_lanes], q2.at[1], gr_ss.at[3], gr_rs.at[3], yn),
    ]
    gr3 = [
        rcopy(gg.at[zs[k], y, x], q3.at[k], gr_ss.at[4 + k], gr_rs.at[4 + k], zn[k])
        for k in range(3)
    ]

    send_x = rcopy(x_ref, x_sib, sib_ss.at[0], sib_rs.at[0], sib)
    own_g = g_all.at[0, own_half]
    pair_g = g_all.at[1, own_half]
    send_g = rcopy(own_g, own_g, sib_ss.at[1], sib_rs.at[1], sib)
    near_g = rcopy(own_g, pair_g, near_ss.at[0], near_rs.at[0], near)
    pass_g = rcopy(pair_g, pair_g, sib_ss.at[2], sib_rs.at[2], sib)
    near_gates = rcopy(gates.at[0], gates.at[1], near_ss.at[1], near_rs.at[1], near)

    def near_x2(b):
        r = own_rows(b)
        return rcopy(x2.at[0, r], x2.at[1, r], x2_ss.at[b], x2_rs.at[b], near)

    def pass_x2(b):
        r = own_rows(b)
        return rcopy(x2.at[1, r], x2.at[1, r], x2f_ss.at[b], x2f_rs.at[b], sib)

    pair_copies = [
        rcopy(pair_s.at[k], pair_r.at[k], sib_ss.at[3 + k], sib_rs.at[3 + k], sib)
        for k in range(2)
    ]
    back_copies = [
        rcopy(x_sib, back_r.at[0], near_ss.at[2], near_rs.at[2], near),
        rcopy(mix_s, back_r.at[1], near_ss.at[3], near_rs.at[3], near),
    ]
    send_mix = rcopy(pair_s.at[1], mix_r, sib_ss.at[5], sib_rs.at[5], sib)
    send_first = rcopy(pair_s.at[0], gfirst_r, sib_ss.at[6], sib_rs.at[6], sib)

    place = (y * 2 + x) * 2 + m

    class SumAll:
        def __init__(self, src, group, line, ss, rs):
            self.src, self.group, self.line = src, group, line
            self.near = [
                rcopy(src.at[0], group.at[place], ss.at[k], rs.at[k], plane[k]) for k in range(7)
            ]
            self.along = [
                rcopy(src.at[1], line.at[z], ss.at[7 + k], rs.at[7 + k], zn[k]) for k in range(3)
            ]

        def one(self):
            start(self.near)
            self.group[place] = self.src[0]

        def two(self):
            arrive(self.near)
            total = self.group[0]
            for k in range(1, 8):
                total = total + self.group[k]
            self.src[1] = total
            start(self.along)
            self.line[z] = total

        def three(self):
            arrive(self.along)
            return (self.line[0] + self.line[1]) + (self.line[2] + self.line[3])

        def done(self):
            sent(self.near + self.along)

    early = SumAll(ar_s, ar_g, ar_z, ar_ss, ar_rs)
    late = SumAll(la_s, la_g, la_z, la_ss, la_rs)
    me = d * 2 + m
    last = [
        rcopy(sc_s, sc_g.at[me], sc_ss.at[k], sc_rs.at[k], peer)
        for k, peer in enumerate(everyone)
    ]

    send_x.start()
    for c in range(3):
        gq[z, y, x, :, part(c)] = qkv_ref[c].astype(BF16)
    gq[z, y, x, :, part(3)] = wo_ref[...].astype(BF16)
    start(gq1)

    load_in.wait()
    load_out.wait()

    def cast_weights(i, carry):
        for a in range(2):
            wsend[a, i] = red_ref[a, other + i].astype(BF16)
        start(ag0(i))
        for a in range(2):
            gw[a, i, z, y, x] = red_ref[a, base + i].astype(BF16)
        return carry

    lax.fori_loop(0, local, cast_weights, 0)

    gain1 = norm_ref[0:1, :]
    bias1 = norm_ref[1:2, :]
    gain2 = norm_ref[2:3, :]
    bias2 = norm_ref[3:4, :]

    def first_norm(rows, source, b):
        unit, _ = row_stats(source[blk_rows(b), :].astype(F32))
        x1[rows, :] = (unit * gain1 + bias1).astype(BF16)

    def first_own(b, carry):
        first_norm(own_rows(b), x_ref, b)
        return carry

    def first_sib(b, carry):
        first_norm(sib_rows(b), x_sib, b)
        return carry

    lax.fori_loop(0, own_blocks, first_own, 0)
    arrive(gq1)
    start(gq2)
    ag_tick(0)
    send_x.wait_recv()
    lax.fori_loop(0, own_blocks, first_sib, 0)
    arrive(gq2)
    start(gq3)

    def cast_cot(b, carry):
        g_all[0, own_rows(b), :] = igrad_ref[blk_rows(b), :].astype(BF16)
        return carry

    load_cot.wait()
    lax.fori_loop(0, own_blocks, cast_cot, 0)
    send_g.start()
    def clear(b, carry):
        r = blk_rows(b)
        for st in range(2):
            mix[st, r, :] = jnp.zeros((tb, D), F32)
            gsec[st, r, :] = jnp.zeros((tb, D), F32)
        return carry

    lax.fori_loop(0, blocks, clear, 0)
    wgt_t[...] = jnp.zeros(wgt_t.shape, F32)
    arrive(gq3)

    for c in range(4):
        wq[c] = gq[:, :, :, :, part(c)].reshape(D, width)

    def flat(c):
        return wq[c]

    def project(b, carry):
        r = blk_rows(b)
        normed = x1[r, :]
        qs[r, :] = (mm(normed, flat(0)).astype(BF16).astype(F32) * SCORE_SCALE).astype(BF16)
        ks[r, :] = mm(normed, flat(1)).astype(BF16)
        vs[r, :] = mm(normed, flat(2)).astype(BF16)
        return carry

    lax.fori_loop(0, blocks, project, 0)
    ag_tick(1)
    near_g.start()

    def att_copy(b):
        r = blk_rows(b)
        return rcopy(att_s.at[r], att_r.at[r], att_ss.at[b], att_rs.at[b], sib)

    def attention(pbuf):
        def p_out(b):
            return pltpu.make_async_copy(pbuf.at[b % 2], p_hbm.at[b], p_sem.at[b % 2])

        def attend(b, carry):
            r = blk_rows(b)

            @pl.when(b >= 2)
            def _():
                p_out(b - 2).wait()

            outs = []
            for h in range(heads):
                cs = slice(h * HD, (h + 1) * HD)
                s = mm(qs[r, cs], ks[:, cs], NT)
                powers = jnp.exp2((s - jnp.max(s, axis=1, keepdims=True)) * LOG2E)
                inv = 1.0 / jnp.sum(powers, axis=1, keepdims=True)
                prob = (powers * inv).astype(BF16)
                pbuf[b % 2, h] = prob
                outs.append(mm(prob, vs[:, cs]))
            p_out(b).start()
            context = jnp.concatenate(outs, axis=1).astype(BF16)
            ctx[r, :] = context
            att_s[r, :] = mm(context, flat(3), NT).astype(BF16)
            att_copy(b).start()
            @pl.when(b == 2)
            def _():
                ag_tick(2)

            return carry

        lax.fori_loop(0, blocks, attend, 0)
        p_out(blocks - 2).wait()
        p_out(blocks - 1).wait()

    pl.run_scoped(attention, pltpu.VMEM(pshape, BF16))

    ag_tick(3)

    router_t = router_ref[:, 0:D]
    router_hi = router_t.astype(BF16)
    router_lo = (router_t - router_hi.astype(F32)).astype(BF16)
    task = task_ref[0]
    n_tasks = router_ref.shape[1] - D
    task_lanes = lax.broadcasted_iota(jnp.int32, (experts, n_tasks), 1)
    task_bias = jnp.sum(
        jnp.where(task_lanes == task, router_ref[:, D:], 0.0), axis=1, keepdims=True
    )
    row_id = lax.broadcasted_iota(jnp.int32, (experts, tb), 0)
    gates[0, experts : 2 * experts, :] = jnp.full((experts, rows_all), task.astype(F32), F32)

    def second_norm(rows, source, b, gb):
        att_copy(gb).wait_recv()
        rows_mid = (
            source[blk_rows(b), :].astype(F32)
            + att_s[rows, :].astype(F32)
            + att_r[rows, :].astype(F32)
        )
        mid[rows, :] = rows_mid
        unit, _ = row_stats(rows_mid)
        normed = (unit * gain2 + bias2).astype(BF16)
        x2[0, rows, :] = normed
        logits = mm(router_hi, normed, NT) + mm(router_lo, normed, NT) + task_bias
        chosen = row_id == routes_ref[0:1, rows]
        for k in range(1, TOP):
            chosen = jnp.logical_or(chosen, row_id == routes_ref[k : k + 1, rows])
        peak = jnp.max(jnp.where(chosen, logits, -jnp.inf), axis=0, keepdims=True)
        powers = jnp.where(chosen, jnp.exp(logits - peak), 0.0)
        share = powers / jnp.sum(powers, axis=0, keepdims=True)
        gates[0, 0:experts, rows] = share

    def second_own(b, carry):
        second_norm(own_rows(b), x_ref, b, m * own_blocks + b)
        near_x2(b).start()
        return carry

    def second_sib(b, carry):
        second_norm(sib_rows(b), x_sib, b, (1 - m) * own_blocks + b)
        return carry

    lax.fori_loop(0, own_blocks, second_own, 0)
    lax.fori_loop(0, own_blocks, second_sib, 0)
    near_gates.start()
    send_g.wait_recv()

    def gate_grad(st, share_all, rows):
        share = wgt_t[st, :, rows]
        grad_logits = share - share_all * jnp.sum(share, axis=0, keepdims=True)
        high = grad_logits.astype(BF16)
        low = (grad_logits - high.astype(F32)).astype(BF16)
        normed = x2[st, rows, :]
        rg = mm(high, normed) + mm(low, normed)
        tg = jnp.sum(grad_logits, axis=1, keepdims=True)
        return gsec[st, rows, :] + mm(high, router_hi, TN), rg, tg

    def pair_rows_in():
        near_gates.wait_recv()
        pass_g.wait_recv()

        def land(b, carry):
            pass_x2(b).wait_recv()
            return carry

        lax.fori_loop(0, own_blocks, land, 0)

    def pass_rows(b, carry):
        near_x2(b).wait_recv()
        pass_x2(b).start()
        return carry

    task_row = lax.broadcasted_iota(jnp.int32, (experts, 128), 1).astype(F32)

    def pair_rows_out():
        def keep(b, carry):
            rg, tg = carry
            rows = own_rows(b)
            upstream, more_rg, more_tg = gate_grad(1, gates[1, 0:experts, rows], rows)
            gsec[1, rows, :] = upstream
            return rg + more_rg, tg + more_tg

        def give(b, carry):
            rg, tg = carry
            rows = sib_rows(b)
            upstream, more_rg, more_tg = gate_grad(1, gates[1, 0:experts, rows], rows)
            pair_s[0, blk_rows(b), :] = upstream.astype(BF16)
            pair_s[1, blk_rows(b), :] = mix[1, rows, :].astype(BF16)
            return rg + more_rg, tg + more_tg

        zero = (jnp.zeros((experts, D), F32), jnp.zeros((experts, 1), F32))
        sums = lax.fori_loop(0, own_blocks, give, zero)
        start(pair_copies)
        rg, tg = lax.fori_loop(0, own_blocks, keep, sums)
        ar_s[0] = jnp.zeros(ar_s.shape[1:], F32)
        ar_s[0, 8:16, :] = rg
        pair_task = gates[1, experts : experts + 1, 0:128]
        ar_s[0, 16:24, 0:128] = jnp.where(task_row == pair_task, tg, 0.0)

    def pair_grads_back():
        pair_copies[0].wait_recv()

        def grads(b, carry):
            r = blk_rows(b)
            x_sib[r, :] = (gsec[1, own_rows(b), :] + pair_r[0, r, :].astype(F32)).astype(BF16)
            return carry

        lax.fori_loop(0, own_blocks, grads, 0)
        back_copies[0].start()

    def pair_mix_back():
        pair_copies[1].wait_recv()

        def rows(b, carry):
            r = blk_rows(b)
            mix_s[r, :] = (mix[1, own_rows(b), :] + pair_r[1, r, :].astype(F32)).astype(BF16)
            return carry

        lax.fori_loop(0, own_blocks, rows, 0)
        back_copies[1].start()

    def all_experts(g_gate, hid, gpre):
        def segment(s, carry):
            pair = jnp.logical_and(s >= 2, s < 6)
            st = jnp.where(pair, 1, 0)
            i = s - jnp.where(s >= 6, 4, jnp.where(s >= 2, 2, 0))
            e = base + i
            first = jnp.logical_or(s < 2, jnp.logical_and(s >= 4, s < 6))

            @pl.when(first)
            def _():
                arrive(ag3(i))

            @pl.when(s == 1)
            def _():
                ag_tick(4)
                near_g.wait_recv()
                pass_g.start()

            @pl.when(s == 2)
            def _():
                pair_rows_in()
                ag_tick(5)

            @pl.when(s == 3)
            def _():
                start(rs1(0))

            @pl.when(s == 4)
            def _():
                start(rs1(1))

            @pl.when(s == 5)
            def _():
                rs_b(0)

            @pl.when(s == 6)
            def _():
                pair_rows_out()
                rs_b(1)
                rs_c(0)
                pair_grads_back()

            @pl.when(s == 7)
            def _():
                start(rs1(2))
                rs_c(1)
                rs_d(0)

            def block(b, carry2):
                r = pl.ds(pl.multiple_of(b * mb, mb), mb)
                w_in = gw[0, i].reshape(D, hidden_width)
                w_out = gw[1, i].reshape(D, hidden_width)
                gate = gates[st, pl.ds(e, 1), r].T
                pre = mm(x2[st, r, :], w_in)
                incoming = (gate * g_all[st, r, :].astype(F32)).astype(BF16)
                g_gate[r, :] = incoming
                grad_hidden = mm(incoming, w_out)
                phi = 0.5 + 0.5 * lax.erf(pre * SQRT_HALF)
                density = jnp.exp2(pre * pre * (-0.5 * LOG2E)) * INV_SQRT_TWO_PI
                hidden = (pre * phi).astype(BF16)
                hid[r, :] = hidden
                grad_pre = (grad_hidden * (phi + pre * density)).astype(BF16)
                gpre[r, :] = grad_pre
                produced = mm(hidden, w_out, NT)
                mix[st, r, :] += gate * produced
                weight = jnp.sum(incoming.astype(F32) * produced, axis=1, keepdims=True)
                wgt_t[st, pl.ds(e, 1), r] = weight.T
                gsec[st, r, :] += mm(grad_pre, w_in, NT)
                return carry2

            lax.fori_loop(0, rows_all // mb, block, 0)

            @pl.when(s == 1)
            def _():
                lax.fori_loop(0, own_blocks, pass_rows, 0)


            def keep_sum(a, value):
                @pl.when(first)
                def _():
                    gd[a, i] = value.astype(BF16)

                @pl.when(jnp.logical_not(first))
                def _():
                    gd[a, i] = (gd[a, i].astype(F32) + value).astype(BF16)

            keep_sum(0, mm(x2[st], gpre[...], TN).reshape(wshape))
            keep_sum(1, mm(g_gate[...], hid[...], TN).reshape(wshape))
            return carry

        lax.fori_loop(0, 2 * local, segment, 0)

    pl.run_scoped(
        all_experts,
        pltpu.VMEM((rows_all, D), BF16),
        pltpu.VMEM((rows_all, hidden_width), BF16),
        pltpu.VMEM((rows_all, hidden_width), BF16),
    )
    start(rs1(3))

    def gs_copy(b):
        r = blk_rows(b)
        return rcopy(att_s.at[r], gs_r.at[r], gs_ss.at[b], gs_rs.at[b], sib)

    for b in range(blocks):
        att_copy(b).wait_send()

    def gate_sib(b, carry):
        rg, tg = carry
        rows = sib_rows(b)
        upstream, more_rg, more_tg = gate_grad(0, gates[0, 0:experts, rows], rows)
        att_s[rows, :] = upstream.astype(BF16)
        gs_copy((1 - m) * own_blocks + b).start()
        return rg + more_rg, tg + more_tg

    def gate_own(b, carry):
        rg, tg = carry
        rows = own_rows(b)
        upstream, more_rg, more_tg = gate_grad(0, gates[0, 0:experts, rows], rows)
        att_s[rows, :] = (upstream + back_r[0, blk_rows(b), :].astype(F32)).astype(BF16)
        gs_copy(m * own_blocks + b).start()
        return rg + more_rg, tg + more_tg

    sums = (jnp.zeros((experts, D), F32), jnp.zeros((experts, 1), F32))
    sums = lax.fori_loop(0, own_blocks, gate_sib, sums)
    back_copies[0].wait_recv()
    rg, tg = lax.fori_loop(0, own_blocks, gate_own, sums)
    ar_s[0, 8:16, :] += rg
    ar_s[0, 16:24, 0:128] += jnp.where(task_row == task.astype(F32), tg, 0.0)

    rs_b(2)
    rs_d(1)
    pair_mix_back()
    sent(pair_copies)

    def mix_out(b, carry):
        pair_s[1, blk_rows(b), :] = mix[0, sib_rows(b), :].astype(BF16)
        return carry

    lax.fori_loop(0, own_blocks, mix_out, 0)
    send_mix.start()

    gml = att_r
    w_o = flat(3)

    def back_second(rows, gb):
        gs_copy(gb).wait_recv()
        grad_second = att_s[rows, :].astype(F32) + gs_r[rows, :].astype(F32)
        unit, inv_std = row_stats(mid[rows, :])
        back = row_back(grad_second, unit, inv_std, gain2)
        return grad_second, unit, back

    def back_own(b, carry):
        gain_sum, bias_sum = carry
        rows = own_rows(b)
        grad_second, unit, back = back_second(rows, m * own_blocks + b)
        grad_mid = igrad_ref[blk_rows(b), :] + back
        igrad_ref[blk_rows(b), :] = grad_mid
        grad_low = grad_mid.astype(BF16)
        gml[rows, :] = grad_low
        gctx[rows, :] = mm(grad_low, w_o).astype(BF16)
        gain_sum = gain_sum + jnp.sum(grad_second * unit, axis=0, keepdims=True)
        bias_sum = bias_sum + jnp.sum(grad_second, axis=0, keepdims=True)
        return gain_sum, bias_sum

    def back_sib(b, carry):
        rows = sib_rows(b)
        grad_second, unit, back = back_second(rows, (1 - m) * own_blocks + b)
        grad_low = (g_all[0, rows, :].astype(F32) + back).astype(BF16)
        gml[rows, :] = grad_low
        gctx[rows, :] = mm(grad_low, w_o).astype(BF16)
        return carry

    zero_row = jnp.zeros((1, D), F32)
    gain2_grad, bias2_grad = lax.fori_loop(0, own_blocks, back_own, (zero_row, zero_row))
    ar_s[0, 2:3, :] = gain2_grad
    ar_s[0, 3:4, :] = bias2_grad
    early.one()
    lax.fori_loop(0, own_blocks, back_sib, 0)
    gg[:, :, :, :, part(3)] = mm(gml[...], ctx[...], TN).reshape(qshape).astype(BF16)

    rs_b(3)
    rs_c(2)
    pass_g.wait_send()

    def last_part(pbuf, keys_acc, values_acc):

        def p_in(b):
            return pltpu.make_async_copy(p_hbm.at[b], pbuf.at[b % 2], p_sem.at[b % 2])

        p_in(0).start()
        keys_acc[...] = jnp.zeros(keys_acc.shape, F32)
        values_acc[...] = jnp.zeros(values_acc.shape, F32)

        def attend_back(b, carry):
            r = blk_rows(b)

            @pl.when(b + 1 < blocks)
            def _():
                p_in(b + 1).start()

            p_in(b).wait()
            outs = []
            for h in range(heads):
                cs = slice(h * HD, (h + 1) * HD)
                grad_block = gctx[r, cs]
                inner = jnp.sum(
                    grad_block.astype(F32) * ctx[r, cs].astype(F32), axis=1, keepdims=True
                )
                grad_prob = mm(grad_block, vs[:, cs], NT)
                prob = pbuf[b % 2, h]
                grad_scores = (prob.astype(F32) * (grad_prob - inner)).astype(BF16)
                outs.append(mm(grad_scores, ks[:, cs]) * SCORE_SCALE)
                keys_acc[cs, :] += mm(qs[r, cs], grad_scores, TN)
                values_acc[cs, :] += mm(grad_block, prob, TN)
            g_all[1, r, 0:width] = jnp.concatenate(outs, axis=1).astype(BF16)

            @pl.when(b == 2)
            def _():
                rs_c(3)

            @pl.when(b == 3)
            def _():
                rs_d(2)
                early.two()

            @pl.when(b == 5)
            def _():
                rs_d(3)
                rs_e(0)
                rs_e(1)

            return carry

        lax.fori_loop(0, blocks, attend_back, 0)

        normed = x1[...]
        gg[:, :, :, :, part(0)] = mm(normed, g_all[1, :, 0:width], TN).reshape(qshape).astype(BF16)
        gg[:, :, :, :, part(1)] = mm(normed, keys_acc[...].astype(BF16), TT).reshape(qshape).astype(BF16)
        gg[:, :, :, :, part(2)] = mm(normed, values_acc[...].astype(BF16), TT).reshape(qshape).astype(BF16)
        start(gr1)
        small_ref[...] = early.three()

        def grad_first(rows):
            return (
                mm(g_all[1, rows, 0:width], flat(0), NT)
                + mm(keys_acc[:, rows].astype(BF16), flat(1), TT)
                + mm(values_acc[:, rows].astype(BF16), flat(2), TT)
            )

        def first_back_sib(b, carry):
            pair_s[0, blk_rows(b), :] = grad_first(sib_rows(b)).astype(BF16)
            return carry

        def first_back_own(b, carry):
            gsec[0, blk_rows(b), :] = grad_first(own_rows(b))
            return carry

        lax.fori_loop(0, own_blocks, first_back_sib, 0)
        send_first.start()
        lax.fori_loop(0, own_blocks, first_back_own, 0)

    pl.run_scoped(
        last_part,
        pltpu.VMEM(pshape, BF16),
        pltpu.VMEM((width, rows_all), F32),
        pltpu.VMEM((width, rows_all), F32),
    )

    arrive(gr1)
    gg[:, y, :, :, low_lanes] = add_low(gg[:, y, :, :, low_lanes], q1[0])
    gg[:, :, x, :, high_lanes] = add_low(gg[:, :, x, :, high_lanes], q1[1])
    start(gr2)
    send_first.wait_recv()

    def back_first(b, carry):
        gain_sum, bias_sum = carry
        r = blk_rows(b)
        upstream = gsec[0, r, :] + gfirst_r[r, :].astype(F32)
        unit, inv_std = row_stats(x_ref[r, :].astype(F32))
        igrad_ref[r, :] += row_back(upstream, unit, inv_std, gain1)
        gain_sum = gain_sum + jnp.sum(upstream * unit, axis=0, keepdims=True)
        bias_sum = bias_sum + jnp.sum(upstream, axis=0, keepdims=True)
        return gain_sum, bias_sum

    gain1_grad, bias1_grad = lax.fori_loop(0, own_blocks, back_first, (zero_row, zero_row))
    la_s[0] = jnp.zeros(la_s.shape[1:], F32)
    la_s[0, 0:1, :] = gain1_grad
    la_s[0, 1:2, :] = bias1_grad

    late.one()

    send_mix.wait_recv()
    back_copies[1].wait_recv()

    def write_out(b, carry):
        r = blk_rows(b)
        rows = own_rows(b)
        out_ref[r, :] = (
            mid[rows, :]
            + mix[0, rows, :]
            + mix_r[r, :].astype(F32)
            + back_r[1, r, :].astype(F32)
        )
        return carry

    lax.fori_loop(0, own_blocks, write_out, 0)

    arrive(gr2)
    gg[:, y, x, :, low_lanes] = add_low(gg[:, y, x, :, low_lanes], q2[0])
    gg[:, y, x, :, high_lanes] = add_low(gg[:, y, x, :, high_lanes], q2[1])
    start(gr3)
    rs_e(2)
    rs_e(3)

    def squares(e, acc):
        for a in range(2):
            acc = acc + jnp.sum(red_ref[a, e] * red_ref[a, e], axis=0, keepdims=True)
        return acc

    columns = lax.fori_loop(0, experts, squares, jnp.zeros((1, hidden_width), F32))
    late.two()

    arrive(gr3)
    total = gg[z, y, x].astype(F32)
    for k in range(3):
        total = total + q3[k].astype(F32)
    redq_ref[...] = total
    columns = columns + jnp.sum(total * total, axis=0, keepdims=True)
    sc_s[...] = jnp.full(sc_s.shape, jnp.sum(columns), F32)
    start(last)
    sc_g[me] = sc_s[...]
    late_ref[0:2, :] = late.three()[0:2]
    arrive(last)
    total = sc_g[0]
    for k in range(1, len(everyone) + 1):
        total = total + sc_g[k]
    late_ref[2:8, :] = jnp.broadcast_to(total[0:1, 0:1], (6, D))

    sent(gq1 + gq2 + gq3 + gr1 + gr2 + gr3)
    early.done()
    late.done()
    sent(last)
    sent([send_x, send_g, near_g, near_gates, send_mix, send_first] + back_copies)
    for i in range(local):
        sent(ag0(i) + ag1(i) + ag2(i) + ag3(i))
        sent(rs1(i) + rs2(i) + rs3(i) + rs4(i))

    def drain_rows(b, carry):
        gs_copy(b).wait_send()
        return carry

    def drain_own(b, carry):
        near_x2(b).wait_send()
        pass_x2(b).wait_send()
        return carry

    lax.fori_loop(0, blocks, drain_rows, 0)
    lax.fori_loop(0, own_blocks, drain_own, 0)


def step_call(x_rows, cotangent, task_ids, routes, norms, qkv, wo, router, win, wout):
    half = x_rows.shape[0]
    rows_all = 2 * half
    experts, shard, hidden = win.shape
    local = experts // 2
    width = wo.shape[1]
    blocks = rows_all // ROW_BLOCK
    own_blocks = half // ROW_BLOCK
    heads = width // HD
    vmem = pl.BlockSpec(memory_space=pltpu.VMEM)
    hbm = pl.BlockSpec(memory_space=pl.ANY)
    grid = (GRID_Z, GRID_Y, GRID_X)
    struct = jax.ShapeDtypeStruct
    dma = pltpu.SemaphoreType.DMA
    outs = (
        struct((half, D), F32),
        struct((half, D), F32),
        struct((2, experts, shard, hidden), F32),
        struct((shard, 4 * width), F32),
        struct((24, D), F32),
        struct((8, D), F32),
        struct((blocks, heads, ROW_BLOCK, rows_all), BF16),
    )
    scratch = [
        pltpu.VMEM((half, D), BF16),
        pltpu.VMEM((2, rows_all, D), BF16),
        pltpu.VMEM((rows_all, D), BF16),
        pltpu.VMEM((rows_all, width), BF16),
        pltpu.VMEM((rows_all, width), BF16),
        pltpu.VMEM((rows_all, width), BF16),
        pltpu.VMEM((rows_all, width), BF16),
        pltpu.VMEM((rows_all, D), BF16),
        pltpu.VMEM((rows_all, D), BF16),
        pltpu.VMEM((rows_all, D), F32),
        pltpu.VMEM((2, rows_all, D), BF16),
        pltpu.VMEM((2, 2 * experts, rows_all), F32),
        pltpu.VMEM((2, experts, rows_all), F32),
        pltpu.VMEM((2, rows_all, D), F32),
        pltpu.VMEM((2, rows_all, D), F32),
        pltpu.VMEM((rows_all, D), BF16),
        pltpu.VMEM((half, D), BF16),
        pltpu.VMEM((half, D), BF16),
        pltpu.VMEM((rows_all, width), BF16),
        pltpu.VMEM((half, D), BF16),
        pltpu.VMEM((2, half, D), BF16),
        pltpu.VMEM((2, half, D), BF16),
        pltpu.VMEM((2, half, D), BF16),
        pltpu.VMEM((2, local) + grid + (shard, hidden), BF16),
        pltpu.VMEM((2, local) + grid + (shard, hidden), BF16),
        pltpu.VMEM((2, local, shard, hidden), BF16),
        pltpu.VMEM((local, 2, 4, 2, shard, hidden), BF16),
        pltpu.VMEM((local, 2, 4, shard, hidden), BF16),
        pltpu.VMEM((local, 2, 2, shard, hidden), BF16),
        pltpu.VMEM((local, 2, shard, hidden), BF16),
        pltpu.VMEM(grid + (shard, 4 * width), BF16),
        pltpu.VMEM((4, D, width), BF16),
        pltpu.VMEM(grid + (shard, 4 * width), BF16),
        pltpu.VMEM((2, 4, 2, shard, 2 * width), BF16),
        pltpu.VMEM((2, 4, shard, 2 * width), BF16),
        pltpu.VMEM((3, shard, 4 * width), BF16),
        pltpu.VMEM((2, 24, D), F32),
        pltpu.VMEM((8, 24, D), F32),
        pltpu.VMEM((4, 24, D), F32),
        pltpu.VMEM((2, 8, D), F32),
        pltpu.VMEM((8, 8, D), F32),
        pltpu.VMEM((4, 8, D), F32),
        pltpu.VMEM((8, 128), F32),
        pltpu.VMEM((32, 8, 128), F32),
    ]
    for size in [
        (local, 6),
        (local, 6),
        (7,),
        (7,),
        (7,),
        (4,),
        (own_blocks,),
        (own_blocks,),
        (blocks,),
        (blocks,),
        (10,),
        (10,),
        (31,),
    ]:
        scratch += [dma(size), dma(size)]
    scratch += [dma((2,)), dma((3,))]
    return pl.pallas_call(
        step_kernel,
        out_shape=outs,
        in_specs=[vmem, hbm, pl.BlockSpec(memory_space=pltpu.SMEM)] + [vmem] * 5 + [hbm] * 2,
        out_specs=[vmem] * 6 + [hbm],
        scratch_shapes=scratch,
        compiler_params=pltpu.CompilerParams(
            collective_id=0, has_side_effects=True, vmem_limit_bytes=64 << 20
        ),
        name="step",
    )(
        x_rows,
        cotangent,
        task_ids,
        routes.T,
        norms,
        qkv,
        wo,
        router.T,
        win,
        wout,
    )


def adam_parts(weight, first, second, average, gradient, clip_scale, rate):
    clipped = clip_scale * gradient
    first_new = BETA_FIRST * first + (1.0 - BETA_FIRST) * clipped
    second_new = BETA_SECOND * second + (1.0 - BETA_SECOND) * clipped * clipped
    first_hat = first_new * (1.0 / (1.0 - BETA_FIRST**STEP))
    second_hat = second_new * (1.0 / (1.0 - BETA_SECOND**STEP))
    weight_new = weight - rate * (
        first_hat / (jnp.sqrt(second_hat) + ADAM_EPS) + WEIGHT_DECAY * weight
    )
    return weight_new, first_new, second_new, EMA_KEEP * average + (1.0 - EMA_KEEP) * weight_new


def adam_kernel(*refs):
    red, redq, small, late, rows_in, back_in = refs[:6]
    state = [refs[6 + 4 * k : 10 + 4 * k] for k in range(6)]
    norm_out, rows_out, back_out = refs[30:33]
    fresh = [refs[33 + 4 * k : 37 + 4 * k] for k in range(6)]
    step = pl.program_id(0)
    width = redq.shape[1] // 4

    rows_out[...] = rows_in[...]
    back_out[...] = back_in[...]
    norm_grad = jnp.concatenate([late[0:2, :], small[2:4, :]], axis=0)
    router_grad = small[8:16, :]
    task_grad = small[16:24, 0:TASKS]
    total = (
        jnp.max(late[2:3, 0:1])
        + jnp.sum(norm_grad * norm_grad)
        + jnp.sum(router_grad * router_grad)
        + jnp.sum(task_grad * task_grad)
    )
    grad_norm = jnp.sqrt(jnp.full((1, 1), total, F32))
    clip = jnp.minimum(1.0, CLIP_LIMIT / (grad_norm + 1e-06))

    def update(k, gradient, rate, *index):
        new = adam_parts(*[r[index] for r in state[k]], gradient, clip, rate)
        for r, v in zip(fresh[k], new):
            r[index] = v

    @pl.when(step == 0)
    def _():
        norm_out[0] = jnp.max(grad_norm)
        update(0, norm_grad, NORM_RATE, slice(None))
        for c in range(3):
            update(1, redq[:, c * width : (c + 1) * width], LEARN_RATE, c)
        update(2, redq[:, 3 * width :], LEARN_RATE, slice(None))
        update(3, router_grad, LEARN_RATE, slice(None), slice(0, D))
        update(3, task_grad, LEARN_RATE, slice(None), slice(D, D + TASKS))

    update(4, red[0], LEARN_RATE, slice(None))
    update(5, red[1], LEARN_RATE, slice(None))


def adam_call(red, redq, small, late, output, input_grad, state):
    experts, shard, hidden = red.shape[1:]
    per = 4
    steps = experts // per

    def fixed(array):
        rank = len(array.shape)
        return pl.BlockSpec(array.shape, lambda s: (0,) * rank)

    rows = pl.BlockSpec((output.shape[0] // steps, D), lambda s: (s, 0))
    tile = pl.BlockSpec((per, shard, hidden), lambda s: (s, 0, 0))
    specs = []
    for k, group in enumerate(state):
        specs += [tile if k >= 4 else fixed(a) for a in group]
    flat = [a for group in state for a in group]
    struct = jax.ShapeDtypeStruct
    results = pl.pallas_call(
        adam_kernel,
        grid=(steps,),
        out_shape=[struct((1,), F32), struct(output.shape, F32), struct(output.shape, F32)]
        + [struct(a.shape, F32) for a in flat],
        in_specs=[
            pl.BlockSpec((2, per, shard, hidden), lambda s: (0, s, 0, 0)),
            fixed(redq),
            fixed(small),
            fixed(late),
            rows,
            rows,
        ]
        + specs,
        out_specs=[pl.BlockSpec(memory_space=pltpu.SMEM), rows, rows] + specs,
        compiler_params=pltpu.CompilerParams(vmem_limit_bytes=64 << 20),
        name="adam",
    )(red, redq, small, late, output, input_grad, *flat)
    fresh = [results[3 + 4 * k : 7 + 4 * k] for k in range(6)]
    return results[0], results[1], results[2], fresh


def shards(
    x_rows,
    cotangent,
    task_ids,
    routes,
    norm_params,
    norm_first,
    norm_second,
    norm_ema,
    qkv_weight,
    qkv_first,
    qkv_second,
    qkv_ema,
    out_weight,
    out_first,
    out_second,
    out_ema,
    router,
    router_first,
    router_second,
    router_ema,
    expert_in,
    expert_in_first,
    expert_in_second,
    expert_in_ema,
    expert_out,
    expert_out_first,
    expert_out_second,
    expert_out_ema,
):
    qkv_full, out_full, in_full, eout_full = (
        lax.all_gather(qkv_weight.astype(jnp.bfloat16), "dp", axis=1, tiled=True),
        lax.all_gather(out_weight.astype(jnp.bfloat16), "dp", axis=0, tiled=True),
        lax.all_gather(expert_in.astype(jnp.bfloat16), "dp", axis=1, tiled=True),
        lax.all_gather(expert_out.astype(jnp.bfloat16), "dp", axis=1, tiled=True),
    )
    local_width = qkv_full.shape[2]
    local_heads = local_width // HD
    x_float = x_rows.astype(jnp.float32)
    first_normed, first_unit, first_inv = norm_forward(x_float, norm_params[0], norm_params[1])
    first_all = lax.all_gather(first_normed.astype(jnp.bfloat16), "mp", axis=0, tiled=True)
    triple = jnp.einsum(
        "rd,cdh->crh", first_all, qkv_full, preferred_element_type=jnp.float32
    ).astype(jnp.bfloat16)
    heads = triple.reshape(3, IMGS, L, local_heads, HD)
    context_heads, log_total = lax.map(
        lambda member: attend_image(member[0], member[1], member[2], QB),
        (heads[0], heads[1], heads[2]),
    )
    context = context_heads.reshape(R, local_width)
    attended_part = jnp.einsum("rh,dh->rd", context, out_full, preferred_element_type=jnp.float32)
    attended = lax.psum_scatter(
        attended_part.astype(jnp.bfloat16), "mp", scatter_dimension=0, tiled=True
    ).astype(jnp.float32)
    mid = x_float + attended
    second_normed, second_unit, second_inv = norm_forward(mid, norm_params[2], norm_params[3])
    second_all = lax.all_gather(second_normed.astype(jnp.bfloat16), "mp", axis=0, tiled=True)
    second_float = second_all.astype(jnp.float32)
    task_onehot = (task_ids[:, None] == jnp.arange(TASKS, dtype=jnp.int32)[None, :]).astype(
        jnp.float32
    )
    task_bias = dense_exact(task_onehot, router[D:])
    logits = dense_exact(second_float, router[:D])
    logits = (logits.reshape(IMGS, L, E) + task_bias[:, None, :]).reshape(R, E)
    route_hot = (routes[:, :, None] == jnp.arange(E, dtype=jnp.int32)[None, None, :]).astype(
        jnp.float32
    )
    chosen = jnp.sum(route_hot * logits[:, None, :], axis=-1)
    gates = jax.nn.softmax(chosen, axis=-1)
    slots = slot_table(routes, E, CAP)
    pair_ids = jnp.arange(R * TOP, dtype=jnp.int32)
    slot_pair = jnp.full((E * CAP,), R * TOP, jnp.int32).at[slots].set(pair_ids)
    slot_token = (slot_pair // TOP).reshape(E, CAP)
    gate_padded = jnp.concatenate([gates.reshape(-1), jnp.zeros((1,), jnp.float32)])
    slot_gate = gate_padded[slot_pair].reshape(E, CAP)
    padded_rows = jnp.concatenate([second_all, jnp.zeros((1, D), jnp.bfloat16)], axis=0)

    def expert_forward(carry, member):
        weight_in, weight_out, owners, owner_gate = member
        dispatched = padded_rows[owners]
        pre = jnp.dot(dispatched, weight_in, preferred_element_type=jnp.float32)
        hidden = gelu_exact(pre).astype(jnp.bfloat16)
        produced = jnp.einsum("cf,df->cd", hidden, weight_out, preferred_element_type=jnp.float32)
        return (carry.at[owners].add(owner_gate[:, None] * produced), None)

    mixture_acc, unused = lax.scan(
        expert_forward,
        jnp.zeros((R + 1, D), jnp.float32),
        (in_full, eout_full, slot_token, slot_gate),
    )
    mixture = lax.psum_scatter(
        mixture_acc[:R].astype(jnp.bfloat16), "mp", scatter_dimension=0, tiled=True
    ).astype(jnp.float32)
    output = mid + mixture
    grad_low_all = lax.all_gather(cotangent.astype(jnp.bfloat16), "mp", axis=0, tiled=True)
    grad_padded = jnp.concatenate([grad_low_all, jnp.zeros((1, D), jnp.bfloat16)], axis=0)

    def expert_backward(carry, member):
        weight_in, weight_out, owners, owner_gate = member
        dispatched = padded_rows[owners]
        pre = jnp.dot(dispatched, weight_in, preferred_element_type=jnp.float32)
        hidden = gelu_exact(pre).astype(jnp.bfloat16)
        produced = jnp.einsum("cf,df->cd", hidden, weight_out, preferred_element_type=jnp.float32)
        incoming = grad_padded[owners].astype(jnp.float32)
        slot_grad_gate = jnp.sum(incoming * produced, axis=-1)
        grad_produced = (owner_gate[:, None] * incoming).astype(jnp.bfloat16)
        grad_hidden = jnp.dot(grad_produced, weight_out, preferred_element_type=jnp.float32)
        grad_pre = (grad_hidden * gelu_slope(pre)).astype(jnp.bfloat16)
        grad_weight_out = jnp.einsum(
            "cd,cf->df", grad_produced, hidden, preferred_element_type=jnp.float32
        )
        grad_weight_in = jnp.einsum(
            "cd,cf->df", dispatched, grad_pre, preferred_element_type=jnp.float32
        )
        grad_dispatched = jnp.einsum(
            "cf,df->cd", grad_pre, weight_in, preferred_element_type=jnp.float32
        )
        return (
            carry.at[owners].add(grad_dispatched),
            (grad_weight_in, grad_weight_out, slot_grad_gate),
        )

    expert_carry, expert_outs = lax.scan(
        expert_backward,
        jnp.zeros((R + 1, D), jnp.float32),
        (in_full, eout_full, slot_token, slot_gate),
    )
    grad_in_stack, grad_eout_stack, slot_grad_gate = expert_outs
    in_reduced, eout_reduced = (
        lax.psum_scatter(grad_in_stack, "dp", scatter_dimension=1, tiled=True),
        lax.psum_scatter(grad_eout_stack, "dp", scatter_dimension=1, tiled=True),
    )
    grad_gates = slot_grad_gate.reshape(-1)[slots].reshape(R, TOP)
    grad_chosen = gates * (grad_gates - jnp.sum(gates * grad_gates, axis=-1, keepdims=True))
    grad_logits = jnp.sum(route_hot * grad_chosen[:, :, None], axis=1)
    router_rows_grad = dense_exact(second_float.T, grad_logits)
    task_rows_grad = dense_exact(task_onehot.T, jnp.sum(grad_logits.reshape(IMGS, L, E), axis=1))
    router_grad_part = jnp.concatenate([router_rows_grad, task_rows_grad], axis=0)
    grad_second_part = expert_carry[:R] + dense_exact(grad_logits, router[:D].T)
    grad_second = lax.psum_scatter(
        grad_second_part.astype(jnp.bfloat16), "mp", scatter_dimension=0, tiled=True
    ).astype(jnp.float32)
    grad_mid_norm, gain_two_grad, shift_two_grad = norm_backward(
        grad_second, second_unit, second_inv, norm_params[2]
    )
    grad_mid = cotangent + grad_mid_norm
    grad_mid_all = lax.all_gather(grad_mid.astype(jnp.bfloat16), "mp", axis=0, tiled=True)
    grad_out_weight = jnp.einsum(
        "rd,rh->dh", grad_mid_all, context, preferred_element_type=jnp.float32
    )
    grad_context = jnp.dot(grad_mid_all, out_full, preferred_element_type=jnp.float32).astype(
        jnp.bfloat16
    )
    grad_context_heads = grad_context.reshape(IMGS, L, local_heads, HD)
    grad_queries, grad_keys, grad_values = lax.map(
        lambda member: attend_image_back(member[0], member[1], member[2], member[3], member[4], QB),
        (heads[0], heads[1], heads[2], log_total, grad_context_heads),
    )
    grad_triple = jnp.stack(
        [
            grad_queries.reshape(R, local_width),
            grad_keys.reshape(R, local_width),
            grad_values.reshape(R, local_width),
        ],
        axis=0,
    )
    grad_qkv_weight = jnp.einsum(
        "rd,crh->cdh", first_all, grad_triple, preferred_element_type=jnp.float32
    )
    grad_first_part = jnp.einsum(
        "crh,cdh->rd", grad_triple, qkv_full, preferred_element_type=jnp.float32
    )
    grad_first = lax.psum_scatter(
        grad_first_part.astype(jnp.bfloat16), "mp", scatter_dimension=0, tiled=True
    ).astype(jnp.float32)
    grad_x_norm, gain_one_grad, shift_one_grad = norm_backward(
        grad_first, first_unit, first_inv, norm_params[0]
    )
    input_grad = grad_mid + grad_x_norm
    norm_grad_part = jnp.stack(
        [gain_one_grad, shift_one_grad, gain_two_grad, shift_two_grad], axis=0
    )
    norm_grad, router_grad = lax.psum((norm_grad_part, router_grad_part), ("dp", "mp"))
    qkv_reduced, out_reduced = (
        lax.psum_scatter(grad_qkv_weight, "dp", scatter_dimension=1, tiled=True),
        lax.psum_scatter(grad_out_weight, "dp", scatter_dimension=0, tiled=True),
    )
    local_squares = (
        jnp.sum(qkv_reduced * qkv_reduced)
        + jnp.sum(out_reduced * out_reduced)
        + jnp.sum(in_reduced * in_reduced)
        + jnp.sum(eout_reduced * eout_reduced)
    )
    share = 1.0 / (lax.axis_size("dp") * lax.axis_size("mp"))
    small_squares = jnp.sum(norm_grad * norm_grad) + jnp.sum(router_grad * router_grad)
    total_squares = lax.psum(local_squares + share * small_squares, ("dp", "mp"))
    grad_norm = jnp.sqrt(total_squares)
    clip_scale = jnp.minimum(1.0, CLIP_LIMIT / (grad_norm + 1e-06))
    norm_new, norm_first_new, norm_second_new, norm_ema_new = adam_update(
        norm_params, norm_first, norm_second, norm_ema, norm_grad, clip_scale, NORM_RATE
    )
    qkv_new, qkv_first_new, qkv_second_new, qkv_ema_new = adam_update(
        qkv_weight, qkv_first, qkv_second, qkv_ema, qkv_reduced, clip_scale, LEARN_RATE
    )
    out_new, out_first_new, out_second_new, out_ema_new = adam_update(
        out_weight, out_first, out_second, out_ema, out_reduced, clip_scale, LEARN_RATE
    )
    router_new, router_first_new, router_second_new, router_ema_new = adam_update(
        router, router_first, router_second, router_ema, router_grad, clip_scale, LEARN_RATE
    )
    in_new, in_first_new, in_second_new, in_ema_new = adam_update(
        expert_in,
        expert_in_first,
        expert_in_second,
        expert_in_ema,
        in_reduced,
        clip_scale,
        LEARN_RATE,
    )
    eout_new, eout_first_new, eout_second_new, eout_ema_new = adam_update(
        expert_out,
        expert_out_first,
        expert_out_second,
        expert_out_ema,
        eout_reduced,
        clip_scale,
        LEARN_RATE,
    )
    return (
        output,
        input_grad,
        grad_norm.reshape(1),
        norm_new,
        norm_first_new,
        norm_second_new,
        norm_ema_new,
        qkv_new,
        qkv_first_new,
        qkv_second_new,
        qkv_ema_new,
        out_new,
        out_first_new,
        out_second_new,
        out_ema_new,
        router_new,
        router_first_new,
        router_second_new,
        router_ema_new,
        in_new,
        in_first_new,
        in_second_new,
        in_ema_new,
        eout_new,
        eout_first_new,
        eout_second_new,
        eout_ema_new,
    )


def shards_fused(
    x_rows,
    cotangent,
    task_ids,
    routes,
    norm_params,
    norm_first,
    norm_second,
    norm_ema,
    qkv_weight,
    qkv_first,
    qkv_second,
    qkv_ema,
    out_weight,
    out_first,
    out_second,
    out_ema,
    router,
    router_first,
    router_second,
    router_ema,
    expert_in,
    expert_in_first,
    expert_in_second,
    expert_in_ema,
    expert_out,
    expert_out_first,
    expert_out_second,
    expert_out_ema,
):
    output, input_grad, expert_red, qkvo_red, small, late, unused = step_call(
        x_rows,
        cotangent,
        task_ids,
        routes,
        norm_params,
        qkv_weight,
        out_weight,
        router,
        expert_in,
        expert_out,
    )
    state = [
        (norm_params, norm_first, norm_second, norm_ema),
        (qkv_weight, qkv_first, qkv_second, qkv_ema),
        (out_weight, out_first, out_second, out_ema),
        (router.T, router_first.T, router_second.T, router_ema.T),
        (expert_in, expert_in_first, expert_in_second, expert_in_ema),
        (expert_out, expert_out_first, expert_out_second, expert_out_ema),
    ]
    grad_norm, output, input_grad, fresh = adam_call(
        expert_red, qkvo_red, small, late, output, input_grad, state
    )
    fresh[3] = [a.T for a in fresh[3]]
    flat = [a for group in fresh for a in group]
    return (output, input_grad, grad_norm, *flat)


def solution(mesh):
    fused = mesh.shape["dp"] == GRID_Z * GRID_Y * GRID_X and mesh.shape["mp"] == 2
    return jax.shard_map(
        shards_fused if fused else shards,
        mesh=mesh,
        in_specs=(
            P(("dp", "mp"), None),
            P(("dp", "mp"), None),
            P("dp"),
            P("dp", None),
            P(),
            P(),
            P(),
            P(),
            P(None, "dp", "mp"),
            P(None, "dp", "mp"),
            P(None, "dp", "mp"),
            P(None, "dp", "mp"),
            P("dp", "mp"),
            P("dp", "mp"),
            P("dp", "mp"),
            P("dp", "mp"),
            P(),
            P(),
            P(),
            P(),
            P(None, "dp", "mp"),
            P(None, "dp", "mp"),
            P(None, "dp", "mp"),
            P(None, "dp", "mp"),
            P(None, "dp", "mp"),
            P(None, "dp", "mp"),
            P(None, "dp", "mp"),
            P(None, "dp", "mp"),
        ),
        out_specs=(
            P(("dp", "mp"), None),
            P(("dp", "mp"), None),
            P(),
            P(),
            P(),
            P(),
            P(),
            P(None, "dp", "mp"),
            P(None, "dp", "mp"),
            P(None, "dp", "mp"),
            P(None, "dp", "mp"),
            P("dp", "mp"),
            P("dp", "mp"),
            P("dp", "mp"),
            P("dp", "mp"),
            P(),
            P(),
            P(),
            P(),
            P(None, "dp", "mp"),
            P(None, "dp", "mp"),
            P(None, "dp", "mp"),
            P(None, "dp", "mp"),
            P(None, "dp", "mp"),
            P(None, "dp", "mp"),
            P(None, "dp", "mp"),
            P(None, "dp", "mp"),
        ),
        check_vma=False,
    )
```
